32 devices in a mesh: dp: 8 (over y, x, core), tensor: 4 (over z).
Axes of the slice: x: 2, y: 2, z: 4, core: 2. Of those that a mesh axis runs over, the one named last changes fastest.
Arguments:
- tokens: bfloat16 [16384, 768], P(('dp', 'tensor')), may hold values from -6 to 6
- cotangent: bfloat16 [16384, 768], P(('dp', 'tensor')), may hold values from -6 to 6
- labels: int32 [8], P('dp'), may hold values from 0 to 13
- piece_start: int32 [8, 2], P('dp'), may hold values from 0 to 8, as said below
- piece_len: int32 [8, 2], P('dp'), may hold values from 0 to 4, as said below
- w_qkv: bfloat16 [768, 3, 768], P('dp', None, 'tensor'), may hold values from -0.21875 to 0.21875
- w_out: bfloat16 [768, 768], P('tensor', 'dp'), may hold values from -6 to 6
- w_up: bfloat16 [768, 3072], P('dp', 'tensor'), may hold values from -0.21875 to 0.21875
- w_down: bfloat16 [3072, 768], P('tensor', 'dp'), may hold values from -0.109375 to 0.109375
- vec_table: float32 [8, 768], replicated, may hold values from -1.2 to 1.4, as said below
- ff_bias: float32 [3072], replicated, may hold values from -1.8 to 1.8
- cls_proj: bfloat16 [768, 128], replicated, may hold values from -0.21875 to 0.21875
- cls_vec: float32 [3, 128], replicated, may hold values from -4 to 4
- cls_hidden: bfloat16 [128, 128], replicated, may hold values from -6 to 6
- cls_out: bfloat16 [128, 14], replicated, may hold values from -1.796875 to 1.796875
- cls_bias: float32 [14], replicated, may hold values from -3 to 3
Outputs:
- layer_out: bfloat16 [16384, 768], P(('dp', 'tensor'))
- logits: float32 [8, 14], P('dp')
- grad_tokens: float32 [16384, 768], P(('dp', 'tensor'))
- grad_w_qkv: float32 [768, 3, 768], P('dp', None, 'tensor')
- grad_w_out: float32 [768, 768], P('tensor', 'dp')
- grad_w_up: float32 [768, 3072], P('dp', 'tensor')
- grad_w_down: float32 [3072, 768], P('tensor', 'dp')
- grad_vec_table: float32 [8, 768], replicated
- grad_ff_bias: float32 [3072], replicated
- grad_cls_proj: float32 [768, 128], replicated
- grad_cls_vec: float32 [3, 128], replicated
- grad_cls_hidden: float32 [128, 128], replicated
- grad_cls_out: float32 [128, 14], replicated
- grad_cls_bias: float32 [14], replicated
The draws below stay inside these ranges and needn't reach their ends.
Inputs may be any that keep to these rules, and one draw needn't show every extreme that they name: Blocks are counted in units of 256 tokens; piece_start[s, p] lies from p * 4 to (p + 1) * 4, and a piece with piece_len above 0 ends within that region. A picture piece covers piece_len whole blocks; 0 leaves the slot empty. `vec_table`: rows 3 and 6 are near 1, the others near 0.
All inputs are finite; a program needn't handle non-finite values.
Results may differ from the reference program's by a relative error of at most 0.017.
Values may be sent and summed in bfloat16 or wider, within the bound.
No kernel may reach another device: no remote copies, remote signals or barrier semaphores. Data moves between devices by JAX's collectives and lax.ppermute only.
A program may use at most 128 MiB of HBM per device.

```python
import jax
import jax.numpy as jnp
from jax import lax

D = 768
HEADS = 12
HEAD_DIM = 64
FF = 3072
CH = 128
POOL_HEADS = 2
CLASSES = 14
SEQ = 2048
PIECE_BLOCK = 256
PIECES = 2
SEQS = 8
TOKENS = 16384


def piece_lengths(base_key):
    region = SEQ // PIECE_BLOCK // PIECES
    drawn = jax.random.randint(jax.random.fold_in(base_key, 11), (SEQS, PIECES), 0, region + 1, dtype=jnp.int32)
    drawn = drawn.at[0, 0].set(region)
    return drawn.at[0, PIECES - 1].set(0)


def draw_piece_len(key, part):
    return piece_lengths(key)


def draw_piece_start(key, part):
    region = SEQ // PIECE_BLOCK // PIECES
    lengths = piece_lengths(key)
    offsets = jax.random.randint(jax.random.fold_in(key, 12), (SEQS, PIECES), 0, region - lengths + 1, dtype=jnp.int32)
    offsets = offsets.at[0, PIECES - 1].set(region)
    bases = jnp.arange(PIECES, dtype=jnp.int32) * region
    return (bases[None, :] + offsets).astype(jnp.int32)


def draw_vec_table(key, part):
    base_draw = jax.random.normal(key, (8, D), jnp.float32)
    row_scale = jnp.array([0.3, 0.03, 0.2, 0.1, 0.2, 0.2, 0.1, 0.2], jnp.float32)
    gain_rows = jnp.array([0.0, 0.0, 0.0, 1.0, 0.0, 0.0, 1.0, 0.0], jnp.float32)
    return jnp.clip(base_draw, -4.0, 4.0) * row_scale[:, None] + gain_rows[:, None]


def draw_cls_vec(key, part):
    base_draw = jax.random.normal(key, (3, CH), jnp.float32)
    row_scale = jnp.array([0.1, 1.0, 0.3], jnp.float32)
    return jnp.clip(base_draw, -4.0, 4.0) * row_scale[:, None]


def plant(values, rng, smallest, top_value):
    extent = values.shape
    spot = [jax.random.randint(jax.random.fold_in(rng, axis), (), 0, extent[axis]) for axis in range(len(extent))]
    values = values.at[tuple(spot)].set(smallest)
    longest = extent.index(max(extent))
    spot[longest] = (spot[longest] + 1) % extent[longest]
    return values.at[tuple(spot)].set(top_value)


def level_of(key, extent, split, least, top_value):
    level = 1.0
    for position, parts in split:
        heights = jax.random.uniform(jax.random.fold_in(jax.random.fold_in(key, 6), position), (parts,), jnp.float32, least / len(split), top_value / len(split))
        level = level * jnp.repeat(jnp.exp(heights), extent[position] // parts).reshape((-1,) + (1,) * (len(extent) - 1 - position))
    return level


def gaussian(own_key, dims, width, limit, cuts=(), kind=jnp.bfloat16):
    values = width * jax.random.normal(own_key, dims, jnp.float32)
    if cuts:
        values = values * level_of(own_key, dims, cuts, -0.22, 0.18)
    return jnp.clip(values, -limit, limit).astype(kind)


def setup_inputs(seed: int = 0) -> dict:
    key_of = jax.random.split(jax.random.key(seed), 17)
    return {
        "tokens": gaussian(key_of[0], (TOKENS, D), 1.0, 6.0, ((0, 32),)),
        "cotangent": gaussian(key_of[1], (TOKENS, D), 1.0, 6.0, ((0, 32),)),
        "labels": plant(jax.random.randint(key_of[2], (SEQS,), 0, CLASSES), jax.random.fold_in(key_of[2], 1), 0, CLASSES - 1).astype(jnp.int32),
        "piece_start": draw_piece_start(jax.random.fold_in(key_of[16], 71), 0),
        "piece_len": draw_piece_len(jax.random.fold_in(key_of[16], 71), 0),
        "w_qkv": gaussian(key_of[5], (D, 3, D), D ** -0.5, 0.21875, ((0, 8), (2, 4))),
        "w_out": gaussian(key_of[6], (D, D), (max(1, 2 * D // SEQ)) ** -0.5, 6.0, ((0, 4), (1, 8))),
        "w_up": gaussian(key_of[7], (D, FF), D ** -0.5, 0.21875, ((0, 8), (1, 4))),
        "w_down": gaussian(key_of[8], (FF, D), FF ** -0.5, 0.109375, ((0, 4), (1, 8))),
        "vec_table": draw_vec_table(jax.random.fold_in(key_of[16], 71), 0),
        "ff_bias": gaussian(key_of[10], (FF,), 0.3, 1.8, (), jnp.float32),
        "cls_proj": gaussian(key_of[11], (D, CH), D ** -0.5, 0.21875),
        "cls_vec": draw_cls_vec(jax.random.fold_in(key_of[16], 71), 0),
        "cls_hidden": gaussian(key_of[13], (CH, CH), 1.0, 6.0),
        "cls_out": gaussian(key_of[14], (CH, CLASSES), 0.3, 1.796875),
        "cls_bias": gaussian(key_of[15], (CLASSES,), 0.5, 3.0, (), jnp.float32),
    }


NORM_EPS = 1e-05
MASK_FILL = -1e+30
PRECISE = lax.Precision.HIGHEST

@jax.custom_vjp
def low(v):
    return lax.optimization_barrier(v.astype(jnp.bfloat16)).astype(jnp.float32)

@jax.custom_vjp
def low_back(v):
    return v

def low_keep(v):
    return (low(v), None)

def low_pass(kept, grad):
    return (grad,)

def back_keep(v):
    return (v, None)

def back_low(kept, grad):
    return (low(grad),)
low.defvjp(low_keep, low_pass)
low_back.defvjp(back_keep, back_low)

def highest(left_mat, right_mat):
    return jnp.dot(left_mat, right_mat, precision=PRECISE)

def layer_norm(values, gain_vec, shift_vec):
    centered = values - lax.optimization_barrier(jnp.mean(values, axis=-1, keepdims=True))
    spread = lax.optimization_barrier(jnp.mean(centered * centered, axis=-1, keepdims=True))
    return centered * lax.rsqrt(spread + NORM_EPS) * gain_vec + shift_vec

def gelu_exact(values):
    return jax.nn.gelu(values, approximate=False)

def piece_ids(starts, counts):
    blocks = jnp.arange(SEQ, dtype=jnp.int32) // PIECE_BLOCK
    inside = (blocks[:, None] >= starts[None, :]) & (blocks[:, None] < starts[None, :] + counts[None, :])
    numbers = jnp.arange(1, PIECES + 1, dtype=jnp.int32)
    return lax.optimization_barrier(jnp.sum(jnp.where(inside, numbers[None, :], 0), axis=1)).astype(jnp.int32)

def allowed_mask(query_pos, query_ids, key_pos, key_ids):
    causal = key_pos[None, :] <= query_pos[:, None]
    same_piece = (key_ids[None, :] == query_ids[:, None]) & (query_ids[:, None] > 0)
    return causal | same_piece

def softmax_rows(scores, axis_num):
    shifted = scores - lax.optimization_barrier(jnp.max(scores, axis=axis_num, keepdims=True))
    powers = jnp.exp(shifted)
    return powers / lax.optimization_barrier(jnp.sum(powers, axis=axis_num, keepdims=True))

def seq_forward(seq_rows, seq_cots, seq_label, starts, counts, params):
    w_qkv, w_out, w_up, w_down, vec_table, ff_bias, cls_proj, cls_vec, cls_hidden, cls_out, cls_bias = params
    head_scale = HEAD_DIM ** (-0.5)
    joined = w_qkv.reshape(D, 3 * D)
    proj_bias = jnp.concatenate([vec_table[0], jnp.zeros((D,), jnp.float32), vec_table[1]])
    qkv_all = low(low_back(highest(seq_rows, joined)) + proj_bias)
    query_heads = qkv_all[:, :D].reshape(SEQ, HEADS, HEAD_DIM)
    key_heads = qkv_all[:, D:2 * D].reshape(SEQ, HEADS, HEAD_DIM)
    value_heads = qkv_all[:, 2 * D:].reshape(SEQ, HEADS, HEAD_DIM)
    seq_ids = piece_ids(starts, counts)
    positions = jnp.arange(SEQ, dtype=jnp.int32)
    block_size = min(512, SEQ)
    count_blocks = SEQ // block_size

    def attend(block_item):
        q_block, id_block, pos_block = block_item
        raw_scores = jnp.einsum('qhd,khd->hqk', q_block, key_heads, precision=PRECISE)
        scores = low_back(raw_scores * head_scale)
        allowed = allowed_mask(pos_block, id_block, positions, seq_ids)
        scores = jnp.where(allowed[None], scores, MASK_FILL)
        prob_block = low(softmax_rows(scores, -1))
        return jnp.einsum('hqk,khd->qhd', prob_block, value_heads, precision=PRECISE)
    attn_mixed = lax.map(jax.checkpoint(attend), (query_heads.reshape(count_blocks, block_size, HEADS, HEAD_DIM), seq_ids.reshape(count_blocks, block_size), positions.reshape(count_blocks, block_size)))
    attn_low = low(low_back(attn_mixed.reshape(SEQ, D)))
    h_one = seq_rows + low_back(highest(attn_low, w_out)) + vec_table[2]
    x_one = layer_norm(h_one, vec_table[3], vec_table[4])
    x_low = low(x_one)
    ff_upper = low_back(highest(x_low, w_up)) + ff_bias
    act_low = low(gelu_exact(ff_upper))
    h_two = x_one + low_back(highest(act_low, w_down)) + vec_table[5]
    normed = layer_norm(h_two, vec_table[6], vec_table[7])
    out_low = low(normed)
    student = low_back(highest(out_low, cls_proj)) + cls_vec[0]
    pool_width = CH // POOL_HEADS
    split_heads = student.reshape(SEQ, POOL_HEADS, pool_width)
    pool_query = cls_vec[1].reshape(POOL_HEADS, pool_width)
    pool_logit = jnp.einsum('shd,hd->sh', split_heads, pool_query, precision=PRECISE) * pool_width ** (-0.5)
    pool_weights = softmax_rows(pool_logit, 0)
    pooled = jnp.einsum('sh,shd->hd', pool_weights, split_heads, precision=PRECISE).reshape(CH)
    hidden_cls = jnp.tanh(highest(pooled[None, :], cls_hidden)[0] + cls_vec[2])
    logits = highest(hidden_cls[None, :], cls_out)[0] + cls_bias
    largest = jnp.max(logits)
    log_total = largest + jnp.log(jnp.sum(jnp.exp(logits - largest)))
    picked = jnp.sum(jnp.where(jnp.arange(CLASSES, dtype=jnp.int32) == seq_label, logits, 0.0))
    objective = jnp.sum(seq_cots * normed) + log_total - picked
    return (objective, (normed, logits))

def reference(tokens, cotangent, labels, piece_start, piece_len, w_qkv, w_out, w_up, w_down, vec_table, ff_bias, cls_proj, cls_vec, cls_hidden, cls_out, cls_bias):
    params = tuple((weight_arr.astype(jnp.float32) for weight_arr in (w_qkv, w_out, w_up, w_down, vec_table, ff_bias, cls_proj, cls_vec, cls_hidden, cls_out, cls_bias)))
    rows_in = tokens.astype(jnp.float32).reshape(SEQS, SEQ, D)
    cots_in = cotangent.astype(jnp.float32).reshape(SEQS, SEQ, D)

    def total(rows_all, params_all):

        def one_seq(carried, seq_item):
            seq_rows, seq_cots, seq_label, starts, counts = seq_item
            seq_value, seq_outs = jax.checkpoint(seq_forward)(seq_rows, seq_cots, seq_label, starts, counts, params_all)
            return (carried + seq_value, seq_outs)
        summed, seq_outs = lax.scan(one_seq, jnp.zeros((), jnp.float32), (rows_all, cots_in, labels, piece_start, piece_len))
        return (summed, seq_outs)
    summed, pullback, (normed, logits) = jax.vjp(total, rows_in, params, has_aux=True)
    grad_rows, grad_params = pullback(jnp.ones((), jnp.float32))
    return (normed.reshape(TOKENS, D).astype(jnp.bfloat16), logits, grad_rows.reshape(TOKENS, D), grad_params[0], grad_params[1], grad_params[2], grad_params[3], grad_params[4], grad_params[5], grad_params[6], grad_params[7], grad_params[8], grad_params[9], grad_params[10])
```

```python
import functools

import jax
import jax.numpy as jnp
from jax import lax
from jax.experimental import pallas as pl
from jax.experimental.pallas import tpu as pltpu
from jax.sharding import PartitionSpec as P

HEAD_DIM = 64
CLASSES = 14
PIECE_BLOCK = 256
POOL_HEADS = 2
LANES = 128
NORM_EPS = 1e-05
MASK_FILL = -1e30
PRECISE = lax.Precision.HIGHEST
F32 = jnp.float32
BF16 = jnp.bfloat16
VMEM_LIMIT = 48 * 1024 * 1024


def dot_nn(a, b, precision=None):
    return lax.dot_general(
        a, b, (((1,), (0,)), ((), ())), preferred_element_type=F32, precision=precision
    )


def dot_nt(a, b, precision=None):
    return lax.dot_general(
        a, b, (((1,), (1,)), ((), ())), preferred_element_type=F32, precision=precision
    )


def dot_tn(a, b, precision=None):
    return lax.dot_general(
        a, b, (((0,), (0,)), ((), ())), preferred_element_type=F32, precision=precision
    )


def shifted(value, axis, size, by):
    return lax.ppermute(value, axis, [(i, (i + by) % size) for i in range(size)])


def swapped(value, axis, size, bit):
    return lax.ppermute(value, axis, [(i, i ^ bit) for i in range(size)])


def bits_of(size):
    return [1 << n for n in range(size.bit_length() - 1)]


def summed(value, dp, tensor, axes=("dp", "tensor")):
    for axis, size in (("dp", dp), ("tensor", tensor)):
        if axis in axes:
            for bit in bits_of(size):
                value = value + swapped(value, axis, size, bit)
    return value


def summed_to_owner(parts, axis, size):
    index = lax.axis_index(axis)
    for bit in bits_of(size):
        mine = (index // bit) % 2
        pairs = parts.reshape(parts.shape[0] // 2, 2, *parts.shape[1:])
        keep = lax.dynamic_index_in_dim(pairs, mine, 1, keepdims=False)
        give = lax.dynamic_index_in_dim(pairs, 1 - mine, 1, keepdims=False)
        parts = keep + swapped(give.astype(BF16), axis, size, bit).astype(F32)
    return parts[0]


def gathered(value, axis, size):
    index = lax.axis_index(axis)
    for bit in bits_of(size):
        other = swapped(value, axis, size, bit)
        low = (index // bit) % 2 == 0
        value = jnp.where(
            low, jnp.concatenate([value, other], 0), jnp.concatenate([other, value], 0)
        )
    return value


def block_range(start_ref, len_ref, block):
    first, stop, inside_any = block, block + 1, jnp.int32(0)
    for piece in range(start_ref.shape[1]):
        begin, count = start_ref[0, piece], len_ref[0, piece]
        inside = jnp.logical_and(block >= begin, block < begin + count)
        first = jnp.where(inside, begin, first)
        stop = jnp.where(inside, begin + count, stop)
        inside_any = jnp.where(inside, jnp.int32(1), inside_any)
    return first, stop, inside_any


def head_lanes(shape, head):
    lane = lax.broadcasted_iota(jnp.int32, shape, len(shape) - 1)
    return (lane >= head * HEAD_DIM) & (lane < (head + 1) * HEAD_DIM)


def attend_forward_kernel(heads, z_ref, start_ref, len_ref, *refs):
    tensor = len(refs) - 2 - 3
    chunks = refs[:tensor]
    o_ref, lse_ref = refs[tensor : tensor + 2]
    q_s, k_s, vt_s = refs[tensor + 2 :]
    rows, padded = chunks[0].shape[0], chunks[0].shape[1] // 3
    blk = PIECE_BLOCK
    blocks = tensor * rows // blk
    per_chunk = rows // blk
    z = z_ref[0]
    scale = HEAD_DIM ** (-0.5)
    for t in range(tensor):
        quarter = lax.rem(z - t + tensor, tensor)
        for part in range(per_chunk):
            b = quarter * per_chunk + part
            here = pl.ds(part * blk, blk)
            q = chunks[t][here, 0:padded]
            for h in range(heads):
                q_s[h, b] = jnp.where(head_lanes(q.shape, h), q * scale, 0.0).astype(BF16)
            pair, at = b // 2, lax.rem(b, 2) * blk
            k_s[pair, pl.ds(at, blk), :] = chunks[t][here, padded : 2 * padded]
            vt = chunks[t][here, 2 * padded : 3 * padded].T
            for side in range(2):

                @pl.when(lax.rem(b, 2) == side)
                def _():
                    vt_s[pair, :, side * blk : (side + 1) * blk] = vt


    def one_query(i, carry):
        _, stop, inside = block_range(start_ref, len_ref, i)
        q_h = [q_s[h, i] for h in range(heads)]
        query = i * blk + lax.broadcasted_iota(jnp.int32, (1, blk), 1)
        limit = jnp.maximum(query, jnp.where(inside > 0, stop * blk - 1, 0))

        def step(j, state, masked):
            tops, totals, mixed = state
            out = ([], [], [])
            keys = 2 * blk
            if masked:
                key = j * keys + lax.broadcasted_iota(jnp.int32, (keys, blk), 0)
                seen = key <= limit
            for h in range(heads):
                s = dot_nt(k_s[j], q_h[h])
                if masked:
                    s = jnp.where(seen, s, MASK_FILL)
                top = jnp.maximum(tops[h], jnp.max(s, axis=0, keepdims=True))
                p = jnp.exp(s - top)
                fade = jnp.exp(tops[h] - top)
                vt = vt_s[j, h * HEAD_DIM : (h + 1) * HEAD_DIM, :]
                out[0].append(top)
                out[1].append(totals[h] * fade + jnp.sum(p, axis=0, keepdims=True))
                out[2].append(mixed[h] * fade + dot_nn(vt, p.astype(BF16)))
            return tuple(tuple(v) for v in out)

        state = (
            tuple(jnp.full((1, blk), MASK_FILL, F32) for _ in range(heads)),
            tuple(jnp.zeros((1, blk), F32) for _ in range(heads)),
            tuple(jnp.zeros((HEAD_DIM, blk), F32) for _ in range(heads)),
        )
        own = i // 2
        state = lax.fori_loop(0, own, lambda j, c: step(j, c, False), state)
        state = step(own, state, True)
        tops, totals, mixed = lax.fori_loop(
            own + 1, (stop + 1) // 2, lambda j, c: step(j, c, True), state
        )
        outs = [mixed[h] * (1.0 / totals[h]) for h in range(heads)]
        lses = [tops[h] + jnp.log(totals[h]) for h in range(heads)]
        t = lax.rem(z - i // per_chunk + tensor, tensor)
        here = pl.ds(lax.rem(i, per_chunk) * blk, blk)
        o_ref[t, here, :] = jnp.concatenate(outs, axis=0).T.astype(BF16)
        lse_ref[i] = jnp.concatenate(lses + [jnp.zeros((8 - heads, blk), F32)], axis=0)
        return carry

    lax.fori_loop(0, blocks, one_query, 0)


def attend_forward(z, starts, lens, chunks, heads):
    tensor = len(chunks)
    rows, width = chunks[0].shape
    padded = width // 3
    seq, blk = tensor * rows, PIECE_BLOCK
    blocks = seq // blk
    smem = pl.BlockSpec(memory_space=pltpu.SMEM)
    vmem = pl.BlockSpec(memory_space=pltpu.VMEM)
    pairs = blocks * (blocks + 1) // 2
    return pl.pallas_call(
        functools.partial(attend_forward_kernel, heads),
        out_shape=(
            jax.ShapeDtypeStruct((tensor, rows, heads * HEAD_DIM), BF16),
            jax.ShapeDtypeStruct((blocks, 8, blk), F32),
        ),
        in_specs=[smem] * 3 + [vmem] * tensor,
        out_specs=(vmem, vmem),
        scratch_shapes=[
            pltpu.VMEM((heads, blocks, blk, padded), BF16),
            pltpu.VMEM((blocks // 2, 2 * blk, padded), BF16),
            pltpu.VMEM((blocks // 2, padded, 2 * blk), BF16),
        ],
        compiler_params=pltpu.CompilerParams(vmem_limit_bytes=VMEM_LIMIT),
        cost_estimate=pl.CostEstimate(
            flops=pairs * heads * blk * blk * 4 * 256,
            bytes_accessed=4 * seq * width,
            transcendentals=pairs * heads * blk * blk,
        ),
        name="attend_forward",
    )(z, starts, lens, *chunks)


def attend_backward_kernel(heads, z_ref, start_ref, len_ref, *refs):
    tensor = (len(refs) - 2 - 2 - 9) // 2
    chunks, grads = refs[:tensor], refs[tensor : 2 * tensor]
    o_ref, lse_ref, dqkv_ref, bias_ref = refs[2 * tensor : 2 * tensor + 4]
    q_s, k_s, kt_s, v_s, g_s, delta_s, dqt_s, dk_s, dv_s = refs[2 * tensor + 4 :]
    rows, padded = chunks[0].shape[0], chunks[0].shape[1] // 3
    width = heads * HEAD_DIM
    blk = PIECE_BLOCK
    blocks = tensor * rows // blk
    per_chunk = rows // blk
    z = z_ref[0]
    scale = HEAD_DIM ** (-0.5)
    for t in range(tensor):
        quarter = lax.rem(z - t + tensor, tensor)
        for part in range(per_chunk):
            b = quarter * per_chunk + part
            here = pl.ds(part * blk, blk)
            q = chunks[t][here, 0:padded]
            g = grads[t][here, :]
            for h in range(heads):
                q_s[h, b] = jnp.where(head_lanes(q.shape, h), q * scale, 0.0).astype(BF16)
                g_s[h, b, :, 0:width] = jnp.where(head_lanes(g.shape, h), g, 0.0).astype(BF16)
                if padded > width:
                    g_s[h, b, :, width:padded] = jnp.zeros((blk, padded - width), BF16)
            k = chunks[t][here, padded : 2 * padded]
            pair, at = b // 2, lax.rem(b, 2) * blk
            k_s[pair, pl.ds(at, blk), :] = k
            v_s[pair, pl.ds(at, blk), :] = chunks[t][here, 2 * padded : 3 * padded]
            kt = k.T
            for side in range(2):

                @pl.when(lax.rem(b, 2) == side)
                def _():
                    kt_s[pair, :, side * blk : (side + 1) * blk] = kt

            prod = (g.astype(F32) * o_ref[t, here, :].astype(F32)).T
            sums = [
                jnp.sum(prod[h * HEAD_DIM : (h + 1) * HEAD_DIM, :], axis=0, keepdims=True)
                for h in range(heads)
            ]
            delta_s[b] = jnp.concatenate(sums + [jnp.zeros((8 - heads, blk), F32)], axis=0)
            dqt_s[b] = jnp.zeros((padded, blk), F32)
    bias_ref[...] = jnp.zeros_like(bias_ref)

    keys = 2 * blk

    def one_pair(j, carry):
        first, _, _ = block_range(start_ref, len_ref, 2 * j)
        also, _, _ = block_range(start_ref, len_ref, 2 * j + 1)
        dk_s[...] = jnp.zeros_like(dk_s)
        dv_s[...] = jnp.zeros_like(dv_s)

        def step(i, masked):
            lse, delta = lse_ref[i], delta_s[i]
            if masked:
                _, stop, inside = block_range(start_ref, len_ref, i)
                query = i * blk + lax.broadcasted_iota(jnp.int32, (1, blk), 1)
                limit = jnp.maximum(query, jnp.where(inside > 0, stop * blk - 1, 0))
                key = j * keys + lax.broadcasted_iota(jnp.int32, (keys, blk), 0)
                seen = key <= limit
            dv, dk = dv_s[...], dk_s[...]
            for h in range(heads):
                q_h, g_h = q_s[h, i], g_s[h, i]
                p = jnp.exp(dot_nt(k_s[j], q_h) - lse[h : h + 1, :])
                if masked:
                    p = jnp.where(seen, p, 0.0)
                ds = (p * (dot_nt(v_s[j], g_h) - delta[h : h + 1, :])).astype(BF16)
                dv = dv + dot_nn(p.astype(BF16), g_h)
                dk = dk + dot_nn(ds, q_h)
                lo, hi = h * HEAD_DIM, (h + 1) * HEAD_DIM
                dqt_s[i, lo:hi, :] = dqt_s[i, lo:hi, :] + dot_nn(kt_s[j, lo:hi, :], ds)
            dv_s[...] = dv
            dk_s[...] = dk

        def masked_step(i, c):
            step(i, True)
            return c

        def open_step(i, c):
            step(i, False)
            return c

        lax.fori_loop(jnp.minimum(first, also), 2 * j + 2, masked_step, 0)
        lax.fori_loop(2 * j + 2, blocks, open_step, 0)
        for part in range(2):
            b = 2 * j + part
            t = lax.rem(z - b // per_chunk + tensor, tensor)
            here = pl.ds(lax.rem(b, per_chunk) * blk, blk)
            own = slice(part * blk, (part + 1) * blk)
            dqkv_ref[t, here, padded : 2 * padded] = dk_s[own, :].astype(BF16)
            dqkv_ref[t, here, 2 * padded : 3 * padded] = dv_s[own, :].astype(BF16)
        bias_ref[1:2, :] = bias_ref[1:2, :] + jnp.sum(dv_s[...], axis=0, keepdims=True)
        return carry

    lax.fori_loop(0, blocks // 2, one_pair, 0)

    def one_query(i, carry):
        dq = dqt_s[i].T * scale
        quarter = i // per_chunk
        t = lax.rem(z - quarter + tensor, tensor)
        here = pl.ds(lax.rem(i, per_chunk) * blk, blk)
        dqkv_ref[t, here, 0:padded] = dq.astype(BF16)
        bias_ref[0:1, :] = bias_ref[0:1, :] + jnp.sum(dq, axis=0, keepdims=True)
        return carry

    lax.fori_loop(0, blocks, one_query, 0)


def attend_backward(z, starts, lens, chunks, grads, mixed, lse, heads):
    tensor = len(chunks)
    rows, width = chunks[0].shape
    padded = width // 3
    seq, blk = tensor * rows, PIECE_BLOCK
    blocks = seq // blk
    smem = pl.BlockSpec(memory_space=pltpu.SMEM)
    vmem = pl.BlockSpec(memory_space=pltpu.VMEM)
    pairs = blocks * (blocks + 1) // 2
    return pl.pallas_call(
        functools.partial(attend_backward_kernel, heads),
        out_shape=(
            jax.ShapeDtypeStruct((tensor, rows, width), BF16),
            jax.ShapeDtypeStruct((8, padded), F32),
        ),
        in_specs=[smem] * 3 + [vmem] * (2 * tensor + 2),
        out_specs=(vmem, vmem),
        scratch_shapes=[
            pltpu.VMEM((heads, blocks, blk, padded), BF16),
            pltpu.VMEM((blocks // 2, 2 * blk, padded), BF16),
            pltpu.VMEM((blocks // 2, padded, 2 * blk), BF16),
            pltpu.VMEM((blocks // 2, 2 * blk, padded), BF16),
            pltpu.VMEM((heads, blocks, blk, padded), BF16),
            pltpu.VMEM((blocks, 8, blk), F32),
            pltpu.VMEM((blocks, padded, blk), F32),
            pltpu.VMEM((2 * blk, padded), F32),
            pltpu.VMEM((2 * blk, padded), F32),
        ],
        compiler_params=pltpu.CompilerParams(vmem_limit_bytes=VMEM_LIMIT),
        cost_estimate=pl.CostEstimate(
            flops=pairs * heads * blk * blk * 10 * 256,
            bytes_accessed=6 * seq * width,
            transcendentals=pairs * heads * blk * blk,
        ),
        name="attend_backward",
    )(z, starts, lens, *chunks, *grads, mixed, lse)


def weight_slots(tensor, dp, shard):
    if shard % 16:
        return [(0, t, t, None) for t in range(tensor)]
    bits = bits_of(dp)
    slots = []
    for side, order in enumerate((bits[1:], bits[1:][::-1])):
        offsets = [0]
        for bit in order:
            offsets = offsets + [o ^ bit for o in offsets]
        half = tensor // 2
        for n, offset in enumerate(offsets):
            for t in range(half):
                slots.append((2 * side, n * half + t, side * half + t, offset))
                slots.append((2 * side + 1, n * half + t, side * half + t, offset ^ bits[0]))
    return slots


def gathered_weights(part, dp, tensor, z):
    shard, columns = part.shape
    if shard % 16:
        whole = lax.all_gather(part, ("tensor", "dp"), axis=0, tiled=True)
        whole = whole.reshape(tensor, dp * shard, columns)
        order = (z - jnp.arange(tensor)) % tensor
        return [jnp.take(whole, order, axis=0)]
    ring = [part]
    for _ in range(tensor - 1):
        ring.append(shifted(ring[-1], "tensor", tensor, 1))
    bits = bits_of(dp)
    half = tensor // 2
    out = []
    for side, order in enumerate((bits[1:], bits[1:][::-1])):
        value = jnp.stack(ring[side * half : (side + 1) * half])
        for bit in order:
            value = jnp.concatenate([value, swapped(value, "dp", dp, bit)], axis=0)
        out += [value, swapped(value, "dp", dp, bits[0])]
    return out


def start_weights(slots, shard, place_ref, pieces, w_s, wo_s, sems, o_sem):
    wide = w_s.shape[2]
    for which, slot, t, offset in slots:
        if offset is None:
            here = slice(None)
        else:
            here = pl.ds(jnp.bitwise_xor(place_ref[1], offset) * shard, shard)
        pltpu.make_async_copy(
            pieces[which].at[slot, :, wide:], wo_s.at[t, here, :], o_sem
        ).start()
    for which, slot, t, offset in slots:
        if offset is None:
            here = slice(None)
        else:
            here = pl.ds(jnp.bitwise_xor(place_ref[1], offset) * shard, shard)
        pltpu.make_async_copy(
            pieces[which].at[slot, :, :wide], w_s.at[t, here, :], sems.at[t]
        ).start()


def center(values):
    mean = jnp.mean(values, axis=-1, keepdims=True)
    centered = values - mean
    spread = jnp.mean(centered * centered, axis=-1, keepdims=True)
    return centered, lax.rsqrt(spread + NORM_EPS)


def same_head(value):
    row = lax.broadcasted_iota(jnp.int32, (value, value), 0) // (value // POOL_HEADS)
    col = lax.broadcasted_iota(jnp.int32, (value, value), 1) // (value // POOL_HEADS)
    return (row == col).astype(F32)


def rows_forward_kernel(tensor, slots, shard, arrays, place_ref, *refs):
    mixed = refs[:tensor]
    tok_ref, vec_ref, bias_ref, proj_ref, cvec_ref = refs[tensor : tensor + 5]
    pieces = refs[tensor + 5 : tensor + 5 + arrays]
    (
        low_ref, xlow_ref, act_ref, slope_ref, xh1_ref, xh2_ref, rs_ref, stud_ref, mall_ref,
        e_ref, stats_ref, acc_s, w_s, wo_s, sems, o_sem,
    ) = refs[tensor + 5 + arrays :]
    j = pl.program_id(0)
    hidden = act_ref.shape[2]

    @pl.when(j == 0)
    def _():
        start_weights(slots, shard, place_ref, pieces, w_s, wo_s, sems, o_sem)
        total = tok_ref[...].astype(F32) + vec_ref[2:3, :]
        pltpu.make_async_copy(wo_s, wo_s, o_sem).wait()
        for s in range(tensor):
            piece = mixed[s][...]
            mall_ref[s] = piece
            total = total + dot_nt(piece, wo_s[s])
        centered, rstd = center(total)
        xhat = centered * rstd
        xh1_ref[...] = xhat
        rs_ref[:, 0:1] = rstd
        x_one = xhat * vec_ref[3:4, :] + vec_ref[4:5, :]
        xlow_ref[...] = x_one.astype(BF16)
        acc_s[...] = x_one + vec_ref[5:6, :]

    pltpu.make_async_copy(w_s.at[j], w_s.at[j], sems.at[j]).wait()
    upper = dot_nn(xlow_ref[...], w_s[j, :, 0:hidden]) + bias_ref[0]
    phi = 0.5 * (1.0 + lax.erf(upper * (0.5**0.5)))
    act = (upper * phi).astype(BF16)
    slope = phi + upper * (jnp.exp(-0.5 * upper * upper) * 0.3989422804014327)
    act_ref[0] = act
    slope_ref[0] = slope.astype(BF16)
    acc_s[...] = acc_s[...] + dot_nt(act, w_s[j, :, hidden:])

    @pl.when(j == pl.num_programs(0) - 1)
    def _():
        centered, rstd = center(acc_s[...])
        xhat = centered * rstd
        xh2_ref[...] = xhat
        rs_ref[:, 1:2] = rstd
        low = (xhat * vec_ref[6:7, :] + vec_ref[7:8, :]).astype(BF16)
        low_ref[...] = low
        student = dot_nn(low, proj_ref[...]) + cvec_ref[0:1, :]
        stud_ref[...] = student
        width = student.shape[1]
        scale = (width // POOL_HEADS) ** (-0.5)
        e = dot_nn(student * (cvec_ref[1:2, :] * scale), same_head(width), PRECISE)
        e_ref[...] = e
        top = jnp.max(e, axis=0, keepdims=True)
        w = jnp.exp(e - top)
        stats_ref[...] = jnp.concatenate(
            [
                top,
                jnp.sum(w, axis=0, keepdims=True),
                jnp.sum(w * student, axis=0, keepdims=True),
                jnp.zeros((5, width), F32),
            ],
            axis=0,
        )


def whole(*shape):
    return pl.BlockSpec(shape, lambda j, *_: (0,) * len(shape))


def block(*shape):
    return pl.BlockSpec((1,) + shape, lambda j, *_: (j,) + (0,) * len(shape))


def rows_forward(place, slots, pieces, mixed, tokens, vec_table, ff_bias, cls_proj, cls_vec):
    tensor = len(mixed)
    rows, width = tokens.shape
    head_width = mixed[0].shape[1]
    shard = pieces[0].shape[1]
    hidden = ff_bias.shape[2]
    ch = cls_proj.shape[1]
    far = pl.BlockSpec(memory_space=pl.ANY)

    def of_block(j, place_ref):
        return (lax.rem(place_ref[0] - j + tensor, tensor), 0, 0)

    return pl.pallas_call(
        functools.partial(rows_forward_kernel, tensor, slots, shard, len(pieces)),
        grid_spec=pltpu.PrefetchScalarGridSpec(
            num_scalar_prefetch=1,
            grid=(tensor,),
            in_specs=[whole(rows, head_width)] * tensor
            + [
                whole(rows, width),
                whole(8, width),
                pl.BlockSpec((1, 1, hidden), of_block),
                whole(width, ch),
                whole(3, ch),
            ]
            + [far] * len(pieces),
            out_specs=(
                whole(rows, width),
                whole(rows, width),
                block(rows, hidden),
                block(rows, hidden),
                whole(rows, width),
                whole(rows, width),
                whole(rows, 2),
                whole(rows, ch),
                whole(tensor, rows, head_width),
                whole(rows, ch),
                whole(8, ch),
            ),
            scratch_shapes=[
                pltpu.VMEM((rows, width), F32),
                pltpu.VMEM((tensor, width, 2 * hidden), BF16),
                pltpu.VMEM((tensor, width, head_width), BF16),
                pltpu.SemaphoreType.DMA((tensor,)),
                pltpu.SemaphoreType.DMA,
            ],
        ),
        out_shape=(
            jax.ShapeDtypeStruct((rows, width), BF16),
            jax.ShapeDtypeStruct((rows, width), BF16),
            jax.ShapeDtypeStruct((tensor, rows, hidden), BF16),
            jax.ShapeDtypeStruct((tensor, rows, hidden), BF16),
            jax.ShapeDtypeStruct((rows, width), F32),
            jax.ShapeDtypeStruct((rows, width), F32),
            jax.ShapeDtypeStruct((rows, 2), F32),
            jax.ShapeDtypeStruct((rows, ch), F32),
            jax.ShapeDtypeStruct((tensor, rows, head_width), BF16),
            jax.ShapeDtypeStruct((rows, ch), F32),
            jax.ShapeDtypeStruct((8, ch), F32),
        ),
        compiler_params=pltpu.CompilerParams(vmem_limit_bytes=VMEM_LIMIT),
        cost_estimate=pl.CostEstimate(
            flops=4 * rows * width * hidden * tensor + 2 * rows * width * width,
            bytes_accessed=4 * width * hidden * tensor + 20 * rows * width,
            transcendentals=2 * rows * hidden * tensor,
        ),
        name="rows_forward",
    )(place, *mixed, tokens, vec_table, ff_bias, cls_proj, cls_vec, *pieces)


def norm_back(grad, xhat, rstd, gain):
    g = grad * gain
    return (
        g - jnp.mean(g, axis=-1, keepdims=True) - xhat * jnp.mean(g * xhat, axis=-1, keepdims=True)
    ) * rstd


def rows_backward_kernel(tensor, slots, shard, arrays, place_ref, *refs):
    stats_refs = refs[:tensor]
    (
        stud_ref, e_ref, cot_ref, xh1_ref, xh2_ref, rs_ref, slope_ref, vec_ref, proj_ref,
        cvec_ref, chid_ref, cout_ref, cbias_ref,
    ) = refs[tensor : tensor + 13]
    pieces = refs[tensor + 13 : tensor + 13 + arrays]
    (
        logit_ref, two_ref, gu_ref, one_ref, gh1_ref, gm_ref, sums_ref, ffb_ref, gsl_ref,
        small_ref, ghid_ref, gout_ref, acc_s, w_s, wo_s, sems, o_sem,
    ) = refs[tensor + 13 + arrays :]
    j = pl.program_id(0)
    ch = stud_ref.shape[1]
    hidden = gu_ref.shape[2]
    scale = (ch // POOL_HEADS) ** (-0.5)

    @pl.when(j == 0)
    def _():
        start_weights(slots, shard, place_ref, pieces, w_s, wo_s, sems, o_sem)
        head_of = same_head(ch)
        first = (place_ref[0] == 0).astype(F32)
        stats = [r[...] for r in stats_refs]
        top = functools.reduce(jnp.maximum, [v[0:1, :] for v in stats])
        weights = [jnp.exp(v[0:1, :] - top) for v in stats]
        total = sum(v[1:2, :] * w for v, w in zip(stats, weights))
        pooled = sum(v[2:3, :] * w for v, w in zip(stats, weights)) / total

        first_row = lax.broadcasted_iota(jnp.int32, (8, ch), 0) == 0
        lane = lax.broadcasted_iota(jnp.int32, (8, ch), 1)
        pooled8 = jnp.broadcast_to(pooled, (8, ch))
        chid = chid_ref[...].astype(F32)
        cout = cout_ref[...].astype(F32)
        hid = jnp.tanh(dot_nn(pooled8, chid, PRECISE) + cvec_ref[2:3, :])
        logits = dot_nn(hid, cout, PRECISE) + cbias_ref[...]
        logit_ref[...] = logits
        real = lane < CLASSES
        masked = jnp.where(real, logits, MASK_FILL)
        powers = jnp.where(real, jnp.exp(masked - jnp.max(masked, axis=1, keepdims=True)), 0.0)
        probs = powers / jnp.sum(powers, axis=1, keepdims=True)
        grad_logits = probs - (lane == place_ref[2]).astype(F32)
        grad_pre = (1.0 - hid * hid) * dot_nt(grad_logits, cout, PRECISE)
        grad_pooled = dot_nt(grad_pre, chid, PRECISE)
        gl_row = jnp.where(first_row, grad_logits, 0.0) * first
        gp_row = jnp.where(first_row, grad_pre, 0.0) * first
        gout_ref[...] = dot_tn(hid, gl_row, PRECISE)
        ghid_ref[...] = dot_tn(pooled8, gp_row, PRECISE)
        base = dot_nn(grad_pooled * pooled8, head_of, PRECISE)[0:1, :]
        gp = grad_pooled[0:1, :]
        query = cvec_ref[1:2, :] * scale
        student = stud_ref[...]
        w = jnp.exp(e_ref[...] - top) / total
        grad_w = dot_nn(student * gp, head_of, PRECISE)
        grad_e = w * (grad_w - base)
        grad_student = w * gp + grad_e * query
        gsl = grad_student.astype(BF16)
        gsl_ref[...] = gsl
        small_ref[...] = jnp.concatenate(
            [
                jnp.sum(grad_student, axis=0, keepdims=True),
                jnp.sum(grad_e * student, axis=0, keepdims=True) * scale,
                gp_row[0:1, :],
                gl_row[0:1, :],
                jnp.zeros((4, ch), F32),
            ],
            axis=0,
        )
        grad = cot_ref[...].astype(F32) + dot_nt(gsl, proj_ref[...])
        xhat = xh2_ref[...]
        sums_ref[...] = jnp.zeros_like(sums_ref)
        sums_ref[6:7, :] = jnp.sum(grad * xhat, axis=0, keepdims=True)
        sums_ref[7:8, :] = jnp.sum(grad, axis=0, keepdims=True)
        two = norm_back(grad, xhat, rs_ref[:, 1:2], vec_ref[6:7, :])
        sums_ref[5:6, :] = jnp.sum(two, axis=0, keepdims=True)
        acc_s[...] = two
        two_ref[...] = two.astype(BF16)

    pltpu.make_async_copy(w_s.at[j], w_s.at[j], sems.at[j]).wait()
    upper = dot_nn(two_ref[...], w_s[j, :, hidden:]) * slope_ref[0].astype(F32)
    ffb_ref[0] = jnp.sum(upper, axis=0, keepdims=True)
    low = upper.astype(BF16)
    gu_ref[0] = low
    acc_s[...] = acc_s[...] + dot_nt(low, w_s[j, :, 0:hidden])

    @pl.when(j == pl.num_programs(0) - 1)
    def _():
        grad = acc_s[...]
        xhat = xh1_ref[...]
        sums_ref[3:4, :] = jnp.sum(grad * xhat, axis=0, keepdims=True)
        sums_ref[4:5, :] = jnp.sum(grad, axis=0, keepdims=True)
        one = norm_back(grad, xhat, rs_ref[:, 0:1], vec_ref[3:4, :])
        sums_ref[2:3, :] = jnp.sum(one, axis=0, keepdims=True)
        gh1_ref[...] = one
        low = one.astype(BF16)
        one_ref[...] = low
        pltpu.make_async_copy(wo_s, wo_s, o_sem).wait()
        for s in range(tensor):
            gm_ref[s] = dot_nn(low, wo_s[s]).astype(BF16)


def rows_backward(
    place, slots, pieces, stats, kept, cotangent, vec_table, cls_proj, cls_vec, cls_hidden,
    cls_out, cls_bias,
):
    _, _, _, slope, xh1, xh2, rs, student, mixed, pool_logit, _ = kept
    tensor, rows, hidden = slope.shape
    width = xh1.shape[1]
    head_width = mixed.shape[2]
    shard = pieces[0].shape[1]
    ch = student.shape[1]
    far = pl.BlockSpec(memory_space=pl.ANY)

    def of_block(j, place_ref):
        return (lax.rem(place_ref[0] - j + tensor, tensor), 0, 0)

    return pl.pallas_call(
        functools.partial(rows_backward_kernel, tensor, slots, shard, len(pieces)),
        grid_spec=pltpu.PrefetchScalarGridSpec(
            num_scalar_prefetch=1,
            grid=(tensor,),
            in_specs=[whole(8, ch)] * tensor
            + [
                whole(rows, ch),
                whole(rows, ch),
                whole(rows, width),
                whole(rows, width),
                whole(rows, width),
                whole(rows, 2),
                block(rows, hidden),
                whole(8, width),
                whole(width, ch),
                whole(3, ch),
                whole(ch, ch),
                whole(ch, ch),
                whole(1, ch),
            ]
            + [far] * len(pieces),
            out_specs=(
                whole(8, ch),
                whole(rows, width),
                block(rows, hidden),
                whole(rows, width),
                whole(rows, width),
                whole(tensor, rows, head_width),
                whole(8, width),
                pl.BlockSpec((1, 1, hidden), of_block),
                whole(rows, ch),
                whole(8, ch),
                whole(ch, ch),
                whole(ch, ch),
            ),
            scratch_shapes=[
                pltpu.VMEM((rows, width), F32),
                pltpu.VMEM((tensor, width, 2 * hidden), BF16),
                pltpu.VMEM((tensor, width, head_width), BF16),
                pltpu.SemaphoreType.DMA((tensor,)),
                pltpu.SemaphoreType.DMA,
            ],
        ),
        out_shape=(
            jax.ShapeDtypeStruct((8, ch), F32),
            jax.ShapeDtypeStruct((rows, width), BF16),
            jax.ShapeDtypeStruct((tensor, rows, hidden), BF16),
            jax.ShapeDtypeStruct((rows, width), BF16),
            jax.ShapeDtypeStruct((rows, width), F32),
            jax.ShapeDtypeStruct((tensor, rows, head_width), BF16),
            jax.ShapeDtypeStruct((8, width), F32),
            jax.ShapeDtypeStruct((tensor, 1, hidden), F32),
            jax.ShapeDtypeStruct((rows, ch), BF16),
            jax.ShapeDtypeStruct((8, ch), F32),
            jax.ShapeDtypeStruct((ch, ch), F32),
            jax.ShapeDtypeStruct((ch, ch), F32),
        ),
        compiler_params=pltpu.CompilerParams(vmem_limit_bytes=VMEM_LIMIT),
        cost_estimate=pl.CostEstimate(
            flops=4 * rows * width * hidden * tensor + 2 * rows * width * width,
            bytes_accessed=4 * width * hidden * tensor + 20 * rows * width,
            transcendentals=rows * ch,
        ),
        name="rows_backward",
    )(
        place, *stats, student, pool_logit, cotangent, xh1, xh2, rs, slope, vec_table, cls_proj,
        cls_vec, cls_hidden, cls_out, cls_bias, *pieces,
    )


def weight_grads_kernel(
    dp, shard, place_ref, x_ref, two_ref, one_ref, gu_ref, act_ref, mix_ref, low_ref, gsl_ref,
    *refs,
):
    outs, proj_ref = refs[:-4], refs[-4]
    lefts = refs[-3:]
    j = pl.program_id(0)
    hidden = gu_ref.shape[2]
    width = x_ref.shape[1]
    apart = len(outs) == 2

    @pl.when(j == 0)
    def _():
        for source, left in zip((x_ref, two_ref, one_ref), lefts):
            turned = source[...].T
            if not apart:
                left[...] = turned
                continue
            for b in range(dp):
                offset = jnp.bitwise_xor(place_ref[1], b)
                at = lax.rem(offset, 2) * (dp // 2) + offset // 2
                left[pl.ds(at * shard, shard), :] = turned[b * shard : (b + 1) * shard, :]
        proj_ref[...] = dot_tn(low_ref[...], gsl_ref[...])

    count = width // len(outs)
    rights = (gu_ref[0], act_ref[0], mix_ref[0])
    ends = (0, hidden, 2 * hidden, 2 * hidden + mix_ref.shape[2])
    for n, out in enumerate(outs):
        here = slice(n * count, (n + 1) * count)
        for m in range(3):
            part = dot_nn(lefts[m][here, :], rights[m]).astype(BF16)
            out[0, :, :, ends[m] : ends[m + 1]] = part.reshape(
                out.shape[1], out.shape[2], ends[m + 1] - ends[m]
            )


def weight_grads(
    place, dp, shard, x_low, two_low, one_low, upper_low, act, mixed, out_low, student_low
):
    tensor, rows, hidden = upper_low.shape
    width = x_low.shape[1]
    head_width = mixed.shape[2]
    ch = student_low.shape[1]
    total = 2 * hidden + head_width
    if shard % 16:
        parts = [(1, width)]
    else:
        parts = [(dp // 2, shard)] * 2
    return pl.pallas_call(
        functools.partial(weight_grads_kernel, dp, shard),
        grid_spec=pltpu.PrefetchScalarGridSpec(
            num_scalar_prefetch=1,
            grid=(tensor,),
            in_specs=[
                whole(rows, width),
                whole(rows, width),
                whole(rows, width),
                block(rows, hidden),
                block(rows, hidden),
                block(rows, head_width),
                whole(rows, width),
                whole(rows, ch),
            ],
            out_specs=tuple(block(*part, total) for part in parts) + (whole(width, ch),),
            scratch_shapes=[pltpu.VMEM((width, rows), BF16)] * 3,
        ),
        out_shape=tuple(jax.ShapeDtypeStruct((tensor, *part, total), BF16) for part in parts)
        + (jax.ShapeDtypeStruct((width, ch), F32),),
        compiler_params=pltpu.CompilerParams(vmem_limit_bytes=VMEM_LIMIT),
        cost_estimate=pl.CostEstimate(
            flops=2 * rows * width * total * tensor,
            bytes_accessed=2 * width * total * tensor + 4 * rows * hidden * tensor,
            transcendentals=0,
        ),
        name="weight_grads",
    )(place, x_low, two_low, one_low, upper_low, act, mixed, out_low, student_low)


def weights_to_owner(parts, dp, tensor, shard, z):
    if len(parts) == 1:
        order = (z - jnp.arange(tensor)) % tensor
        whole_parts = jnp.take(parts[0], order, axis=0)
        columns = whole_parts.shape[-1]
        return lax.psum_scatter(
            whole_parts.reshape(-1, columns), ("tensor", "dp"), scatter_dimension=0, tiled=True
        ).astype(F32)
    keep, give = parts
    bits = bits_of(dp)
    got = swapped(give, "dp", dp, bits[0])
    half = tensor // 2
    own = []
    for side, order in enumerate((bits[1:], bits[1:][::-1])):
        here = slice(side * half, (side + 1) * half)
        value = keep[here].astype(F32) + got[here].astype(F32)
        left = list(bits[1:])
        for bit in order:
            place = left.index(bit)
            low, high = 1 << place, 1 << (len(left) - 1 - place)
            shape = value.shape
            pairs = value.reshape(half, high, 2, low, *shape[2:])
            sent = swapped(pairs[:, :, 1].astype(BF16), "dp", dp, bit)
            value = (pairs[:, :, 0] + sent.astype(F32)).reshape(half, high * low, *shape[2:])
            left.remove(bit)
        own += [value[t, 0] for t in range(half)]
    total = own[1]
    for t in list(range(2, tensor)) + [0]:
        total = own[t] + shifted(total.astype(BF16), "tensor", tensor, 1).astype(F32)
    return total


def per_device(
    dp, tensor, tokens, cotangent, labels, piece_start, piece_len, w_qkv, w_out, w_up, w_down,
    vec_table, ff_bias, cls_proj, cls_vec, cls_hidden, cls_out, cls_bias,
):
    rows, width = tokens.shape
    local = w_qkv.shape[2]
    heads = local // HEAD_DIM
    padded = -(-local // LANES) * LANES
    shard = w_qkv.shape[0]
    hidden = w_up.shape[1]
    ch = cls_proj.shape[1]
    z = lax.axis_index("tensor")
    z_one = z.reshape(1).astype(jnp.int32)
    place = jnp.stack([z, lax.axis_index("dp"), labels[0]]).astype(jnp.int32)

    extra = padded - local
    qkv_shard = jnp.pad(w_qkv, ((0, 0), (0, 0), (0, extra))).reshape(shard, 3 * padded)
    w_in = gathered(qkv_shard, "dp", dp)
    pieces = gathered_weights(
        jnp.concatenate([w_up, w_down.T, w_out.T], axis=1), dp, tensor, z
    )
    slots = weight_slots(tensor, dp, shard)

    q_bias = lax.dynamic_slice_in_dim(vec_table[0], z * local, local, 0)
    v_bias = lax.dynamic_slice_in_dim(vec_table[1], z * local, local, 0)
    in_bias = jnp.pad(
        jnp.stack([q_bias, jnp.zeros_like(q_bias), v_bias]), ((0, 0), (0, extra))
    ).reshape(1, 3 * padded)

    seq_rows = [tokens]
    for _ in range(tensor - 1):
        seq_rows.append(shifted(seq_rows[-1], "tensor", tensor, 1))
    chunks = [
        (jnp.dot(part, w_in, preferred_element_type=F32) + in_bias).astype(BF16)
        for part in seq_rows
    ]
    mixed, lse = attend_forward(z_one, piece_start, piece_len, chunks, heads)

    def to_rows(parts):
        return [parts[0]] + [
            shifted(parts[tensor - s], "tensor", tensor, s) for s in range(1, tensor)
        ]

    kept = rows_forward(
        place, slots, pieces, to_rows(mixed), tokens, vec_table,
        ff_bias.reshape(tensor, 1, hidden), cls_proj, cls_vec,
    )
    out_low, x_low, act, _, _, _, _, _, mixed_all, _, stats = kept
    all_stats = [stats] + [shifted(stats, "tensor", tensor, s) for s in range(1, tensor)]
    (
        logits, two_low, upper_low, one_low, grad_h_one, grad_mixed, sums, ff_sums, student_low,
        small, grad_hid, grad_out_w,
    ) = rows_backward(
        place, slots, pieces, all_stats, kept, cotangent, vec_table, cls_proj, cls_vec,
        cls_hidden, jnp.pad(cls_out, ((0, 0), (0, ch - CLASSES))),
        jnp.pad(cls_bias, (0, ch - CLASSES)).reshape(1, ch),
    )
    grad_rows = to_rows(grad_mixed)
    *ff_parts, grad_proj = weight_grads(
        place, dp, shard, x_low, two_low, one_low, upper_low, act, mixed_all, out_low, student_low
    )
    ff_own = weights_to_owner(ff_parts, dp, tensor, shard, z)

    proj_sum, hid_sum, out_w_sum, small_sum, vec_sum, ff_bias_sum = lax.psum(
        (grad_proj, grad_hid, grad_out_w, small, sums, ff_sums.reshape(tensor, hidden)),
        ("dp", "tensor"),
    )

    d_chunks, bias_sums = attend_backward(
        z_one, piece_start, piece_len, chunks, grad_rows, mixed, lse, heads
    )
    total = None
    for t in list(range(1, tensor)) + [0]:
        part = lax.dot_general(
            d_chunks[t], w_in, (((1,), (1,)), ((), ())), preferred_element_type=F32
        )
        if total is not None:
            part = part + total.astype(F32)
        total = shifted(part.astype(BF16), "tensor", tensor, 1) if t else part
    grad_tokens = grad_h_one + total

    grad_in = None
    for t in range(tensor):
        part = lax.dot_general(
            seq_rows[t], d_chunks[t], (((0,), (0,)), ((), ())), preferred_element_type=F32
        )
        grad_in = part if grad_in is None else grad_in + part
    grad_in = summed_to_owner(grad_in.reshape(dp, shard, 3 * padded), "dp", dp)
    grad_w_qkv = grad_in.reshape(shard, 3, padded)[:, :, :local]

    bias_rows = lax.dynamic_update_slice(
        jnp.zeros((2, width), F32), bias_sums[:2, :local], (0, z * local)
    )
    bias_sum = summed(bias_rows, dp, tensor)
    grad_vec = jnp.concatenate([bias_sum, vec_sum[2:]], axis=0)
    return (
        out_low,
        logits[0:1, :CLASSES],
        grad_tokens,
        grad_w_qkv,
        ff_own[:, 2 * hidden :].T,
        ff_own[:, :hidden],
        ff_own[:, hidden : 2 * hidden].T,
        grad_vec,
        ff_bias_sum.reshape(-1),
        proj_sum,
        small_sum[:3],
        hid_sum,
        out_w_sum[:, :CLASSES],
        small_sum[3, :CLASSES],
    )


def solution(mesh):
    dp, tensor = mesh.shape["dp"], mesh.shape["tensor"]
    return jax.shard_map(
        functools.partial(per_device, dp, tensor),
        mesh=mesh,
        in_specs=(
            P(("dp", "tensor"), None),
            P(("dp", "tensor"), None),
            P("dp"),
            P("dp", None),
            P("dp", None),
            P("dp", None, "tensor"),
            P("tensor", "dp"),
            P("dp", "tensor"),
            P("tensor", "dp"),
            P(),
            P(),
            P(),
            P(),
            P(),
            P(),
            P(),
        ),
        out_specs=(
            P(("dp", "tensor"), None),
            P("dp", None),
            P(("dp", "tensor"), None),
            P("dp", None, "tensor"),
            P("tensor", "dp"),
            P("dp", "tensor"),
            P("tensor", "dp"),
            P(),
            P(),
            P(),
            P(),
            P(),
            P(),
            P(),
        ),
        check_vma=False,
    )
```

```python
import functools

import jax
import jax.numpy as jnp
from jax import lax
from jax.experimental import pallas as pl
from jax.experimental.pallas import tpu as pltpu
from jax.sharding import PartitionSpec as P

HEAD_DIM = 64
CLASSES = 14
PIECE_BLOCK = 256
POOL_HEADS = 2
LANES = 128
NORM_EPS = 1e-05
MASK_FILL = -1e30
PRECISE = lax.Precision.HIGHEST
F32 = jnp.float32
BF16 = jnp.bfloat16
VMEM_LIMIT = 48 * 1024 * 1024
LIGHT = pl.CostEstimate(flops=1024, bytes_accessed=1024, transcendentals=0)


def dot_nn(a, b, precision=None):
    return lax.dot_general(
        a, b, (((1,), (0,)), ((), ())), preferred_element_type=F32, precision=precision
    )


def dot_nt(a, b, precision=None):
    return lax.dot_general(
        a, b, (((1,), (1,)), ((), ())), preferred_element_type=F32, precision=precision
    )


def dot_tn(a, b, precision=None):
    return lax.dot_general(
        a, b, (((0,), (0,)), ((), ())), preferred_element_type=F32, precision=precision
    )


def bits_of(size):
    return [1 << n for n in range(size.bit_length() - 1)]


def swapped(value, axis, size, bit):
    return lax.ppermute(value, axis, [(i, i ^ bit) for i in range(size)])


def shifted(value, axis, size, by):
    return lax.ppermute(value, axis, [(i, (i + by) % size) for i in range(size)])


def after(value, *others):
    return lax.optimization_barrier((value, others))[0]


def in_turn(mark, chains, turns):
    under_way, results = {}, {}

    def advance(name, value):
        try:
            under_way[name] = chains[name].send(value)
        except StopIteration as end:
            under_way.pop(name, None)
            results[name] = end.value

    for name in chains:
        advance(name, None)
    turns = list(turns)
    while under_way:
        turn = turns.pop(0) if turns else tuple(under_way)
        names = [name for name in turn if name in under_way]
        if not names:
            continue
        sent = [value for value, _ in under_way.values()]
        there, mark, _ = lax.optimization_barrier(
            ([under_way[name][1] for name in names], mark, sent)
        )
        for name, value in zip(names, there):
            advance(name, value)
    return [results[name] for name in chains]


def ring_chain(value, size, kept):
    kept.append(value)
    for _ in range(size - 1):
        value = yield value, shifted(value, "tensor", size, 1)
        kept.append(value)
    return kept


def gather_chain(value, axis, size):
    index = lax.axis_index(axis)
    for bit in bits_of(size):
        other = yield value, swapped(value, axis, size, bit)
        low = (index // bit) % 2 == 0
        value = jnp.where(
            low, jnp.concatenate([value, other], 0), jnp.concatenate([other, value], 0)
        )
    return value


def owner_chain(parts, rider, axis, size, other, other_size):
    index = lax.axis_index(axis)
    riding = rider.shape[0]
    for bit in bits_of(size):
        mine = (index // bit) % 2
        count, rows, columns = parts.shape
        pairs = parts.reshape(count // 2, 2, rows, columns)
        keep = lax.dynamic_index_in_dim(pairs, mine, 1, keepdims=False)
        give = lax.dynamic_index_in_dim(pairs, 1 - mine, 1, keepdims=False)
        give = give.reshape(count // 2 * rows, columns)
        give = jnp.concatenate([give, rider]).astype(BF16)
        got = yield give, swapped(give, axis, size, bit)
        parts = keep + got[:-riding].reshape(keep.shape).astype(F32)
        rider = rider.astype(BF16).astype(F32) + got[-riding:].astype(F32)
    got = yield rider, [shifted(rider, other, other_size, by) for by in range(1, other_size)]
    place = lax.axis_index(other)
    riders = jnp.zeros((other_size, *rider.shape), F32)
    for by, value in enumerate([rider] + list(got)):
        riders = lax.dynamic_update_index_in_dim(riders, value, (place - by) % other_size, 0)
    return parts[0], riders


INFO_Z, INFO_D, INFO_LABEL, INFO_PIECES = 0, 1, 2, 3


def part_of(info_ref, place, tensor):
    return lax.rem(info_ref[INFO_Z] - place + tensor, tensor)


def block_range(info_ref, block):
    first, stop, inside_any = block, block + 1, jnp.int32(0)
    pieces = (info_ref.shape[0] - INFO_PIECES) // 2
    for piece in range(pieces):
        begin, count = info_ref[INFO_PIECES + piece], info_ref[INFO_PIECES + pieces + piece]
        inside = jnp.logical_and(block >= begin, block < begin + count)
        first = jnp.where(inside, begin, first)
        stop = jnp.where(inside, begin + count, stop)
        inside_any = jnp.where(inside, jnp.int32(1), inside_any)
    return first, stop, inside_any


def head_lanes(shape, head):
    lane = lax.broadcasted_iota(jnp.int32, shape, len(shape) - 1)
    return (lane >= head * HEAD_DIM) & (lane < (head + 1) * HEAD_DIM)


def attend_forward_kernel(heads, info_ref, *refs):
    tensor = len(refs) - 2 - 3
    chunks = refs[:tensor]
    o_ref, lse_ref = refs[tensor : tensor + 2]
    q_s, k_s, vt_s = refs[tensor + 2 :]
    rows, padded = chunks[0].shape[0], chunks[0].shape[1] // 3
    blk = PIECE_BLOCK
    blocks = tensor * rows // blk
    per_chunk = rows // blk
    scale = HEAD_DIM ** (-0.5)
    for t in range(tensor):
        quarter = part_of(info_ref, t, tensor)
        for part in range(per_chunk):
            b = quarter * per_chunk + part
            here = pl.ds(part * blk, blk)
            q = chunks[t][here, 0:padded]
            for h in range(heads):
                q_s[h, b] = jnp.where(head_lanes(q.shape, h), q * scale, 0.0).astype(BF16)
            pair, at = b // 2, lax.rem(b, 2) * blk
            k_s[pair, pl.ds(at, blk), :] = chunks[t][here, padded : 2 * padded]
            vt = chunks[t][here, 2 * padded : 3 * padded].T
            for side in range(2):

                @pl.when(lax.rem(b, 2) == side)
                def _():
                    vt_s[pair, :, side * blk : (side + 1) * blk] = vt


    def one_query(i, carry):
        _, stop, inside = block_range(info_ref, i)
        q_h = [q_s[h, i] for h in range(heads)]
        query = i * blk + lax.broadcasted_iota(jnp.int32, (1, blk), 1)
        limit = jnp.maximum(query, jnp.where(inside > 0, stop * blk - 1, 0))

        def step(j, state, masked):
            tops, totals, mixed = state
            keys = 2 * blk
            if masked:
                key = j * keys + lax.broadcasted_iota(jnp.int32, (keys, blk), 0)
                seen = key <= limit
            k_j = k_s[j]
            scores = [dot_nt(k_j, q_h[h]) for h in range(heads)]
            if masked:
                scores = [jnp.where(seen, s, MASK_FILL) for s in scores]
            new_tops = [
                jnp.maximum(tops[h], jnp.max(scores[h], axis=0, keepdims=True))
                for h in range(heads)
            ]
            ps = [jnp.exp(scores[h] - new_tops[h]) for h in range(heads)]
            fades = [jnp.exp(tops[h] - new_tops[h]) for h in range(heads)]
            new_totals = [
                totals[h] * fades[h] + jnp.sum(ps[h], axis=0, keepdims=True) for h in range(heads)
            ]
            new_mixed = [
                mixed[h] * fades[h]
                + dot_nn(vt_s[j, h * HEAD_DIM : (h + 1) * HEAD_DIM, :], ps[h].astype(BF16))
                for h in range(heads)
            ]
            return tuple(new_tops), tuple(new_totals), tuple(new_mixed)

        state = (
            tuple(jnp.full((1, blk), MASK_FILL, F32) for _ in range(heads)),
            tuple(jnp.zeros((1, blk), F32) for _ in range(heads)),
            tuple(jnp.zeros((HEAD_DIM, blk), F32) for _ in range(heads)),
        )
        last = i // 2
        state = lax.fori_loop(0, last, lambda j, c: step(j, c, False), state)
        state = step(last, state, True)
        tops, totals, mixed = lax.fori_loop(
            last + 1, (stop + 1) // 2, lambda j, c: step(j, c, True), state
        )
        outs = [mixed[h] * (1.0 / totals[h]) for h in range(heads)]
        lses = [tops[h] + jnp.log(totals[h]) for h in range(heads)]
        t = part_of(info_ref, i // per_chunk, tensor)
        here = pl.ds(lax.rem(i, per_chunk) * blk, blk)
        o_ref[t, here, :] = jnp.concatenate(outs, axis=0).T.astype(BF16)
        lse_ref[i] = jnp.concatenate(lses + [jnp.zeros((8 - heads, blk), F32)], axis=0)
        return carry

    lax.fori_loop(0, blocks, one_query, 0)


def attend_forward(info, chunks, heads):
    tensor = len(chunks)
    rows, width = chunks[0].shape
    padded = width // 3
    seq, blk = tensor * rows, PIECE_BLOCK
    blocks = seq // blk
    smem = pl.BlockSpec(memory_space=pltpu.SMEM)
    vmem = pl.BlockSpec(memory_space=pltpu.VMEM)
    return pl.pallas_call(
        functools.partial(attend_forward_kernel, heads),
        out_shape=(
            jax.ShapeDtypeStruct((tensor, rows, heads * HEAD_DIM), BF16),
            jax.ShapeDtypeStruct((blocks, 8, blk), F32),
        ),
        in_specs=[smem] + [vmem] * tensor,
        out_specs=(vmem, vmem),
        scratch_shapes=[
            pltpu.VMEM((heads, blocks, blk, padded), BF16),
            pltpu.VMEM((blocks // 2, 2 * blk, padded), BF16),
            pltpu.VMEM((blocks // 2, padded, 2 * blk), BF16),
        ],
        compiler_params=pltpu.CompilerParams(vmem_limit_bytes=VMEM_LIMIT),
        cost_estimate=LIGHT,
        name="attend_forward",
    )(info, *chunks)


def attend_backward_kernel(heads, info_ref, *refs):
    tensor = (len(refs) - 2 - 2 - 9) // 2
    chunks, grads = refs[:tensor], refs[tensor : 2 * tensor]
    o_ref, lse_ref, dqkv_ref, bias_ref = refs[2 * tensor : 2 * tensor + 4]
    q_s, k_s, kt_s, v_s, g_s, delta_s, dqt_s, dk_s, dv_s = refs[2 * tensor + 4 :]
    rows, padded = chunks[0].shape[0], chunks[0].shape[1] // 3
    width = heads * HEAD_DIM
    blk = PIECE_BLOCK
    blocks = tensor * rows // blk
    per_chunk = rows // blk
    scale = HEAD_DIM ** (-0.5)
    for t in range(tensor):
        quarter = part_of(info_ref, t, tensor)
        for part in range(per_chunk):
            b = quarter * per_chunk + part
            here = pl.ds(part * blk, blk)
            q = chunks[t][here, 0:padded]
            g = grads[t][here, :]
            for h in range(heads):
                q_s[h, b] = jnp.where(head_lanes(q.shape, h), q * scale, 0.0).astype(BF16)
                g_s[h, b, :, 0:width] = jnp.where(head_lanes(g.shape, h), g, 0.0).astype(BF16)
                if padded > width:
                    g_s[h, b, :, width:padded] = jnp.zeros((blk, padded - width), BF16)
            k = chunks[t][here, padded : 2 * padded]
            pair, at = b // 2, lax.rem(b, 2) * blk
            k_s[pair, pl.ds(at, blk), :] = k
            v_s[pair, pl.ds(at, blk), :] = chunks[t][here, 2 * padded : 3 * padded]
            kt = k.T
            for side in range(2):

                @pl.when(lax.rem(b, 2) == side)
                def _():
                    kt_s[pair, :, side * blk : (side + 1) * blk] = kt

            prod = (g.astype(F32) * o_ref[t, here, :].astype(F32)).T
            sums = [
                jnp.sum(prod[h * HEAD_DIM : (h + 1) * HEAD_DIM, :], axis=0, keepdims=True)
                for h in range(heads)
            ]
            delta_s[b] = jnp.concatenate(sums + [jnp.zeros((8 - heads, blk), F32)], axis=0)
            dqt_s[b] = jnp.zeros((padded, blk), F32)
    bias_ref[...] = jnp.zeros_like(bias_ref)

    keys = 2 * blk

    def one_pair(j, carry):
        first, _, _ = block_range(info_ref, 2 * j)
        also, _, _ = block_range(info_ref, 2 * j + 1)
        dk_s[...] = jnp.zeros_like(dk_s)
        dv_s[...] = jnp.zeros_like(dv_s)

        def step(i, masked):
            lse, delta = lse_ref[i], delta_s[i]
            if masked:
                _, stop, inside = block_range(info_ref, i)
                query = i * blk + lax.broadcasted_iota(jnp.int32, (1, blk), 1)
                limit = jnp.maximum(query, jnp.where(inside > 0, stop * blk - 1, 0))
                key = j * keys + lax.broadcasted_iota(jnp.int32, (keys, blk), 0)
                seen = key <= limit
            k_j, v_j = k_s[j], v_s[j]
            q_h = [q_s[h, i] for h in range(heads)]
            g_h = [g_s[h, i] for h in range(heads)]
            lows, ds = [], []
            for h in range(heads):
                p = jnp.exp(dot_nt(k_j, q_h[h]) - lse[h : h + 1, :])
                dp = dot_nt(v_j, g_h[h])
                if masked:
                    p = jnp.where(seen, p, 0.0)
                lows.append(p.astype(BF16))
                ds.append((p * (dp - delta[h : h + 1, :])).astype(BF16))
            dv_s[...] += dot_nn(jnp.concatenate(lows, axis=1), jnp.concatenate(g_h, axis=0))
            dk_s[...] += dot_nn(jnp.concatenate(ds, axis=1), jnp.concatenate(q_h, axis=0))
            for h in range(heads):
                lo, hi = h * HEAD_DIM, (h + 1) * HEAD_DIM
                dqt_s[i, lo:hi, :] += dot_nn(kt_s[j, lo:hi, :], ds[h])

        def masked_step(i, c):
            step(i, True)
            return c

        def open_step(i, c):
            step(i, False)
            return c

        lax.fori_loop(jnp.minimum(first, also), 2 * j + 2, masked_step, 0)
        lax.fori_loop(2 * j + 2, blocks, open_step, 0)
        for part in range(2):
            b = 2 * j + part
            t = part_of(info_ref, b // per_chunk, tensor)
            here = pl.ds(lax.rem(b, per_chunk) * blk, blk)
            side = slice(part * blk, (part + 1) * blk)
            dqkv_ref[t, here, padded : 2 * padded] = dk_s[side, :].astype(BF16)
            dqkv_ref[t, here, 2 * padded : 3 * padded] = dv_s[side, :].astype(BF16)
        bias_ref[1:2, :] = bias_ref[1:2, :] + jnp.sum(dv_s[...], axis=0, keepdims=True)
        return carry

    lax.fori_loop(0, blocks // 2, one_pair, 0)

    def one_query(i, carry):
        dq = dqt_s[i].T * scale
        t = part_of(info_ref, i // per_chunk, tensor)
        here = pl.ds(lax.rem(i, per_chunk) * blk, blk)
        dqkv_ref[t, here, 0:padded] = dq.astype(BF16)
        bias_ref[0:1, :] = bias_ref[0:1, :] + jnp.sum(dq, axis=0, keepdims=True)
        return carry

    lax.fori_loop(0, blocks, one_query, 0)


def attend_backward(info, chunks, grads, mixed, lse, heads):
    tensor = len(chunks)
    rows, width = chunks[0].shape
    padded = width // 3
    seq, blk = tensor * rows, PIECE_BLOCK
    blocks = seq // blk
    smem = pl.BlockSpec(memory_space=pltpu.SMEM)
    vmem = pl.BlockSpec(memory_space=pltpu.VMEM)
    return pl.pallas_call(
        functools.partial(attend_backward_kernel, heads),
        out_shape=(
            jax.ShapeDtypeStruct((tensor, rows, width), BF16),
            jax.ShapeDtypeStruct((8, padded), F32),
        ),
        in_specs=[smem] + [vmem] * (2 * tensor + 2),
        out_specs=(vmem, vmem),
        scratch_shapes=[
            pltpu.VMEM((heads, blocks, blk, padded), BF16),
            pltpu.VMEM((blocks // 2, 2 * blk, padded), BF16),
            pltpu.VMEM((blocks // 2, padded, 2 * blk), BF16),
            pltpu.VMEM((blocks // 2, 2 * blk, padded), BF16),
            pltpu.VMEM((heads, blocks, blk, padded), BF16),
            pltpu.VMEM((blocks, 8, blk), F32),
            pltpu.VMEM((blocks, padded, blk), F32),
            pltpu.VMEM((2 * blk, padded), F32),
            pltpu.VMEM((2 * blk, padded), F32),
        ],
        compiler_params=pltpu.CompilerParams(vmem_limit_bytes=VMEM_LIMIT),
        cost_estimate=LIGHT,
        name="attend_backward",
    )(info, *chunks, *grads, mixed, lse)


def start_weights(pieces, w_s, wo_s, sems, o_sem):
    wide = w_s.shape[2]
    copies = []
    t = 0
    for piece in pieces:
        blocks, parts, rows, _ = piece.shape
        for part in range(parts):
            for n in range(blocks):
                copies.append((piece.at[n, part], t, pl.ds(n * rows, rows)))
            t += 1
    for source, t, here in copies:
        pltpu.make_async_copy(source.at[:, wide:], wo_s.at[t, here, :], o_sem).start()
    for source, t, here in copies:
        pltpu.make_async_copy(source.at[:, :wide], w_s.at[t, here, :], sems.at[t]).start()


def center(values):
    mean = jnp.mean(values, axis=-1, keepdims=True)
    centered = values - mean
    spread = jnp.mean(centered * centered, axis=-1, keepdims=True)
    return centered, lax.rsqrt(spread + NORM_EPS)


def same_head(value):
    row = lax.broadcasted_iota(jnp.int32, (value, value), 0) // (value // POOL_HEADS)
    col = lax.broadcasted_iota(jnp.int32, (value, value), 1) // (value // POOL_HEADS)
    return (row == col).astype(F32)


def rows_forward_kernel(tensor, arrays, info_ref, *refs):
    mixed = refs[:tensor]
    tok_ref, vec_ref, bias_ref, proj_ref, cvec_ref = refs[tensor : tensor + 5]
    pieces = refs[tensor + 5 : tensor + 5 + arrays]
    (
        low_ref, xlow_ref, act_ref, slope_ref, xh1_ref, xh2_ref, rs_ref, stud_ref, mall_ref,
        e_ref, stats_ref, acc_s, w_s, wo_s, sems, o_sem,
    ) = refs[tensor + 5 + arrays :]
    j = pl.program_id(0)
    hidden = act_ref.shape[2]

    @pl.when(j == 0)
    def _():
        start_weights(pieces, w_s, wo_s, sems, o_sem)
        total = tok_ref[...].astype(F32) + vec_ref[2:3, :]
        pltpu.make_async_copy(wo_s, wo_s, o_sem).wait()
        for s in range(tensor):
            piece = mixed[s][...]
            mall_ref[s] = piece
            total = total + dot_nt(piece, wo_s[s])
        centered, rstd = center(total)
        xhat = centered * rstd
        xh1_ref[...] = xhat
        rs_ref[:, 0:1] = rstd
        x_one = xhat * vec_ref[3:4, :] + vec_ref[4:5, :]
        xlow_ref[...] = x_one.astype(BF16)
        acc_s[...] = x_one + vec_ref[5:6, :]

    pltpu.make_async_copy(w_s.at[j], w_s.at[j], sems.at[j]).wait()
    upper = dot_nn(xlow_ref[...], w_s[j, :, 0:hidden]) + bias_ref[0]
    phi = 0.5 * (1.0 + lax.erf(upper * (0.5**0.5)))
    act = (upper * phi).astype(BF16)
    slope = phi + upper * (jnp.exp(-0.5 * upper * upper) * 0.3989422804014327)
    act_ref[0] = act
    slope_ref[0] = slope.astype(BF16)
    acc_s[...] = acc_s[...] + dot_nt(act, w_s[j, :, hidden:])

    @pl.when(j == pl.num_programs(0) - 1)
    def _():
        centered, rstd = center(acc_s[...])
        xhat = centered * rstd
        xh2_ref[...] = xhat
        rs_ref[:, 1:2] = rstd
        low = (xhat * vec_ref[6:7, :] + vec_ref[7:8, :]).astype(BF16)
        low_ref[...] = low
        student = dot_nn(low, proj_ref[...]) + cvec_ref[0:1, :]
        stud_ref[...] = student
        width = student.shape[1]
        scale = (width // POOL_HEADS) ** (-0.5)
        e = dot_nn(student * (cvec_ref[1:2, :] * scale), same_head(width), PRECISE)
        e_ref[...] = e
        top = jnp.max(e, axis=0, keepdims=True)
        w = jnp.exp(e - top)
        stats_ref[...] = jnp.concatenate(
            [
                top,
                jnp.sum(w, axis=0, keepdims=True),
                jnp.sum(w * student, axis=0, keepdims=True),
                jnp.zeros((5, width), F32),
            ],
            axis=0,
        )


def whole(*shape):
    return pl.BlockSpec(shape, lambda j, *_: (0,) * len(shape))


def block(*shape):
    return pl.BlockSpec((1,) + shape, lambda j, *_: (j,) + (0,) * len(shape))


def rows_forward(info, pieces, mixed, tokens, vec_table, ff_bias, cls_proj, cls_vec):
    tensor = len(mixed)
    rows, width = tokens.shape
    head_width = mixed[0].shape[1]
    hidden = ff_bias.shape[2]
    ch = cls_proj.shape[1]
    far = pl.BlockSpec(memory_space=pl.ANY)

    def of_block(j, info_ref):
        return (part_of(info_ref, j, tensor), 0, 0)

    return pl.pallas_call(
        functools.partial(rows_forward_kernel, tensor, len(pieces)),
        grid_spec=pltpu.PrefetchScalarGridSpec(
            num_scalar_prefetch=1,
            grid=(tensor,),
            in_specs=[whole(rows, head_width)] * tensor
            + [
                whole(rows, width),
                whole(8, width),
                pl.BlockSpec((1, 1, hidden), of_block),
                whole(width, ch),
                whole(3, ch),
            ]
            + [far] * len(pieces),
            out_specs=(
                whole(rows, width),
                whole(rows, width),
                block(rows, hidden),
                block(rows, hidden),
                whole(rows, width),
                whole(rows, width),
                whole(rows, 2),
                whole(rows, ch),
                whole(tensor, rows, head_width),
                whole(rows, ch),
                whole(8, ch),
            ),
            scratch_shapes=[
                pltpu.VMEM((rows, width), F32),
                pltpu.VMEM((tensor, width, 2 * hidden), BF16),
                pltpu.VMEM((tensor, width, head_width), BF16),
                pltpu.SemaphoreType.DMA((tensor,)),
                pltpu.SemaphoreType.DMA,
            ],
        ),
        out_shape=(
            jax.ShapeDtypeStruct((rows, width), BF16),
            jax.ShapeDtypeStruct((rows, width), BF16),
            jax.ShapeDtypeStruct((tensor, rows, hidden), BF16),
            jax.ShapeDtypeStruct((tensor, rows, hidden), BF16),
            jax.ShapeDtypeStruct((rows, width), F32),
            jax.ShapeDtypeStruct((rows, width), F32),
            jax.ShapeDtypeStruct((rows, 2), F32),
            jax.ShapeDtypeStruct((rows, ch), F32),
            jax.ShapeDtypeStruct((tensor, rows, head_width), BF16),
            jax.ShapeDtypeStruct((rows, ch), F32),
            jax.ShapeDtypeStruct((8, ch), F32),
        ),
        compiler_params=pltpu.CompilerParams(vmem_limit_bytes=VMEM_LIMIT),
        cost_estimate=LIGHT,
        name="rows_forward",
    )(info, *mixed, tokens, vec_table, ff_bias, cls_proj, cls_vec, *pieces)


def norm_back(grad, xhat, rstd, gain):
    g = grad * gain
    return (
        g - jnp.mean(g, axis=-1, keepdims=True) - xhat * jnp.mean(g * xhat, axis=-1, keepdims=True)
    ) * rstd


def rows_backward_kernel(tensor, arrays, info_ref, *refs):
    stats_refs = refs[:tensor]
    (
        stud_ref, e_ref, cot_ref, xh1_ref, xh2_ref, rs_ref, slope_ref, vec_ref, proj_ref,
        cvec_ref, chid_ref, cout_ref, cbias_ref,
    ) = refs[tensor : tensor + 13]
    pieces = refs[tensor + 13 : tensor + 13 + arrays]
    (
        logit_ref, two_ref, gu_ref, one_ref, gh1_ref, gm_ref, gsl_ref, pack_ref, acc_s, w_s, wo_s,
        sems, o_sem,
    ) = refs[tensor + 13 + arrays :]
    j = pl.program_id(0)
    ch = stud_ref.shape[1]
    hidden = gu_ref.shape[2]
    scale = (ch // POOL_HEADS) ** (-0.5)
    width = cot_ref.shape[1]
    sums_at = 8 + 2 * ch
    bias_at = sums_at + 6 * (width // ch)

    def pack_row(row, value):
        at = sums_at + (row - 2) * (width // ch)
        for n in range(width // ch):
            pack_ref[at + n : at + n + 1, :] = value[:, n * ch : (n + 1) * ch]

    @pl.when(j == 0)
    def _():
        start_weights(pieces, w_s, wo_s, sems, o_sem)
        head_of = same_head(ch)
        first = (info_ref[INFO_Z] == 0).astype(F32)
        stats = [r[...] for r in stats_refs]
        top = functools.reduce(jnp.maximum, [v[0:1, :] for v in stats])
        weights = [jnp.exp(v[0:1, :] - top) for v in stats]
        total = sum(v[1:2, :] * w for v, w in zip(stats, weights))
        pooled = sum(v[2:3, :] * w for v, w in zip(stats, weights)) / total

        first_row = lax.broadcasted_iota(jnp.int32, (8, ch), 0) == 0
        lane = lax.broadcasted_iota(jnp.int32, (8, ch), 1)
        pooled8 = jnp.broadcast_to(pooled, (8, ch))
        chid = chid_ref[...].astype(F32)
        cout = cout_ref[...].astype(F32)
        hid = jnp.tanh(dot_nn(pooled8, chid, PRECISE) + cvec_ref[2:3, :])
        logits = dot_nn(hid, cout, PRECISE) + cbias_ref[...]
        logit_ref[...] = logits
        real = lane < CLASSES
        masked = jnp.where(real, logits, MASK_FILL)
        powers = jnp.where(real, jnp.exp(masked - jnp.max(masked, axis=1, keepdims=True)), 0.0)
        probs = powers / jnp.sum(powers, axis=1, keepdims=True)
        grad_logits = probs - (lane == info_ref[INFO_LABEL]).astype(F32)
        grad_pre = (1.0 - hid * hid) * dot_nt(grad_logits, cout, PRECISE)
        grad_pooled = dot_nt(grad_pre, chid, PRECISE)
        gl_row = jnp.where(first_row, grad_logits, 0.0) * first
        gp_row = jnp.where(first_row, grad_pre, 0.0) * first
        pack_ref[8 : 8 + ch, :] = dot_tn(pooled8, gp_row, PRECISE)
        pack_ref[8 + ch : 8 + 2 * ch, :] = dot_tn(hid, gl_row, PRECISE)
        base = dot_nn(grad_pooled * pooled8, head_of, PRECISE)[0:1, :]
        gp = grad_pooled[0:1, :]
        query = cvec_ref[1:2, :] * scale
        student = stud_ref[...]
        w = jnp.exp(e_ref[...] - top) / total
        grad_w = dot_nn(student * gp, head_of, PRECISE)
        grad_e = w * (grad_w - base)
        grad_student = w * gp + grad_e * query
        gsl = grad_student.astype(BF16)
        gsl_ref[...] = gsl
        pack_ref[0:8, :] = jnp.concatenate(
            [
                jnp.sum(grad_student, axis=0, keepdims=True),
                jnp.sum(grad_e * student, axis=0, keepdims=True) * scale,
                gp_row[0:1, :],
                gl_row[0:1, :],
                jnp.zeros((4, ch), F32),
            ],
            axis=0,
        )
        grad = cot_ref[...].astype(F32) + dot_nt(gsl, proj_ref[...])
        xhat = xh2_ref[...]
        pack_row(6, jnp.sum(grad * xhat, axis=0, keepdims=True))
        pack_row(7, jnp.sum(grad, axis=0, keepdims=True))
        two = norm_back(grad, xhat, rs_ref[:, 1:2], vec_ref[6:7, :])
        pack_row(5, jnp.sum(two, axis=0, keepdims=True))
        acc_s[...] = two
        two_ref[...] = two.astype(BF16)

    pltpu.make_async_copy(w_s.at[j], w_s.at[j], sems.at[j]).wait()
    upper = dot_nn(two_ref[...], w_s[j, :, hidden:]) * slope_ref[0].astype(F32)
    heads_row = part_of(info_ref, j, tensor)
    bias_row = jnp.sum(upper, axis=0, keepdims=True)
    for n in range(hidden // ch):
        pack_ref[pl.ds(bias_at + heads_row * (hidden // ch) + n, 1), :] = bias_row[
            :, n * ch : (n + 1) * ch
        ]
    low = upper.astype(BF16)
    gu_ref[0] = low
    acc_s[...] = acc_s[...] + dot_nt(low, w_s[j, :, 0:hidden])

    @pl.when(j == pl.num_programs(0) - 1)
    def _():
        grad = acc_s[...]
        xhat = xh1_ref[...]
        pack_row(3, jnp.sum(grad * xhat, axis=0, keepdims=True))
        pack_row(4, jnp.sum(grad, axis=0, keepdims=True))
        one = norm_back(grad, xhat, rs_ref[:, 0:1], vec_ref[3:4, :])
        pack_row(2, jnp.sum(one, axis=0, keepdims=True))
        gh1_ref[...] = one
        low = one.astype(BF16)
        one_ref[...] = low
        pltpu.make_async_copy(wo_s, wo_s, o_sem).wait()
        for s in range(tensor):
            gm_ref[s] = dot_nn(low, wo_s[s]).astype(BF16)


def rows_backward(
    info, pieces, stats, kept, cotangent, vec_table, cls_proj, cls_vec, cls_hidden,
    cls_out, cls_bias,
):
    _, _, _, slope, xh1, xh2, rs, student, mixed, pool_logit, _ = kept
    tensor, rows, hidden = slope.shape
    width = xh1.shape[1]
    head_width = mixed.shape[2]
    ch = student.shape[1]
    far = pl.BlockSpec(memory_space=pl.ANY)
    pack_rows = 8 + 2 * ch + (6 * width + tensor * hidden) // ch

    return pl.pallas_call(
        functools.partial(rows_backward_kernel, tensor, len(pieces)),
        grid_spec=pltpu.PrefetchScalarGridSpec(
            num_scalar_prefetch=1,
            grid=(tensor,),
            in_specs=[whole(8, ch)] * tensor
            + [
                whole(rows, ch),
                whole(rows, ch),
                whole(rows, width),
                whole(rows, width),
                whole(rows, width),
                whole(rows, 2),
                block(rows, hidden),
                whole(8, width),
                whole(width, ch),
                whole(3, ch),
                whole(ch, ch),
                whole(ch, ch),
                whole(1, ch),
            ]
            + [far] * len(pieces),
            out_specs=(
                whole(8, ch),
                whole(rows, width),
                block(rows, hidden),
                whole(rows, width),
                whole(rows, width),
                whole(tensor, rows, head_width),
                whole(rows, ch),
                whole(pack_rows, ch),
            ),
            scratch_shapes=[
                pltpu.VMEM((rows, width), F32),
                pltpu.VMEM((tensor, width, 2 * hidden), BF16),
                pltpu.VMEM((tensor, width, head_width), BF16),
                pltpu.SemaphoreType.DMA((tensor,)),
                pltpu.SemaphoreType.DMA,
            ],
        ),
        out_shape=(
            jax.ShapeDtypeStruct((8, ch), F32),
            jax.ShapeDtypeStruct((rows, width), BF16),
            jax.ShapeDtypeStruct((tensor, rows, hidden), BF16),
            jax.ShapeDtypeStruct((rows, width), BF16),
            jax.ShapeDtypeStruct((rows, width), F32),
            jax.ShapeDtypeStruct((tensor, rows, head_width), BF16),
            jax.ShapeDtypeStruct((rows, ch), BF16),
            jax.ShapeDtypeStruct((pack_rows, ch), F32),
        ),
        compiler_params=pltpu.CompilerParams(vmem_limit_bytes=VMEM_LIMIT),
        cost_estimate=LIGHT,
        name="rows_backward",
    )(
        info, *stats, student, pool_logit, cotangent, xh1, xh2, rs, slope, vec_table, cls_proj,
        cls_vec, cls_hidden, cls_out, cls_bias, *pieces,
    )


def weight_grads_kernel(
    dp, shard, info_ref, x_ref, two_ref, one_ref, gu_ref, act_ref, mix_ref, low_ref, gsl_ref,
    *refs,
):
    outs, proj_ref = refs[:-4], refs[-4]
    lefts = refs[-3:]
    j = pl.program_id(0)
    hidden = gu_ref.shape[2]
    width = x_ref.shape[1]
    apart = len(outs) == 2

    @pl.when(j == 0)
    def _():
        for source, left in zip((x_ref, two_ref, one_ref), lefts):
            turned = source[...].T
            if not apart:
                left[...] = turned
                continue
            for b in range(dp):
                offset = jnp.bitwise_xor(info_ref[INFO_D], b)
                at = lax.rem(offset, 2) * (dp // 2) + offset // 2
                left[pl.ds(at * shard, shard), :] = turned[b * shard : (b + 1) * shard, :]
        proj_ref[...] = dot_tn(low_ref[...], gsl_ref[...])

    count = width // len(outs)
    rights = (gu_ref[0], act_ref[0], mix_ref[0])
    ends = (0, hidden, 2 * hidden, 2 * hidden + mix_ref.shape[2])
    for n, out in enumerate(outs):
        here = slice(n * count, (n + 1) * count)
        for m in range(3):
            part = dot_nn(lefts[m][here, :], rights[m]).astype(BF16)
            out[0, :, :, ends[m] : ends[m + 1]] = part.reshape(
                out.shape[1], out.shape[2], ends[m + 1] - ends[m]
            )


def weight_grads(
    info, dp, shard, x_low, two_low, one_low, upper_low, act, mixed, out_low, student_low
):
    tensor, rows, hidden = upper_low.shape
    width = x_low.shape[1]
    head_width = mixed.shape[2]
    ch = student_low.shape[1]
    total = 2 * hidden + head_width
    if shard % 16:
        parts = [(1, width)]
    else:
        parts = [(dp // 2, shard)] * 2
    return pl.pallas_call(
        functools.partial(weight_grads_kernel, dp, shard),
        grid_spec=pltpu.PrefetchScalarGridSpec(
            num_scalar_prefetch=1,
            grid=(tensor,),
            in_specs=[
                whole(rows, width),
                whole(rows, width),
                whole(rows, width),
                block(rows, hidden),
                block(rows, hidden),
                block(rows, head_width),
                whole(rows, width),
                whole(rows, ch),
            ],
            out_specs=tuple(block(*part, total) for part in parts) + (whole(width, ch),),
            scratch_shapes=[pltpu.VMEM((width, rows), BF16)] * 3,
        ),
        out_shape=tuple(jax.ShapeDtypeStruct((tensor, *part, total), BF16) for part in parts)
        + (jax.ShapeDtypeStruct((width, ch), F32),),
        compiler_params=pltpu.CompilerParams(vmem_limit_bytes=VMEM_LIMIT),
        cost_estimate=LIGHT,
        name="weight_grads",
    )(info, x_low, two_low, one_low, upper_low, act, mixed, out_low, student_low)


def weights_to_owner(parts, dp, tensor, z):
    if len(parts) == 1:
        order = (z - jnp.arange(tensor)) % tensor
        whole_parts = jnp.take(parts[0], order, axis=0)
        owned = lax.psum_scatter(
            whole_parts.reshape(-1, whole_parts.shape[-1]), ("tensor", "dp"),
            scatter_dimension=0, tiled=True,
        ).astype(F32)

        def done(came, late):
            yield (), owned
            return owned

        return (), (), lambda sent: (), done
    keep, give = parts
    bits = bits_of(dp)
    got = swapped(give, "dp", dp, bits[0])
    half = tensor // 2
    orders = (bits[1:], bits[1:][::-1])
    sides = [slice(0, half), slice(half, tensor)]
    sent = []
    for side, order in zip(sides, orders):
        value = split_by(keep[side], bits[1:], order[0], 1).astype(F32)
        value = value + split_by(got[side], bits[1:], order[0], 1).astype(F32)
        sent.append(value.astype(BF16))

    def first(sent):
        return [swapped(sent[k], "dp", dp, orders[k][0]) for k in range(2)]

    def finish(came, late):
        sent = None
        values, lefts = [], [list(bits[1:]), list(bits[1:])]
        for side, order in zip(sides, orders):
            value = split_by(keep[side], bits[1:], order[0], 0).astype(F32)
            values.append(value + split_by(late[side], bits[1:], order[0], 0).astype(F32))
        for n in range(len(bits) - 1):
            if n:
                came = [swapped(sent[k], "dp", dp, orders[k][n]) for k in range(2)]
                came = yield sent, came
            sent = []
            for k in range(2):
                value = values[k] + came[k].astype(F32)
                lefts[k].remove(orders[k][n])
                if n + 2 < len(bits):
                    bit = orders[k][n + 1]
                    sent.append(split_by(value, lefts[k], bit, 1).astype(BF16))
                    value = split_by(value, lefts[k], bit, 0)
                values[k] = value
        own = [value[t, 0] for value in values for t in range(half)]
        total = own[1]
        for t in list(range(2, tensor)) + [0]:
            total = total.astype(BF16)
            came = yield total, shifted(total, "tensor", tensor, 1)
            total = own[t] + came.astype(F32)
        return total

    return sent, got, first, finish


def split_by(value, left, bit, side):
    shape = value.shape
    place = left.index(bit)
    low, high = 1 << place, 1 << (len(left) - 1 - place)
    pairs = value.reshape(shape[0], high, 2, low, *shape[2:])
    return pairs[:, :, side].reshape(shape[0], high * low, *shape[2:])


def first_rows_kernel(d_ref, w_ref, out_ref):
    out_ref[...] = dot_nt(d_ref[0], w_ref[...]).astype(BF16)


def first_rows(d_chunks, w_in):
    _, rows, width = d_chunks.shape
    return pl.pallas_call(
        first_rows_kernel,
        grid=(1,),
        out_shape=jax.ShapeDtypeStruct((rows, w_in.shape[0]), BF16),
        in_specs=[
            pl.BlockSpec((1, rows, width), lambda n: (1, 0, 0)),
            whole(*w_in.shape),
        ],
        out_specs=whole(rows, w_in.shape[0]),
        compiler_params=pltpu.CompilerParams(vmem_limit_bytes=VMEM_LIMIT),
        cost_estimate=LIGHT,
        name="first_rows",
    )(d_chunks, w_in)


def other_rows_kernel(tensor, d_ref, w_ref, *refs):
    seq_refs, (out_ref, grad_ref) = refs[:tensor], refs[tensor:]
    n = pl.program_id(0)
    for t in range(tensor):

        @pl.when(n == t)
        def _():
            part = dot_tn(seq_refs[t][...], d_ref[0])
            if t == 0:
                grad_ref[...] = part
            else:
                grad_ref[...] += part

    out_ref[0] = dot_nt(d_ref[0], w_ref[...]).astype(BF16)


def other_rows(d_chunks, w_in, seq_rows):
    tensor, rows, width = d_chunks.shape
    model = w_in.shape[0]
    return pl.pallas_call(
        functools.partial(other_rows_kernel, tensor),
        grid=(tensor,),
        out_shape=(
            jax.ShapeDtypeStruct((tensor, rows, model), BF16),
            jax.ShapeDtypeStruct((model, width), F32),
        ),
        in_specs=[block(rows, width), whole(*w_in.shape)] + [whole(rows, model)] * tensor,
        out_specs=(block(rows, model), whole(model, width)),
        compiler_params=pltpu.CompilerParams(vmem_limit_bytes=VMEM_LIMIT),
        cost_estimate=LIGHT,
        name="other_rows",
    )(d_chunks, w_in, *seq_rows)


def per_device(
    dp, tensor, tokens, cotangent, labels, piece_start, piece_len, w_qkv, w_out, w_up, w_down,
    vec_table, ff_bias, cls_proj, cls_vec, cls_hidden, cls_out, cls_bias,
):
    rows, width = tokens.shape
    local = w_qkv.shape[2]
    heads = local // HEAD_DIM
    padded = -(-local // LANES) * LANES
    shard = w_qkv.shape[0]
    hidden = w_up.shape[1]
    ch = cls_proj.shape[1]
    z = lax.axis_index("tensor")
    info = jnp.concatenate(
        [z.reshape(1), lax.axis_index("dp").reshape(1), labels, piece_start[0], piece_len[0]]
    ).astype(jnp.int32)

    extra = padded - local
    qkv_shard = jnp.pad(w_qkv, ((0, 0), (0, 0), (0, extra))).reshape(shard, 3 * padded)
    ff_ring, seq_rows = [], []
    ff_shard = jnp.concatenate([w_up, w_down.T, w_out.T], axis=1)
    _, _, w_in = in_turn(
        vec_table[0, 0],
        {
            "rows": ring_chain(tokens, tensor, seq_rows),
            "ff": ring_chain(ff_shard, tensor, ff_ring),
            "in": gather_chain(qkv_shard, "dp", dp),
        },
        [("in",), ("in", "ff"), ("in",), ("ff",), ("rows",), ("ff",), ("rows",), ("rows",)],
    )
    half = tensor // 2
    pieces = [
        lax.all_gather(jnp.stack(ff_ring[n : n + half]), "dp") for n in (0, half)
    ]
    if shard % 16:
        pieces = [
            p.transpose(1, 0, 2, 3).reshape(1, half, dp * shard, p.shape[-1]) for p in pieces
        ]

    q_bias = lax.dynamic_slice_in_dim(vec_table[0], z * local, local, 0)
    v_bias = lax.dynamic_slice_in_dim(vec_table[1], z * local, local, 0)
    in_bias = jnp.pad(
        jnp.stack([q_bias, jnp.zeros_like(q_bias), v_bias]), ((0, 0), (0, extra))
    ).reshape(1, 3 * padded)

    def exchanged(parts):
        return [parts[0]] + [
            shifted(parts[tensor - s], "tensor", tensor, s) for s in range(1, tensor)
        ]

    chunks = [
        (jnp.dot(part, w_in, preferred_element_type=F32) + in_bias).astype(BF16)
        for part in seq_rows
    ]
    mixed, lse = attend_forward(info, chunks, heads)
    kept = rows_forward(
        info, pieces, exchanged(mixed), tokens, vec_table,
        ff_bias.reshape(tensor, 1, hidden), cls_proj, cls_vec,
    )
    out_low, x_low, act, _, _, _, _, _, mixed_all, _, stats = kept
    all_stats = exchanged([stats] * tensor)
    (
        logits, two_low, upper_low, one_low, grad_h_one, grad_mixed, student_low, pack,
    ) = rows_backward(
        info, pieces, all_stats, kept, cotangent, vec_table, cls_proj, cls_vec,
        cls_hidden, jnp.pad(cls_out, ((0, 0), (0, ch - CLASSES))),
        jnp.pad(cls_bias, (0, ch - CLASSES)).reshape(1, ch),
    )
    grad_rows = exchanged(grad_mixed)
    *ff_parts, grad_proj = weight_grads(
        info, dp, shard, x_low, two_low, one_low, upper_low, act, mixed_all, out_low, student_low
    )
    small = jnp.concatenate([grad_proj, pack], axis=0).astype(BF16)
    bits = bits_of(tensor)
    small_came = swapped(small, "tensor", tensor, bits[0])
    sent, got, first, finish = weights_to_owner(ff_parts, dp, tensor, z)
    sent, grad_rows, small_came = lax.optimization_barrier((sent, grad_rows, small_came))
    small = small + small_came
    small, grad_rows = lax.optimization_barrier((small, grad_rows))
    small_came = swapped(small, "tensor", tensor, bits[1])

    d_chunks, bias_sums = attend_backward(info, chunks, grad_rows, mixed, lse, heads)
    d_chunks, bias_sums, came, late, small_came = lax.optimization_barrier(
        (d_chunks, bias_sums, first(sent), got, small_came)
    )
    first_part = first_rows(d_chunks, w_in)
    came, late = after((came, late), first_part)

    def small_chain():
        total = small + small_came
        for bit in bits[2:]:
            got = yield total, swapped(total, "tensor", tensor, bit)
            total = total + got
        for bit in bits_of(dp):
            got = yield total, swapped(total, "dp", dp, bit)
            total = total + got
        return total.astype(F32)

    shared = {}

    def rows_chain():
        total = first_part
        for t in range(2, tensor):
            came = yield total, shifted(total, "tensor", tensor, 1)
            total = (shared["parts"][t].astype(F32) + came.astype(F32)).astype(BF16)
        came = yield total, shifted(total, "tensor", tensor, 1)
        return grad_h_one + shared["parts"][0].astype(F32) + came.astype(F32)

    def in_chain():
        later = yield (), d_chunks
        shared["parts"], grad = other_rows(later, w_in, seq_rows)
        grad = yield (), grad
        rider = jnp.pad(bias_sums, ((0, 8), (0, 2 * padded)))
        return (
            yield from owner_chain(
                grad.reshape(dp, shard, 3 * padded), rider, "dp", dp, "tensor", tensor
            )
        )

    grad_tokens, ff_own, (grad_in, riders), sums = in_turn(
        bias_sums[0, 0],
        {
            "rows": rows_chain(),
            "ff": finish(came, late),
            "in": in_chain(),
            "small": small_chain(),
        },
        [
            ("in",), ("rows",), ("in",), ("small",), ("ff",), ("in",), ("small",), ("rows",),
            ("ff",), ("in",), ("small",), ("ff",), ("in",), ("small",), ("ff",), ("in",), ("rows",),
        ],
    )
    grad_w_qkv = grad_in.reshape(shard, 3, padded)[:, :, :local]
    bias_sum = riders[:, :2, :local].transpose(1, 0, 2).reshape(2, width)

    proj_sum, pack_sum = sums[:width], sums[width:]
    hid_sum = pack_sum[8 : 8 + ch]
    out_w_sum = pack_sum[8 + ch : 8 + 2 * ch, :CLASSES]
    at = 8 + 2 * ch
    vec_sum = pack_sum[at : at + 6 * width // ch].reshape(6, width)
    ff_bias_sum = pack_sum[at + 6 * width // ch :].reshape(-1)
    return (
        out_low,
        logits[0:1, :CLASSES],
        grad_tokens,
        grad_w_qkv,
        ff_own[:, 2 * hidden :].T,
        ff_own[:, :hidden],
        ff_own[:, hidden : 2 * hidden].T,
        jnp.concatenate([bias_sum, vec_sum], axis=0),
        ff_bias_sum,
        proj_sum,
        pack_sum[:3],
        hid_sum,
        out_w_sum,
        pack_sum[3, :CLASSES],
    )


def solution(mesh):
    dp, tensor = mesh.shape["dp"], mesh.shape["tensor"]
    rows = P(("dp", "tensor"), None)
    cut = P("dp", "tensor")
    turned_cut = P("tensor", "dp")
    return jax.shard_map(
        functools.partial(per_device, dp, tensor),
        mesh=mesh,
        in_specs=(
            rows, rows, P("dp"), P("dp", None), P("dp", None), P("dp", None, "tensor"),
            turned_cut, cut, turned_cut, P(), P(), P(), P(), P(), P(), P(),
        ),
        out_specs=(
            rows, P("dp", None), rows, P("dp", None, "tensor"), turned_cut, cut, turned_cut,
            P(), P(), P(), P(), P(), P(), P(),
        ),
        check_vma=False,
    )
```

```python
import functools

import jax
import jax.numpy as jnp
from jax import lax
from jax.experimental import pallas as pl
from jax.experimental.pallas import tpu as pltpu
from jax.sharding import PartitionSpec as P

HEAD_DIM = 64
CLASSES = 14
PIECE_BLOCK = 256
POOL_HEADS = 2
LANES = 128
NORM_EPS = 1e-05
MASK_FILL = -1e30
PRECISE = lax.Precision.HIGHEST
F32 = jnp.float32
BF16 = jnp.bfloat16
MIB = 1024 * 1024
LIGHT = pl.CostEstimate(flops=1024, bytes_accessed=1024, transcendentals=0)
HEAVY = pl.CostEstimate(flops=4 * 10**10, bytes_accessed=1024, transcendentals=0)


def dot_nn(a, b, precision=None):
    return lax.dot_general(
        a, b, (((1,), (0,)), ((), ())), preferred_element_type=F32, precision=precision
    )


def dot_nt(a, b, precision=None):
    return lax.dot_general(
        a, b, (((1,), (1,)), ((), ())), preferred_element_type=F32, precision=precision
    )


def dot_tn(a, b, precision=None):
    return lax.dot_general(
        a, b, (((0,), (0,)), ((), ())), preferred_element_type=F32, precision=precision
    )


def bits_of(size):
    return [1 << n for n in range(size.bit_length() - 1)]


def swapped(value, axis, size, bit):
    return lax.ppermute(value, axis, [(i, i ^ bit) for i in range(size)])


def shifted(value, axis, size, by):
    return lax.ppermute(value, axis, [(i, (i + by) % size) for i in range(size)])


def after(value, *others):
    return lax.optimization_barrier((value, others))[0]


def in_turn(mark, chains, turns):
    under_way, results = {}, {}

    def advance(name, value):
        try:
            under_way[name] = chains[name].send(value)
        except StopIteration as end:
            under_way.pop(name, None)
            results[name] = end.value

    for name in chains:
        advance(name, None)
    turns = list(turns)
    while under_way:
        turn = turns.pop(0) if turns else tuple(under_way)
        names = [name for name in turn if name in under_way]
        if not names:
            continue
        sent = [value for value, _ in under_way.values()]
        there, mark, _ = lax.optimization_barrier(
            ([under_way[name][1] for name in names], mark, sent)
        )
        for name, value in zip(names, there):
            advance(name, value)
    return [results[name] for name in chains]


def ring_chain(value, size, kept):
    kept.append(value)
    for _ in range(size - 1):
        value = yield value, shifted(value, "tensor", size, 1)
        kept.append(value)
    return kept


def gather_chain(value, axis, size):
    index = lax.axis_index(axis)
    for bit in bits_of(size):
        other = yield value, swapped(value, axis, size, bit)
        low = (index // bit) % 2 == 0
        value = jnp.where(
            low, jnp.concatenate([value, other], 0), jnp.concatenate([other, value], 0)
        )
    return value


def owner_chain(parts, rider, axis, size, other, other_size):
    index = lax.axis_index(axis)
    riding = rider.shape[0]
    for bit in bits_of(size):
        mine = (index // bit) % 2
        count, rows, columns = parts.shape
        pairs = parts.reshape(count // 2, 2, rows, columns)
        keep = lax.dynamic_index_in_dim(pairs, mine, 1, keepdims=False)
        give = lax.dynamic_index_in_dim(pairs, 1 - mine, 1, keepdims=False)
        give = give.reshape(count // 2 * rows, columns)
        give = jnp.concatenate([give, rider]).astype(BF16)
        got = yield give, swapped(give, axis, size, bit)
        parts = keep + got[:-riding].reshape(keep.shape).astype(F32)
        rider = rider.astype(BF16).astype(F32) + got[-riding:].astype(F32)
    got = yield rider, [shifted(rider, other, other_size, by) for by in range(1, other_size)]
    place = lax.axis_index(other)
    riders = jnp.zeros((other_size, *rider.shape), F32)
    for by, value in enumerate([rider] + list(got)):
        riders = lax.dynamic_update_index_in_dim(riders, value, (place - by) % other_size, 0)
    return parts[0], riders


def far_off(*values):
    return [pltpu.with_memory_space_constraint(v, pltpu.HBM) for v in values]


INFO_Z, INFO_D, INFO_LABEL, INFO_PIECES = 0, 1, 2, 3


def part_of(info_ref, place, tensor):
    return lax.rem(info_ref[INFO_Z] - place + tensor, tensor)


def block_range(info_ref, block):
    first, stop, inside_any = block, block + 1, jnp.int32(0)
    pieces = (info_ref.shape[0] - INFO_PIECES) // 2
    for piece in range(pieces):
        begin, count = info_ref[INFO_PIECES + piece], info_ref[INFO_PIECES + pieces + piece]
        inside = jnp.logical_and(block >= begin, block < begin + count)
        first = jnp.where(inside, begin, first)
        stop = jnp.where(inside, begin + count, stop)
        inside_any = jnp.where(inside, jnp.int32(1), inside_any)
    return first, stop, inside_any


def head_lanes(shape, head):
    lane = lax.broadcasted_iota(jnp.int32, shape, len(shape) - 1)
    return (lane >= head * HEAD_DIM) & (lane < (head + 1) * HEAD_DIM)


def attend_forward_kernel(heads, info_ref, *refs):
    tensor = len(refs) - 2 - 3
    chunks = refs[:tensor]
    o_ref, lse_ref = refs[tensor : tensor + 2]
    q_s, k_s, vt_s = refs[tensor + 2 :]
    rows, padded = chunks[0].shape[0], chunks[0].shape[1] // 3
    blk = PIECE_BLOCK
    blocks = tensor * rows // blk
    per_chunk = rows // blk
    scale = HEAD_DIM ** (-0.5)
    for t in range(tensor):
        quarter = part_of(info_ref, t, tensor)

        def one_block(part, carry):
            b = quarter * per_chunk + part
            here = pl.ds(part * blk, blk)
            q = chunks[t][here, 0:padded]
            for h in range(heads):
                q_s[h, b] = jnp.where(head_lanes(q.shape, h), q * scale, 0.0).astype(BF16)
            pair, at = b // 2, pl.multiple_of(lax.rem(b, 2) * blk, blk)
            k_s[pair, pl.ds(at, blk), :] = chunks[t][here, padded : 2 * padded]
            vt_s[pair, :, pl.ds(at, blk)] = chunks[t][here, 2 * padded : 3 * padded].T
            return carry

        lax.fori_loop(0, per_chunk, one_block, 0)


    def one_query(i, carry):
        _, stop, inside = block_range(info_ref, i)
        q_h = [q_s[h, i] for h in range(heads)]
        query = i * blk + lax.broadcasted_iota(jnp.int32, (1, blk), 1)
        limit = jnp.maximum(query, jnp.where(inside > 0, stop * blk - 1, 0))

        def step(j, state, masked):
            tops, totals, mixed = state
            keys = 2 * blk
            if masked:
                key = j * keys + lax.broadcasted_iota(jnp.int32, (keys, blk), 0)
                seen = key <= limit
            k_j = k_s[j]
            scores = [dot_nt(k_j, q_h[h]) for h in range(heads)]
            if masked:
                scores = [jnp.where(seen, s, MASK_FILL) for s in scores]
            new_tops = [
                jnp.maximum(tops[h], jnp.max(scores[h], axis=0, keepdims=True))
                for h in range(heads)
            ]
            ps = [jnp.exp(scores[h] - new_tops[h]) for h in range(heads)]
            fades = [jnp.exp(tops[h] - new_tops[h]) for h in range(heads)]
            new_totals = [
                totals[h] * fades[h] + jnp.sum(ps[h], axis=0, keepdims=True) for h in range(heads)
            ]
            new_mixed = [
                mixed[h] * fades[h]
                + dot_nn(vt_s[j, h * HEAD_DIM : (h + 1) * HEAD_DIM, :], ps[h].astype(BF16))
                for h in range(heads)
            ]
            return tuple(new_tops), tuple(new_totals), tuple(new_mixed)

        state = (
            tuple(jnp.full((1, blk), MASK_FILL, F32) for _ in range(heads)),
            tuple(jnp.zeros((1, blk), F32) for _ in range(heads)),
            tuple(jnp.zeros((HEAD_DIM, blk), F32) for _ in range(heads)),
        )
        last = i // 2
        state = lax.fori_loop(0, last, lambda j, c: step(j, c, False), state)
        state = step(last, state, True)
        tops, totals, mixed = lax.fori_loop(
            last + 1, (stop + 1) // 2, lambda j, c: step(j, c, True), state
        )
        outs = [mixed[h] * (1.0 / totals[h]) for h in range(heads)]
        lses = [tops[h] + jnp.log(totals[h]) for h in range(heads)]
        t = part_of(info_ref, i // per_chunk, tensor)
        here = pl.ds(lax.rem(i, per_chunk) * blk, blk)
        o_ref[t, here, :] = jnp.concatenate(outs, axis=0).T.astype(BF16)
        lse_ref[i] = jnp.concatenate(lses + [jnp.zeros((8 - heads, blk), F32)], axis=0)
        return carry

    lax.fori_loop(0, blocks, one_query, 0)


def attend_forward(info, chunks, heads):
    tensor = len(chunks)
    rows, width = chunks[0].shape
    padded = width // 3
    seq, blk = tensor * rows, PIECE_BLOCK
    blocks = seq // blk
    smem = pl.BlockSpec(memory_space=pltpu.SMEM)
    vmem = pl.BlockSpec(memory_space=pltpu.VMEM)
    return pl.pallas_call(
        functools.partial(attend_forward_kernel, heads),
        out_shape=(
            jax.ShapeDtypeStruct((tensor, rows, heads * HEAD_DIM), BF16),
            jax.ShapeDtypeStruct((blocks, 8, blk), F32),
        ),
        in_specs=[smem] + [vmem] * tensor,
        out_specs=(vmem, vmem),
        scratch_shapes=[
            pltpu.VMEM((heads, blocks, blk, padded), BF16),
            pltpu.VMEM((blocks // 2, 2 * blk, padded), BF16),
            pltpu.VMEM((blocks // 2, padded, 2 * blk), BF16),
        ],
        compiler_params=pltpu.CompilerParams(vmem_limit_bytes=24 * MIB),
        cost_estimate=LIGHT,
        name="attend_forward",
    )(info, *chunks)


def attend_backward_kernel(heads, info_ref, *refs):
    tensor = (len(refs) - 2 - 2 - 9) // 2
    chunks, grads = refs[:tensor], refs[tensor : 2 * tensor]
    o_ref, lse_ref, dqkv_ref, bias_ref = refs[2 * tensor : 2 * tensor + 4]
    q_s, k_s, kt_s, v_s, g_s, delta_s, dqt_s, dk_s, dv_s = refs[2 * tensor + 4 :]
    rows, padded = chunks[0].shape[0], chunks[0].shape[1] // 3
    width = heads * HEAD_DIM
    blk = PIECE_BLOCK
    blocks = tensor * rows // blk
    per_chunk = rows // blk
    scale = HEAD_DIM ** (-0.5)
    for t in range(tensor):
        quarter = part_of(info_ref, t, tensor)

        def one_block(part, carry):
            b = quarter * per_chunk + part
            here = pl.ds(part * blk, blk)
            q = chunks[t][here, 0:padded]
            g = grads[t][here, :]
            for h in range(heads):
                q_s[h, b] = jnp.where(head_lanes(q.shape, h), q * scale, 0.0).astype(BF16)
                g_s[h, b, :, 0:width] = jnp.where(head_lanes(g.shape, h), g, 0.0).astype(BF16)
                if padded > width:
                    g_s[h, b, :, width:padded] = jnp.zeros((blk, padded - width), BF16)
            k = chunks[t][here, padded : 2 * padded]
            pair, at = b // 2, pl.multiple_of(lax.rem(b, 2) * blk, blk)
            k_s[pair, pl.ds(at, blk), :] = k
            v_s[pair, pl.ds(at, blk), :] = chunks[t][here, 2 * padded : 3 * padded]
            kt_s[pair, :, pl.ds(at, blk)] = k.T
            prod = (g.astype(F32) * o_ref[t, here, :].astype(F32)).T
            sums = [
                jnp.sum(prod[h * HEAD_DIM : (h + 1) * HEAD_DIM, :], axis=0, keepdims=True)
                for h in range(heads)
            ]
            delta_s[b] = jnp.concatenate(sums + [jnp.zeros((8 - heads, blk), F32)], axis=0)
            dqt_s[b] = jnp.zeros((padded, blk), F32)
            return carry

        lax.fori_loop(0, per_chunk, one_block, 0)
    bias_ref[...] = jnp.zeros_like(bias_ref)

    keys = 2 * blk

    def one_pair(j, carry):
        first, _, _ = block_range(info_ref, 2 * j)
        also, _, _ = block_range(info_ref, 2 * j + 1)
        dk_s[...] = jnp.zeros_like(dk_s)
        dv_s[...] = jnp.zeros_like(dv_s)

        def step(i, masked):
            lse, delta = lse_ref[i], delta_s[i]
            if masked:
                _, stop, inside = block_range(info_ref, i)
                query = i * blk + lax.broadcasted_iota(jnp.int32, (1, blk), 1)
                limit = jnp.maximum(query, jnp.where(inside > 0, stop * blk - 1, 0))
                key = j * keys + lax.broadcasted_iota(jnp.int32, (keys, blk), 0)
                seen = key <= limit
            k_j, v_j = k_s[j], v_s[j]
            q_h = [q_s[h, i] for h in range(heads)]
            g_h = [g_s[h, i] for h in range(heads)]
            lows, ds = [], []
            for h in range(heads):
                p = jnp.exp(dot_nt(k_j, q_h[h]) - lse[h : h + 1, :])
                dp = dot_nt(v_j, g_h[h])
                if masked:
                    p = jnp.where(seen, p, 0.0)
                lows.append(p.astype(BF16))
                ds.append((p * (dp - delta[h : h + 1, :])).astype(BF16))
            dv_s[...] += dot_nn(jnp.concatenate(lows, axis=1), jnp.concatenate(g_h, axis=0))
            dk_s[...] += dot_nn(jnp.concatenate(ds, axis=1), jnp.concatenate(q_h, axis=0))
            for h in range(heads):
                lo, hi = h * HEAD_DIM, (h + 1) * HEAD_DIM
                dqt_s[i, lo:hi, :] += dot_nn(kt_s[j, lo:hi, :], ds[h])

        def masked_step(i, c):
            step(i, True)
            return c

        def open_step(i, c):
            step(i, False)
            return c

        lax.fori_loop(jnp.minimum(first, also), 2 * j + 2, masked_step, 0)
        lax.fori_loop(2 * j + 2, blocks, open_step, 0)
        for part in range(2):
            b = 2 * j + part
            t = part_of(info_ref, b // per_chunk, tensor)
            here = pl.ds(lax.rem(b, per_chunk) * blk, blk)
            side = slice(part * blk, (part + 1) * blk)
            dqkv_ref[t, here, padded : 2 * padded] = dk_s[side, :].astype(BF16)
            dqkv_ref[t, here, 2 * padded : 3 * padded] = dv_s[side, :].astype(BF16)
        bias_ref[1:2, :] = bias_ref[1:2, :] + jnp.sum(dv_s[...], axis=0, keepdims=True)
        return carry

    lax.fori_loop(0, blocks // 2, one_pair, 0)

    def one_query(i, carry):
        dq = dqt_s[i].T * scale
        t = part_of(info_ref, i // per_chunk, tensor)
        here = pl.ds(lax.rem(i, per_chunk) * blk, blk)
        dqkv_ref[t, here, 0:padded] = dq.astype(BF16)
        bias_ref[0:1, :] = bias_ref[0:1, :] + jnp.sum(dq, axis=0, keepdims=True)
        return carry

    lax.fori_loop(0, blocks, one_query, 0)


def attend_backward(info, chunks, grads, mixed, lse, heads):
    tensor = len(chunks)
    rows, width = chunks[0].shape
    padded = width // 3
    seq, blk = tensor * rows, PIECE_BLOCK
    blocks = seq // blk
    smem = pl.BlockSpec(memory_space=pltpu.SMEM)
    vmem = pl.BlockSpec(memory_space=pltpu.VMEM)
    return pl.pallas_call(
        functools.partial(attend_backward_kernel, heads),
        out_shape=(
            jax.ShapeDtypeStruct((tensor, rows, width), BF16),
            jax.ShapeDtypeStruct((8, padded), F32),
        ),
        in_specs=[smem] + [vmem] * (2 * tensor + 2),
        out_specs=(vmem, vmem),
        scratch_shapes=[
            pltpu.VMEM((heads, blocks, blk, padded), BF16),
            pltpu.VMEM((blocks // 2, 2 * blk, padded), BF16),
            pltpu.VMEM((blocks // 2, padded, 2 * blk), BF16),
            pltpu.VMEM((blocks // 2, 2 * blk, padded), BF16),
            pltpu.VMEM((heads, blocks, blk, padded), BF16),
            pltpu.VMEM((blocks, 8, blk), F32),
            pltpu.VMEM((blocks, padded, blk), F32),
            pltpu.VMEM((2 * blk, padded), F32),
            pltpu.VMEM((2 * blk, padded), F32),
        ],
        compiler_params=pltpu.CompilerParams(vmem_limit_bytes=34 * MIB),
        cost_estimate=LIGHT,
        name="attend_backward",
    )(info, *far_off(*chunks, *grads, mixed, lse))


def start_weights(pieces, w_s, wo_s, sems, o_sem):
    wide = w_s.shape[2]
    copies = []
    t = 0
    for piece in pieces:
        blocks, parts, rows, _ = piece.shape
        for part in range(parts):
            for n in range(blocks):
                copies.append((piece.at[n, part], t, pl.ds(n * rows, rows)))
            t += 1
    for source, t, here in copies:
        pltpu.make_async_copy(source.at[:, wide:], wo_s.at[t, here, :], o_sem).start()
    for source, t, here in copies:
        pltpu.make_async_copy(source.at[:, :wide], w_s.at[t, here, :], sems.at[t]).start()


def center(values):
    mean = jnp.mean(values, axis=-1, keepdims=True)
    centered = values - mean
    spread = jnp.mean(centered * centered, axis=-1, keepdims=True)
    return centered, lax.rsqrt(spread + NORM_EPS)


def same_head(value):
    row = lax.broadcasted_iota(jnp.int32, (value, value), 0) // (value // POOL_HEADS)
    col = lax.broadcasted_iota(jnp.int32, (value, value), 1) // (value // POOL_HEADS)
    return (row == col).astype(F32)


def rows_forward_kernel(tensor, arrays, info_ref, *refs):
    mixed = refs[:tensor]
    tok_ref, vec_ref, bias_ref, proj_ref, cvec_ref = refs[tensor : tensor + 5]
    pieces = refs[tensor + 5 : tensor + 5 + arrays]
    (
        low_ref, xlow_ref, act_ref, slope_ref, xh1_ref, xh2_ref, rs_ref, stud_ref, e_ref,
        stats_ref, acc_s, w_s, wo_s, sems, o_sem,
    ) = refs[tensor + 5 + arrays :]
    j = pl.program_id(0)
    hidden = act_ref.shape[2]

    @pl.when(j == 0)
    def _():
        start_weights(pieces, w_s, wo_s, sems, o_sem)
        total = tok_ref[...].astype(F32) + vec_ref[2:3, :]
        pltpu.make_async_copy(wo_s, wo_s, o_sem).wait()
        for s in range(tensor):
            piece = mixed[s][...]
            total = total + dot_nt(piece, wo_s[s])
        centered, rstd = center(total)
        xhat = centered * rstd
        xh1_ref[...] = xhat
        rs_ref[:, 0:1] = rstd
        x_one = xhat * vec_ref[3:4, :] + vec_ref[4:5, :]
        xlow_ref[...] = x_one.astype(BF16)
        acc_s[...] = x_one + vec_ref[5:6, :]

    pltpu.make_async_copy(w_s.at[j], w_s.at[j], sems.at[j]).wait()
    half = min(256, xlow_ref.shape[0])

    def rows_part(n, carry):
        here = pl.ds(n * half, half)
        upper = dot_nn(xlow_ref[here, :], w_s[j, :, 0:hidden]) + bias_ref[0]
        phi = 0.5 * (1.0 + lax.erf(upper * (0.5**0.5)))
        act = (upper * phi).astype(BF16)
        slope = phi + upper * (jnp.exp(-0.5 * upper * upper) * 0.3989422804014327)
        act_ref[0, here, :] = act
        slope_ref[0, here, :] = slope.astype(BF16)
        acc_s[here, :] = acc_s[here, :] + dot_nt(act, w_s[j, :, hidden:])
        return carry

    lax.fori_loop(0, xlow_ref.shape[0] // half, rows_part, 0)

    @pl.when(j == pl.num_programs(0) - 1)
    def _():
        centered, rstd = center(acc_s[...])
        xhat = centered * rstd
        xh2_ref[...] = xhat
        rs_ref[:, 1:2] = rstd
        low = (xhat * vec_ref[6:7, :] + vec_ref[7:8, :]).astype(BF16)
        low_ref[...] = low
        student = dot_nn(low, proj_ref[...]) + cvec_ref[0:1, :]
        stud_ref[...] = student
        width = student.shape[1]
        scale = (width // POOL_HEADS) ** (-0.5)
        e = dot_nn(student * (cvec_ref[1:2, :] * scale), same_head(width), PRECISE)
        e_ref[...] = e
        top = jnp.max(e, axis=0, keepdims=True)
        w = jnp.exp(e - top)
        stats_ref[...] = jnp.concatenate(
            [
                top,
                jnp.sum(w, axis=0, keepdims=True),
                jnp.sum(w * student, axis=0, keepdims=True),
                jnp.zeros((5, width), F32),
            ],
            axis=0,
        )


def whole(*shape):
    return pl.BlockSpec(shape, lambda j, *_: (0,) * len(shape))


def block(*shape):
    return pl.BlockSpec((1,) + shape, lambda j, *_: (j,) + (0,) * len(shape))


def rows_forward(info, pieces, mixed, tokens, vec_table, ff_bias, cls_proj, cls_vec):
    tensor = len(mixed)
    rows, width = tokens.shape
    head_width = mixed[0].shape[1]
    hidden = ff_bias.shape[2]
    ch = cls_proj.shape[1]
    far = pl.BlockSpec(memory_space=pl.ANY)

    def of_block(j, info_ref):
        return (part_of(info_ref, j, tensor), 0, 0)

    return pl.pallas_call(
        functools.partial(rows_forward_kernel, tensor, len(pieces)),
        grid_spec=pltpu.PrefetchScalarGridSpec(
            num_scalar_prefetch=1,
            grid=(tensor,),
            in_specs=[whole(rows, head_width)] * tensor
            + [
                whole(rows, width),
                whole(8, width),
                pl.BlockSpec((1, 1, hidden), of_block),
                whole(width, ch),
                whole(3, ch),
            ]
            + [far] * len(pieces),
            out_specs=(
                whole(rows, width),
                whole(rows, width),
                block(rows, hidden),
                block(rows, hidden),
                whole(rows, width),
                whole(rows, width),
                whole(rows, 2),
                whole(rows, ch),
                whole(rows, ch),
                whole(8, ch),
            ),
            scratch_shapes=[
                pltpu.VMEM((rows, width), F32),
                pltpu.VMEM((tensor, width, 2 * hidden), BF16),
                pltpu.VMEM((tensor, width, head_width), BF16),
                pltpu.SemaphoreType.DMA((tensor,)),
                pltpu.SemaphoreType.DMA,
            ],
        ),
        out_shape=(
            pltpu.HBM((rows, width), BF16),
            pltpu.HBM((rows, width), BF16),
            pltpu.HBM((tensor, rows, hidden), BF16),
            pltpu.HBM((tensor, rows, hidden), BF16),
            pltpu.HBM((rows, width), F32),
            pltpu.HBM((rows, width), F32),
            pltpu.HBM((rows, 2), F32),
            pltpu.HBM((rows, ch), F32),
            pltpu.HBM((rows, ch), F32),
            jax.ShapeDtypeStruct((8, ch), F32),
        ),
        compiler_params=pltpu.CompilerParams(vmem_limit_bytes=34 * MIB),
        cost_estimate=LIGHT,
        name="rows_forward",
    )(info, *far_off(*mixed, tokens), vec_table, ff_bias, cls_proj, cls_vec,
      *far_off(*pieces))


def norm_back(grad, xhat, rstd, gain):
    g = grad * gain
    return (
        g - jnp.mean(g, axis=-1, keepdims=True) - xhat * jnp.mean(g * xhat, axis=-1, keepdims=True)
    ) * rstd


def rows_backward_kernel(tensor, arrays, info_ref, *refs):
    stats_refs = refs[:tensor]
    (
        stud_ref, e_ref, cot_ref, xh1_ref, xh2_ref, rs_ref, slope_ref, vec_ref, proj_ref,
        cvec_ref, chid_ref, cout_ref, cbias_ref, outlow_ref,
    ) = refs[tensor : tensor + 14]
    pieces = refs[tensor + 14 : tensor + 14 + arrays]
    (
        logit_ref, two_ref, gu_ref, one_ref, gh1_ref, gm_ref, small_ref, acc_s, pack_ref, w_s,
        wo_s, sems, o_sem,
    ) = refs[tensor + 14 + arrays :]
    j = pl.program_id(0)
    ch = stud_ref.shape[1]
    hidden = gu_ref.shape[2]
    scale = (ch // POOL_HEADS) ** (-0.5)
    width = cot_ref.shape[1]
    sums_at = 8 + 2 * ch
    bias_at = sums_at + 6 * (width // ch)

    def pack_row(row, value):
        at = sums_at + (row - 2) * (width // ch)
        for n in range(width // ch):
            pack_ref[at + n : at + n + 1, :] = value[:, n * ch : (n + 1) * ch]

    @pl.when(j == 0)
    def _():
        start_weights(pieces, w_s, wo_s, sems, o_sem)
        head_of = same_head(ch)
        first = (info_ref[INFO_Z] == 0).astype(F32)
        stats = [r[...] for r in stats_refs]
        top = functools.reduce(jnp.maximum, [v[0:1, :] for v in stats])
        weights = [jnp.exp(v[0:1, :] - top) for v in stats]
        total = sum(v[1:2, :] * w for v, w in zip(stats, weights))
        pooled = sum(v[2:3, :] * w for v, w in zip(stats, weights)) / total

        first_row = lax.broadcasted_iota(jnp.int32, (8, ch), 0) == 0
        lane = lax.broadcasted_iota(jnp.int32, (8, ch), 1)
        pooled8 = jnp.broadcast_to(pooled, (8, ch))
        chid = chid_ref[...].astype(F32)
        cout = cout_ref[...].astype(F32)
        hid = jnp.tanh(dot_nn(pooled8, chid, PRECISE) + cvec_ref[2:3, :])
        logits = dot_nn(hid, cout, PRECISE) + cbias_ref[...]
        logit_ref[...] = logits
        real = lane < CLASSES
        masked = jnp.where(real, logits, MASK_FILL)
        powers = jnp.where(real, jnp.exp(masked - jnp.max(masked, axis=1, keepdims=True)), 0.0)
        probs = powers / jnp.sum(powers, axis=1, keepdims=True)
        grad_logits = probs - (lane == info_ref[INFO_LABEL]).astype(F32)
        grad_pre = (1.0 - hid * hid) * dot_nt(grad_logits, cout, PRECISE)
        grad_pooled = dot_nt(grad_pre, chid, PRECISE)
        gl_row = jnp.where(first_row, grad_logits, 0.0) * first
        gp_row = jnp.where(first_row, grad_pre, 0.0) * first
        pack_ref[8 : 8 + ch, :] = dot_tn(pooled8, gp_row, PRECISE)
        pack_ref[8 + ch : 8 + 2 * ch, :] = dot_tn(hid, gl_row, PRECISE)
        base = dot_nn(grad_pooled * pooled8, head_of, PRECISE)[0:1, :]
        gp = grad_pooled[0:1, :]
        query = cvec_ref[1:2, :] * scale
        student = stud_ref[...]
        w = jnp.exp(e_ref[...] - top) / total
        grad_w = dot_nn(student * gp, head_of, PRECISE)
        grad_e = w * (grad_w - base)
        grad_student = w * gp + grad_e * query
        gsl = grad_student.astype(BF16)
        small_ref[0:width, :] = dot_tn(outlow_ref[...], gsl).astype(BF16)
        pack_ref[0:8, :] = jnp.concatenate(
            [
                jnp.sum(grad_student, axis=0, keepdims=True),
                jnp.sum(grad_e * student, axis=0, keepdims=True) * scale,
                gp_row[0:1, :],
                gl_row[0:1, :],
                jnp.zeros((4, ch), F32),
            ],
            axis=0,
        )
        grad = cot_ref[...].astype(F32) + dot_nt(gsl, proj_ref[...])
        xhat = xh2_ref[...]
        pack_row(6, jnp.sum(grad * xhat, axis=0, keepdims=True))
        pack_row(7, jnp.sum(grad, axis=0, keepdims=True))
        two = norm_back(grad, xhat, rs_ref[:, 1:2], vec_ref[6:7, :])
        pack_row(5, jnp.sum(two, axis=0, keepdims=True))
        acc_s[...] = two
        two_ref[...] = two.astype(BF16)

    pltpu.make_async_copy(w_s.at[j], w_s.at[j], sems.at[j]).wait()
    heads_row = part_of(info_ref, j, tensor)
    half = min(256, two_ref.shape[0])

    def rows_part(n, bias_row):
        here = pl.ds(n * half, half)
        upper = dot_nn(two_ref[here, :], w_s[j, :, hidden:]) * slope_ref[0, here, :].astype(F32)
        low = upper.astype(BF16)
        gu_ref[0, here, :] = low
        acc_s[here, :] = acc_s[here, :] + dot_nt(low, w_s[j, :, 0:hidden])
        return bias_row + jnp.sum(upper, axis=0, keepdims=True)

    bias_row = lax.fori_loop(
        0, two_ref.shape[0] // half, rows_part, jnp.zeros((1, hidden), F32)
    )
    for n in range(hidden // ch):
        pack_ref[pl.ds(bias_at + heads_row * (hidden // ch) + n, 1), :] = bias_row[
            :, n * ch : (n + 1) * ch
        ]

    @pl.when(j == pl.num_programs(0) - 1)
    def _():
        grad = acc_s[...]
        xhat = xh1_ref[...]
        pack_row(3, jnp.sum(grad * xhat, axis=0, keepdims=True))
        pack_row(4, jnp.sum(grad, axis=0, keepdims=True))
        one = norm_back(grad, xhat, rs_ref[:, 0:1], vec_ref[3:4, :])
        pack_row(2, jnp.sum(one, axis=0, keepdims=True))
        gh1_ref[...] = one
        low = one.astype(BF16)
        one_ref[...] = low
        pltpu.make_async_copy(wo_s, wo_s, o_sem).wait()
        for s in range(tensor):
            gm_ref[s] = dot_nn(low, wo_s[s]).astype(BF16)
        small_ref[width:, :] = pack_ref[...].astype(BF16)


def rows_backward(
    info, pieces, stats, kept, cotangent, vec_table, cls_proj, cls_vec, cls_hidden,
    cls_out, cls_bias,
):
    out_low, _, _, slope, xh1, xh2, rs, student, pool_logit, _ = kept
    tensor, rows, hidden = slope.shape
    width = xh1.shape[1]
    head_width = pieces[0].shape[3] - 2 * hidden
    ch = student.shape[1]
    far = pl.BlockSpec(memory_space=pl.ANY)
    pack_rows = 8 + 2 * ch + (6 * width + tensor * hidden) // ch

    return pl.pallas_call(
        functools.partial(rows_backward_kernel, tensor, len(pieces)),
        grid_spec=pltpu.PrefetchScalarGridSpec(
            num_scalar_prefetch=1,
            grid=(tensor,),
            in_specs=[whole(8, ch)] * tensor
            + [
                whole(rows, ch),
                whole(rows, ch),
                whole(rows, width),
                whole(rows, width),
                whole(rows, width),
                whole(rows, 2),
                block(rows, hidden),
                whole(8, width),
                whole(width, ch),
                whole(3, ch),
                whole(ch, ch),
                whole(ch, ch),
                whole(1, ch),
                whole(rows, width),
            ]
            + [far] * len(pieces),
            out_specs=(
                whole(8, ch),
                whole(rows, width),
                block(rows, hidden),
                whole(rows, width),
                whole(rows, width),
                whole(tensor, rows, head_width),
                whole(width + pack_rows, ch),
            ),
            scratch_shapes=[
                pltpu.VMEM((rows, width), F32),
                pltpu.VMEM((pack_rows, ch), F32),
                pltpu.VMEM((tensor, width, 2 * hidden), BF16),
                pltpu.VMEM((tensor, width, head_width), BF16),
                pltpu.SemaphoreType.DMA((tensor,)),
                pltpu.SemaphoreType.DMA,
            ],
        ),
        out_shape=(
            jax.ShapeDtypeStruct((8, ch), F32),
            jax.ShapeDtypeStruct((rows, width), BF16),
            jax.ShapeDtypeStruct((tensor, rows, hidden), BF16),
            jax.ShapeDtypeStruct((rows, width), BF16),
            jax.ShapeDtypeStruct((rows, width), F32),
            jax.ShapeDtypeStruct((tensor, rows, head_width), BF16),
            jax.ShapeDtypeStruct((width + pack_rows, ch), BF16),
        ),
        compiler_params=pltpu.CompilerParams(vmem_limit_bytes=34 * MIB),
        cost_estimate=LIGHT,
        name="rows_backward",
    )(
        info, *stats, *far_off(student, pool_logit, cotangent, xh1, xh2, rs, slope), vec_table,
        cls_proj, cls_vec, cls_hidden, cls_out, cls_bias, *far_off(out_low, *pieces),
    )


def weight_grads_kernel(dp, shard, tensor, info_ref, x_ref, two_ref, one_ref, gu_ref, act_ref, *refs):
    mixed, outs, lefts, mixed_s = refs[:tensor], refs[tensor:-4], refs[-4:-1], refs[-1]
    j = pl.program_id(0)
    hidden = gu_ref.shape[2]
    width = x_ref.shape[1]
    halves = 2 if len(outs) == 4 else 1

    @pl.when(j == 0)
    def _():
        for t in range(tensor):
            mixed_s[t] = mixed[t][...]
        for source, left in zip((x_ref, two_ref, one_ref), lefts):
            turned = source[...].T
            if halves == 1:
                left[...] = turned
                continue
            for b in range(dp):
                offset = jnp.bitwise_xor(info_ref[INFO_D], b)
                at = lax.rem(offset, 2) * (dp // 2) + offset // 2
                left[pl.ds(at * shard, shard), :] = turned[b * shard : (b + 1) * shard, :]

    count = width // halves
    rights = (gu_ref[0], act_ref[0], mixed_s[j])
    ends = (0, hidden, 2 * hidden, 2 * hidden + mixed_s.shape[2])

    def write(out, n):
        here = slice(n * count, (n + 1) * count)
        for m in range(3):
            part = dot_nn(lefts[m][here, :], rights[m]).astype(BF16)
            out[0, :, :, ends[m] : ends[m + 1]] = part.reshape(
                out.shape[1], out.shape[2], ends[m + 1] - ends[m]
            )

    if halves == 1:
        write(outs[0], 0)
    for side in range(halves if halves > 1 else 0):

        @pl.when((j < tensor // 2) if side == 0 else (j >= tensor // 2))
        def _():
            write(outs[side], 0)
            write(outs[2 + side], 1)


def weight_grads(info, dp, shard, x_low, two_low, one_low, upper_low, act, mixed):
    tensor, rows, hidden = upper_low.shape
    width = x_low.shape[1]
    head_width = mixed[0].shape[1]
    total = 2 * hidden + head_width
    half = tensor // 2
    if shard % 16:
        out_specs = (block(1, width, total),)
        shapes = (jax.ShapeDtypeStruct((tensor, 1, width, total), BF16),)
    else:
        shape = (dp // 2, shard, total)
        near = pl.BlockSpec((1,) + shape, lambda j, *_: (jnp.minimum(j, half - 1), 0, 0, 0))
        far = pl.BlockSpec((1,) + shape, lambda j, *_: (jnp.maximum(j - half, 0), 0, 0, 0))
        out_specs = (near, far) * 2
        shapes = (jax.ShapeDtypeStruct((half,) + shape, BF16),) * 4
    return pl.pallas_call(
        functools.partial(weight_grads_kernel, dp, shard, tensor),
        grid_spec=pltpu.PrefetchScalarGridSpec(
            num_scalar_prefetch=1,
            grid=(tensor,),
            in_specs=[
                whole(rows, width),
                whole(rows, width),
                whole(rows, width),
                block(rows, hidden),
                block(rows, hidden),
            ]
            + [whole(rows, head_width)] * tensor,
            out_specs=out_specs,
            scratch_shapes=[pltpu.VMEM((width, rows), BF16)] * 3
            + [pltpu.VMEM((tensor, rows, head_width), BF16)],
        ),
        out_shape=shapes,
        compiler_params=pltpu.CompilerParams(vmem_limit_bytes=26 * MIB),
        cost_estimate=LIGHT,
        name="weight_grads",
    )(info, *far_off(x_low), two_low, one_low, upper_low, *far_off(act, *mixed))


def weights_to_owner(parts, dp, tensor, z):
    if len(parts) == 1:
        order = (z - jnp.arange(tensor)) % tensor
        whole_parts = jnp.take(parts[0], order, axis=0)
        owned = lax.psum_scatter(
            whole_parts.reshape(-1, whole_parts.shape[-1]), ("tensor", "dp"),
            scatter_dimension=0, tiled=True,
        ).astype(F32)

        def done(came, late):
            yield (), owned
            return owned

        return (), (), lambda sent: (), done
    keep, give = parts[:2], parts[2:]
    bits = bits_of(dp)
    got = [swapped(v, "dp", dp, bits[0]) for v in give]
    half = tensor // 2
    orders = (bits[1:], bits[1:][::-1])
    sent = []
    for side, order in enumerate(orders):
        value = split_by(keep[side], bits[1:], order[0], 1).astype(F32)
        value = value + split_by(got[side], bits[1:], order[0], 1).astype(F32)
        sent.append(value.astype(BF16))

    def first(sent):
        return [swapped(sent[k], "dp", dp, orders[k][0]) for k in range(2)]

    def finish(came, late):
        sent = None
        values, lefts = [], [list(bits[1:]), list(bits[1:])]
        for side, order in enumerate(orders):
            value = split_by(keep[side], bits[1:], order[0], 0).astype(F32)
            values.append(value + split_by(late[side], bits[1:], order[0], 0).astype(F32))
        for n in range(len(bits) - 1):
            if n:
                came = [swapped(sent[k], "dp", dp, orders[k][n]) for k in range(2)]
                came = yield sent, came
            sent = []
            for k in range(2):
                value = values[k] + came[k].astype(F32)
                lefts[k].remove(orders[k][n])
                if n + 2 < len(bits):
                    bit = orders[k][n + 1]
                    sent.append(split_by(value, lefts[k], bit, 1).astype(BF16))
                    value = split_by(value, lefts[k], bit, 0)
                values[k] = value
        own = [value[t, 0] for value in values for t in range(half)]
        total = own[1]
        for t in list(range(2, tensor)) + [0]:
            total = total.astype(BF16)
            came = yield total, shifted(total, "tensor", tensor, 1)
            total = own[t] + came.astype(F32)
        return total

    return sent, got, first, finish


def split_by(value, left, bit, side):
    shape = value.shape
    place = left.index(bit)
    low, high = 1 << place, 1 << (len(left) - 1 - place)
    pairs = value.reshape(shape[0], high, 2, low, *shape[2:])
    return pairs[:, :, side].reshape(shape[0], high * low, *shape[2:])


def first_rows_kernel(d_ref, w_ref, out_ref):
    out_ref[...] = dot_nt(d_ref[0], w_ref[...]).astype(BF16)


def first_rows(d_chunks, w_in):
    _, rows, width = d_chunks.shape
    return pl.pallas_call(
        first_rows_kernel,
        grid=(1,),
        out_shape=jax.ShapeDtypeStruct((rows, w_in.shape[0]), BF16),
        in_specs=[
            pl.BlockSpec((1, rows, width), lambda n: (1, 0, 0)),
            whole(*w_in.shape),
        ],
        out_specs=whole(rows, w_in.shape[0]),
        compiler_params=pltpu.CompilerParams(vmem_limit_bytes=12 * MIB),
        cost_estimate=LIGHT,
        name="first_rows",
    )(d_chunks, w_in)


def rest_rows_kernel(d_ref, w_ref, out_ref):
    out_ref[0] = dot_nt(d_ref[0], w_ref[...]).astype(BF16)


def rest_rows(d_chunks, w_in):
    tensor, rows, width = d_chunks.shape
    model = w_in.shape[0]
    return pl.pallas_call(
        rest_rows_kernel,
        grid=(tensor - 1,),
        out_shape=jax.ShapeDtypeStruct((tensor - 1, rows, model), BF16),
        in_specs=[
            pl.BlockSpec((1, rows, width), lambda n: (lax.rem(n + 2, tensor), 0, 0)),
            whole(*w_in.shape),
        ],
        out_specs=block(rows, model),
        compiler_params=pltpu.CompilerParams(vmem_limit_bytes=12 * MIB),
        cost_estimate=LIGHT,
        name="rest_rows",
    )(d_chunks, w_in)


def in_grad_kernel(tensor, d_ref, *refs):
    seq_refs, grad_ref = refs[:tensor], refs[tensor]
    n = pl.program_id(0)
    for t in range(tensor):

        @pl.when(n == t)
        def _():
            part = dot_tn(seq_refs[t][...], d_ref[0])
            if t == 0:
                grad_ref[...] = part
            else:
                grad_ref[...] += part


def in_grad(d_chunks, seq_rows):
    tensor, rows, width = d_chunks.shape
    model = seq_rows[0].shape[1]
    return pl.pallas_call(
        functools.partial(in_grad_kernel, tensor),
        grid=(tensor,),
        out_shape=jax.ShapeDtypeStruct((model, width), F32),
        in_specs=[block(rows, width)] + [whole(rows, model)] * tensor,
        out_specs=whole(model, width),
        compiler_params=pltpu.CompilerParams(vmem_limit_bytes=16 * MIB),
        cost_estimate=HEAVY,
        name="in_grad",
    )(d_chunks, *seq_rows)


def per_device(
    dp, tensor, tokens, cotangent, labels, piece_start, piece_len, w_qkv, w_out, w_up, w_down,
    vec_table, ff_bias, cls_proj, cls_vec, cls_hidden, cls_out, cls_bias,
):
    rows, width = tokens.shape
    local = w_qkv.shape[2]
    heads = local // HEAD_DIM
    padded = -(-local // LANES) * LANES
    shard = w_qkv.shape[0]
    hidden = w_up.shape[1]
    ch = cls_proj.shape[1]
    z = lax.axis_index("tensor")
    info = jnp.concatenate(
        [z.reshape(1), lax.axis_index("dp").reshape(1), labels, piece_start[0], piece_len[0]]
    ).astype(jnp.int32)

    extra = padded - local
    qkv_shard = jnp.pad(w_qkv, ((0, 0), (0, 0), (0, extra))).reshape(shard, 3 * padded)
    ff_ring, seq_rows = [], []
    ff_shard = jnp.concatenate([w_up, w_down.T, w_out.T], axis=1)
    _, _, w_in = in_turn(
        vec_table[0, 0],
        {
            "rows": ring_chain(tokens, tensor, seq_rows),
            "ff": ring_chain(ff_shard, tensor, ff_ring),
            "in": gather_chain(qkv_shard, "dp", dp),
        },
        [("in",), ("in", "ff"), ("in",), ("ff",), ("rows",), ("ff",), ("rows",), ("rows",)],
    )
    half = tensor // 2
    pieces = [
        lax.all_gather(jnp.stack(ff_ring[n : n + half]), "dp") for n in (0, half)
    ]
    if shard % 16:
        pieces = [
            p.transpose(1, 0, 2, 3).reshape(1, half, dp * shard, p.shape[-1]) for p in pieces
        ]

    q_bias = lax.dynamic_slice_in_dim(vec_table[0], z * local, local, 0)
    v_bias = lax.dynamic_slice_in_dim(vec_table[1], z * local, local, 0)
    in_bias = jnp.pad(
        jnp.stack([q_bias, jnp.zeros_like(q_bias), v_bias]), ((0, 0), (0, extra))
    ).reshape(1, 3 * padded)

    def exchanged(parts):
        return [parts[0]] + [
            shifted(parts[tensor - s], "tensor", tensor, s) for s in range(1, tensor)
        ]

    chunks = [
        (jnp.dot(part, w_in, preferred_element_type=F32) + in_bias).astype(BF16)
        for part in seq_rows
    ]
    mixed, lse = attend_forward(info, chunks, heads)
    mixed_parts = exchanged(mixed)
    kept = rows_forward(
        info, pieces, mixed_parts, tokens, vec_table,
        ff_bias.reshape(tensor, 1, hidden), cls_proj, cls_vec,
    )
    out_low, x_low, act, _, _, _, _, _, _, stats = kept
    all_stats = exchanged([stats] * tensor)
    (
        logits, two_low, upper_low, one_low, grad_h_one, grad_mixed, small,
    ) = rows_backward(
        info, pieces, all_stats, kept, cotangent, vec_table, cls_proj, cls_vec,
        cls_hidden, jnp.pad(cls_out, ((0, 0), (0, ch - CLASSES))),
        jnp.pad(cls_bias, (0, ch - CLASSES)).reshape(1, ch),
    )
    grad_rows = exchanged(grad_mixed)
    bits = bits_of(tensor)
    small_came = swapped(small, "tensor", tensor, bits[0])
    ff_parts = weight_grads(
        info, dp, shard, x_low, two_low, one_low, upper_low, act, mixed_parts
    )
    ff_parts, grad_rows[1], small_came = lax.optimization_barrier(
        (ff_parts, grad_rows[1], small_came)
    )
    sent, got, first, finish = weights_to_owner(ff_parts, dp, tensor, z)
    small = small + small_came
    sent, small, grad_rows = lax.optimization_barrier((sent, small, grad_rows))
    small_came = swapped(small, "tensor", tensor, bits[1])

    d_chunks, bias_sums = attend_backward(info, chunks, grad_rows, mixed, lse, heads)
    d_chunks, bias_sums, came, late, small_came = lax.optimization_barrier(
        (d_chunks, bias_sums, first(sent), got, small_came)
    )
    first_part = first_rows(d_chunks, w_in)
    came, late = after((came, late), first_part)

    def small_chain():
        total = small + small_came
        for bit in bits[2:]:
            got = yield total, swapped(total, "tensor", tensor, bit)
            total = total + got
        for bit in bits_of(dp):
            got = yield total, swapped(total, "dp", dp, bit)
            total = total + got
        return total.astype(F32)

    def rows_chain():
        came = shifted(first_part, "tensor", tensor, 1)
        later = yield first_part, d_chunks
        rest = rest_rows(later, w_in)
        total = first_part
        for t in range(2, tensor):
            came = yield (total, rest), came
            total = (rest[t - 2].astype(F32) + came.astype(F32)).astype(BF16)
            came = shifted(total, "tensor", tensor, 1)
        came = yield total, came
        return grad_h_one + rest[tensor - 2].astype(F32) + came.astype(F32)

    def in_chain():
        later = yield (), d_chunks
        grad = in_grad(later, seq_rows)
        grad = yield (), grad
        rider = jnp.pad(bias_sums, ((0, 8), (0, 2 * padded)))
        return (
            yield from owner_chain(
                grad.reshape(dp, shard, 3 * padded), rider, "dp", dp, "tensor", tensor
            )
        )

    grad_tokens, ff_own, (grad_in, riders), sums = in_turn(
        bias_sums[0, 0],
        {
            "rows": rows_chain(),
            "ff": finish(came, late),
            "in": in_chain(),
            "small": small_chain(),
        },
        [
            ("rows",), ("rows",), ("in",), ("ff",), ("in",), ("small",), ("in",), ("small",),
            ("rows",), ("in",), ("ff",), ("small",), ("in",), ("ff",), ("in",), ("small",),
            ("rows",), ("ff",),
        ],
    )
    grad_w_qkv = grad_in.reshape(shard, 3, padded)[:, :, :local]
    bias_sum = riders[:, :2, :local].transpose(1, 0, 2).reshape(2, width)

    proj_sum, pack_sum = sums[:width], sums[width:]
    hid_sum = pack_sum[8 : 8 + ch]
    out_w_sum = pack_sum[8 + ch : 8 + 2 * ch, :CLASSES]
    at = 8 + 2 * ch
    vec_sum = pack_sum[at : at + 6 * width // ch].reshape(6, width)
    ff_bias_sum = pack_sum[at + 6 * width // ch :].reshape(-1)
    return (
        out_low,
        logits[0:1, :CLASSES],
        grad_tokens,
        grad_w_qkv,
        ff_own[:, 2 * hidden :].T,
        ff_own[:, :hidden],
        ff_own[:, hidden : 2 * hidden].T,
        jnp.concatenate([bias_sum, vec_sum], axis=0),
        ff_bias_sum,
        proj_sum,
        pack_sum[:3],
        hid_sum,
        out_w_sum,
        pack_sum[3, :CLASSES],
    )


def solution(mesh):
    dp, tensor = mesh.shape["dp"], mesh.shape["tensor"]
    rows = P(("dp", "tensor"), None)
    cut = P("dp", "tensor")
    turned_cut = P("tensor", "dp")
    return jax.shard_map(
        functools.partial(per_device, dp, tensor),
        mesh=mesh,
        in_specs=(
            rows, rows, P("dp"), P("dp", None), P("dp", None), P("dp", None, "tensor"),
            turned_cut, cut, turned_cut, P(), P(), P(), P(), P(), P(), P(),
        ),
        out_specs=(
            rows, P("dp", None), rows, P("dp", None, "tensor"), turned_cut, cut, turned_cut,
            P(), P(), P(), P(), P(), P(), P(),
        ),
        check_vma=False,
    )
```

```python
import functools

import jax
import jax.numpy as jnp
from jax import lax
from jax.experimental import pallas as pl
from jax.experimental.pallas import tpu as pltpu
from jax.sharding import PartitionSpec as P

HEAD_DIM = 64
CLASSES = 14
PIECE_BLOCK = 256
POOL_HEADS = 2
LANES = 128
NORM_EPS = 1e-05
MASK_FILL = -1e30
PRECISE = lax.Precision.HIGHEST
F32 = jnp.float32
BF16 = jnp.bfloat16
MIB = 1024 * 1024
LIGHT = pl.CostEstimate(flops=1024, bytes_accessed=1024, transcendentals=0)
HEAVY = pl.CostEstimate(flops=4 * 10**10, bytes_accessed=1024, transcendentals=0)


def dot_nn(a, b, precision=None):
    return lax.dot_general(
        a, b, (((1,), (0,)), ((), ())), preferred_element_type=F32, precision=precision
    )


def dot_nt(a, b, precision=None):
    return lax.dot_general(
        a, b, (((1,), (1,)), ((), ())), preferred_element_type=F32, precision=precision
    )


def dot_tn(a, b, precision=None):
    return lax.dot_general(
        a, b, (((0,), (0,)), ((), ())), preferred_element_type=F32, precision=precision
    )


def bits_of(size):
    return [1 << n for n in range(size.bit_length() - 1)]


def swapped(value, axis, size, bit):
    return lax.ppermute(value, axis, [(i, i ^ bit) for i in range(size)])


def shifted(value, axis, size, by):
    return lax.ppermute(value, axis, [(i, (i + by) % size) for i in range(size)])


def after(value, *others):
    return lax.optimization_barrier((value, others))[0]


def in_turn(mark, chains, turns):
    under_way, results = {}, {}

    def advance(name, value):
        try:
            under_way[name] = chains[name].send(value)
        except StopIteration as end:
            under_way.pop(name, None)
            results[name] = end.value

    for name in chains:
        advance(name, None)
    turns = list(turns)
    while under_way:
        turn = turns.pop(0) if turns else tuple(under_way)
        names = [name for name in turn if name in under_way]
        if not names:
            continue
        sent = [value for value, _ in under_way.values()]
        there, mark, _ = lax.optimization_barrier(
            ([under_way[name][1] for name in names], mark, sent)
        )
        for name, value in zip(names, there):
            advance(name, value)
    return [results[name] for name in chains]


def ring_chain(value, size, kept):
    kept.append(value)
    for _ in range(size - 1):
        value = yield value, shifted(value, "tensor", size, 1)
        kept.append(value)
    return kept


def gather_chain(value, axis, size):
    index = lax.axis_index(axis)
    for bit in bits_of(size):
        other = yield value, swapped(value, axis, size, bit)
        low = (index // bit) % 2 == 0
        value = jnp.where(
            low, jnp.concatenate([value, other], 0), jnp.concatenate([other, value], 0)
        )
    return value


def owner_chain(parts, rider, axis, size, other, other_size):
    index = lax.axis_index(axis)
    riding = rider.shape[0]
    for bit in bits_of(size):
        mine = (index // bit) % 2
        count, rows, columns = parts.shape
        pairs = parts.reshape(count // 2, 2, rows, columns)
        keep = lax.dynamic_index_in_dim(pairs, mine, 1, keepdims=False)
        give = lax.dynamic_index_in_dim(pairs, 1 - mine, 1, keepdims=False)
        give = give.reshape(count // 2 * rows, columns)
        give = jnp.concatenate([give, rider]).astype(BF16)
        got = yield give, swapped(give, axis, size, bit)
        parts = keep + got[:-riding].reshape(keep.shape).astype(F32)
        rider = rider.astype(BF16).astype(F32) + got[-riding:].astype(F32)
    rider = rider[:2]
    got = yield rider, [shifted(rider, other, other_size, by) for by in range(1, other_size)]
    index = lax.axis_index(other)
    places = jnp.arange(other_size)[:, None, None]
    riders = 0.0
    for by, value in enumerate([rider] + list(got)):
        mine = places == (index - by) % other_size
        riders = riders + jnp.where(mine, value[None], 0.0)
    return parts[0], riders


def far_off(*values):
    return [pltpu.with_memory_space_constraint(v, pltpu.HBM) for v in values]


INFO_Z, INFO_D, INFO_LABEL, INFO_PIECES = 0, 1, 2, 3


def part_of(info_ref, place, tensor):
    return lax.rem(info_ref[INFO_Z] - place + tensor, tensor)


def block_range(info_ref, block):
    first, stop, inside_any = block, block + 1, jnp.int32(0)
    pieces = (info_ref.shape[0] - INFO_PIECES) // 2
    for piece in range(pieces):
        begin, count = info_ref[INFO_PIECES + piece], info_ref[INFO_PIECES + pieces + piece]
        inside = jnp.logical_and(block >= begin, block < begin + count)
        first = jnp.where(inside, begin, first)
        stop = jnp.where(inside, begin + count, stop)
        inside_any = jnp.where(inside, jnp.int32(1), inside_any)
    return first, stop, inside_any


def head_lanes(shape, head):
    lane = lax.broadcasted_iota(jnp.int32, shape, len(shape) - 1)
    return (lane >= head * HEAD_DIM) & (lane < (head + 1) * HEAD_DIM)


def attend_forward_kernel(heads, info_ref, *refs):
    tensor = len(refs) - 2 - 3
    chunks = refs[:tensor]
    o_ref, lse_ref = refs[tensor : tensor + 2]
    q_s, k_s, vt_s = refs[tensor + 2 :]
    rows, padded = chunks[0].shape[0], chunks[0].shape[1] // 3
    blk = PIECE_BLOCK
    blocks = tensor * rows // blk
    per_chunk = rows // blk
    scale = HEAD_DIM ** (-0.5)
    for t in range(tensor):
        quarter = part_of(info_ref, t, tensor)

        def one_block(part, carry):
            b = quarter * per_chunk + part
            here = pl.ds(part * blk, blk)
            q = chunks[t][here, 0:padded]
            for h in range(heads):
                q_s[h, b] = jnp.where(head_lanes(q.shape, h), q * scale, 0.0).astype(BF16)
            pair, at = b // 2, pl.multiple_of(lax.rem(b, 2) * blk, blk)
            k_s[pair, pl.ds(at, blk), :] = chunks[t][here, padded : 2 * padded]
            vt_s[pair, :, pl.ds(at, blk)] = chunks[t][here, 2 * padded : 3 * padded].T
            return carry

        lax.fori_loop(0, per_chunk, one_block, 0)


    def one_query(i, carry):
        _, stop, inside = block_range(info_ref, i)
        q_h = [q_s[h, i] for h in range(heads)]
        query = i * blk + lax.broadcasted_iota(jnp.int32, (1, blk), 1)
        limit = jnp.maximum(query, jnp.where(inside > 0, stop * blk - 1, 0))

        def step(j, state, masked):
            tops, totals, mixed = state
            keys = 2 * blk
            if masked:
                key = j * keys + lax.broadcasted_iota(jnp.int32, (keys, blk), 0)
                seen = key <= limit
            k_j = k_s[j]
            scores = [dot_nt(k_j, q_h[h]) for h in range(heads)]
            if masked:
                scores = [jnp.where(seen, s, MASK_FILL) for s in scores]
            new_tops = [
                jnp.maximum(tops[h], jnp.max(scores[h], axis=0, keepdims=True))
                for h in range(heads)
            ]
            ps = [jnp.exp(scores[h] - new_tops[h]) for h in range(heads)]
            fades = [jnp.exp(tops[h] - new_tops[h]) for h in range(heads)]
            new_totals = [
                totals[h] * fades[h] + jnp.sum(ps[h], axis=0, keepdims=True) for h in range(heads)
            ]
            new_mixed = [
                mixed[h] * fades[h]
                + dot_nn(vt_s[j, h * HEAD_DIM : (h + 1) * HEAD_DIM, :], ps[h].astype(BF16))
                for h in range(heads)
            ]
            return tuple(new_tops), tuple(new_totals), tuple(new_mixed)

        state = (
            tuple(jnp.full((1, blk), MASK_FILL, F32) for _ in range(heads)),
            tuple(jnp.zeros((1, blk), F32) for _ in range(heads)),
            tuple(jnp.zeros((HEAD_DIM, blk), F32) for _ in range(heads)),
        )
        last = i // 2
        state = lax.fori_loop(0, last, lambda j, c: step(j, c, False), state)
        tops, totals, mixed = lax.fori_loop(
            last, (stop + 1) // 2, lambda j, c: step(j, c, True), state
        )
        outs = [mixed[h] * (1.0 / totals[h]) for h in range(heads)]
        lses = [tops[h] + jnp.log(totals[h]) for h in range(heads)]
        t = part_of(info_ref, i // per_chunk, tensor)
        here = pl.ds(lax.rem(i, per_chunk) * blk, blk)
        o_ref[t, here, :] = jnp.concatenate(outs, axis=0).T.astype(BF16)
        lse_ref[i] = jnp.concatenate(lses + [jnp.zeros((8 - heads, blk), F32)], axis=0)
        return carry

    lax.fori_loop(0, blocks, one_query, 0)


def attend_forward(info, chunks, heads):
    tensor = len(chunks)
    rows, width = chunks[0].shape
    padded = width // 3
    seq, blk = tensor * rows, PIECE_BLOCK
    blocks = seq // blk
    smem = pl.BlockSpec(memory_space=pltpu.SMEM)
    vmem = pl.BlockSpec(memory_space=pltpu.VMEM)
    return pl.pallas_call(
        functools.partial(attend_forward_kernel, heads),
        out_shape=(
            jax.ShapeDtypeStruct((tensor, rows, heads * HEAD_DIM), BF16),
            jax.ShapeDtypeStruct((blocks, 8, blk), F32),
        ),
        in_specs=[smem] + [vmem] * tensor,
        out_specs=(vmem, vmem),
        scratch_shapes=[
            pltpu.VMEM((heads, blocks, blk, padded), BF16),
            pltpu.VMEM((blocks // 2, 2 * blk, padded), BF16),
            pltpu.VMEM((blocks // 2, padded, 2 * blk), BF16),
        ],
        compiler_params=pltpu.CompilerParams(vmem_limit_bytes=24 * MIB),
        cost_estimate=LIGHT,
        name="attend_forward",
    )(info, *chunks)


def attend_backward_kernel(heads, info_ref, *refs):
    tensor = (len(refs) - 2 - 2 - 9) // 2
    chunks, grads = refs[:tensor], refs[tensor : 2 * tensor]
    o_ref, lse_ref, dqkv_ref, bias_ref = refs[2 * tensor : 2 * tensor + 4]
    q_s, k_s, kt_s, v_s, g_s, delta_s, dqt_s, dk_s, dv_s = refs[2 * tensor + 4 :]
    rows, padded = chunks[0].shape[0], chunks[0].shape[1] // 3
    width = heads * HEAD_DIM
    blk = PIECE_BLOCK
    blocks = tensor * rows // blk
    per_chunk = rows // blk
    scale = HEAD_DIM ** (-0.5)
    for t in range(tensor):
        quarter = part_of(info_ref, t, tensor)

        def one_block(part, carry):
            b = quarter * per_chunk + part
            here = pl.ds(part * blk, blk)
            q = chunks[t][here, 0:padded]
            g = grads[t][here, :]
            for h in range(heads):
                q_s[h, b] = jnp.where(head_lanes(q.shape, h), q * scale, 0.0).astype(BF16)
                g_s[h, b, :, 0:width] = jnp.where(head_lanes(g.shape, h), g, 0.0).astype(BF16)
                if padded > width:
                    g_s[h, b, :, width:padded] = jnp.zeros((blk, padded - width), BF16)
            k = chunks[t][here, padded : 2 * padded]
            pair, at = b // 2, pl.multiple_of(lax.rem(b, 2) * blk, blk)
            k_s[pair, pl.ds(at, blk), :] = k
            v_s[pair, pl.ds(at, blk), :] = chunks[t][here, 2 * padded : 3 * padded]
            kt_s[pair, :, pl.ds(at, blk)] = k.T
            prod = (g.astype(F32) * o_ref[t, here, :].astype(F32)).T
            sums = [
                jnp.sum(prod[h * HEAD_DIM : (h + 1) * HEAD_DIM, :], axis=0, keepdims=True)
                for h in range(heads)
            ]
            delta_s[b] = jnp.concatenate(sums + [jnp.zeros((8 - heads, blk), F32)], axis=0)
            dqt_s[b] = jnp.zeros((padded, blk), F32)
            return carry

        lax.fori_loop(0, per_chunk, one_block, 0)
    bias_ref[...] = jnp.zeros_like(bias_ref)

    keys = 2 * blk

    def one_pair(j, carry):
        first, _, _ = block_range(info_ref, 2 * j)
        also, _, _ = block_range(info_ref, 2 * j + 1)
        dk_s[...] = jnp.zeros_like(dk_s)
        dv_s[...] = jnp.zeros_like(dv_s)

        def step(i, masked):
            lse, delta = lse_ref[i], delta_s[i]
            if masked:
                _, stop, inside = block_range(info_ref, i)
                query = i * blk + lax.broadcasted_iota(jnp.int32, (1, blk), 1)
                limit = jnp.maximum(query, jnp.where(inside > 0, stop * blk - 1, 0))
                key = j * keys + lax.broadcasted_iota(jnp.int32, (keys, blk), 0)
                seen = key <= limit
            k_j, v_j = k_s[j], v_s[j]
            q_h = [q_s[h, i] for h in range(heads)]
            g_h = [g_s[h, i] for h in range(heads)]
            lows, ds = [], []
            for h in range(heads):
                p = jnp.exp(dot_nt(k_j, q_h[h]) - lse[h : h + 1, :])
                dp = dot_nt(v_j, g_h[h])
                if masked:
                    p = jnp.where(seen, p, 0.0)
                lows.append(p.astype(BF16))
                ds.append((p * (dp - delta[h : h + 1, :])).astype(BF16))
            dv_s[...] += dot_nn(jnp.concatenate(lows, axis=1), jnp.concatenate(g_h, axis=0))
            dk_s[...] += dot_nn(jnp.concatenate(ds, axis=1), jnp.concatenate(q_h, axis=0))
            for h in range(heads):
                lo, hi = h * HEAD_DIM, (h + 1) * HEAD_DIM
                dqt_s[i, lo:hi, :] += dot_nn(kt_s[j, lo:hi, :], ds[h])

        def masked_step(i, c):
            step(i, True)
            return c

        def open_step(i, c):
            step(i, False)
            return c

        lax.fori_loop(jnp.minimum(first, also), 2 * j + 2, masked_step, 0)
        lax.fori_loop(2 * j + 2, blocks, open_step, 0)
        for part in range(2):
            b = 2 * j + part
            t = part_of(info_ref, b // per_chunk, tensor)
            here = pl.ds(lax.rem(b, per_chunk) * blk, blk)
            side = slice(part * blk, (part + 1) * blk)
            dqkv_ref[t, here, padded : 2 * padded] = dk_s[side, :].astype(BF16)
            dqkv_ref[t, here, 2 * padded : 3 * padded] = dv_s[side, :].astype(BF16)
        bias_ref[1:2, :] = bias_ref[1:2, :] + jnp.sum(dv_s[...], axis=0, keepdims=True)
        return carry

    lax.fori_loop(0, blocks // 2, one_pair, 0)

    def one_query(i, carry):
        dq = dqt_s[i].T * scale
        t = part_of(info_ref, i // per_chunk, tensor)
        here = pl.ds(lax.rem(i, per_chunk) * blk, blk)
        dqkv_ref[t, here, 0:padded] = dq.astype(BF16)
        bias_ref[0:1, :] = bias_ref[0:1, :] + jnp.sum(dq, axis=0, keepdims=True)
        return carry

    lax.fori_loop(0, blocks, one_query, 0)


def attend_backward(info, chunks, grads, mixed, lse, heads):
    tensor = len(chunks)
    rows, width = chunks[0].shape
    padded = width // 3
    seq, blk = tensor * rows, PIECE_BLOCK
    blocks = seq // blk
    smem = pl.BlockSpec(memory_space=pltpu.SMEM)
    vmem = pl.BlockSpec(memory_space=pltpu.VMEM)
    return pl.pallas_call(
        functools.partial(attend_backward_kernel, heads),
        out_shape=(
            jax.ShapeDtypeStruct((tensor, rows, width), BF16),
            jax.ShapeDtypeStruct((8, padded), F32),
        ),
        in_specs=[smem] + [vmem] * (2 * tensor + 2),
        out_specs=(vmem, vmem),
        scratch_shapes=[
            pltpu.VMEM((heads, blocks, blk, padded), BF16),
            pltpu.VMEM((blocks // 2, 2 * blk, padded), BF16),
            pltpu.VMEM((blocks // 2, padded, 2 * blk), BF16),
            pltpu.VMEM((blocks // 2, 2 * blk, padded), BF16),
            pltpu.VMEM((heads, blocks, blk, padded), BF16),
            pltpu.VMEM((blocks, 8, blk), F32),
            pltpu.VMEM((blocks, padded, blk), F32),
            pltpu.VMEM((2 * blk, padded), F32),
            pltpu.VMEM((2 * blk, padded), F32),
        ],
        compiler_params=pltpu.CompilerParams(vmem_limit_bytes=34 * MIB),
        cost_estimate=LIGHT,
        name="attend_backward",
    )(info, *far_off(*chunks, *grads, mixed, lse))


def start_weights(pieces, w_s, wo_s, sems, o_sem):
    wide = w_s.shape[2]
    copies = []
    t = 0
    for piece in pieces:
        blocks, parts, rows, _ = piece.shape
        for part in range(parts):
            for n in range(blocks):
                copies.append((piece.at[n, part], t, pl.ds(n * rows, rows)))
            t += 1
    for source, t, here in copies:
        pltpu.make_async_copy(source.at[:, wide:], wo_s.at[t, here, :], o_sem).start()
    for source, t, here in copies:
        pltpu.make_async_copy(source.at[:, :wide], w_s.at[t, here, :], sems.at[t]).start()


def center(values):
    mean = jnp.mean(values, axis=-1, keepdims=True)
    centered = values - mean
    spread = jnp.mean(centered * centered, axis=-1, keepdims=True)
    return centered, lax.rsqrt(spread + NORM_EPS)


def same_head(value):
    row = lax.broadcasted_iota(jnp.int32, (value, value), 0) // (value // POOL_HEADS)
    col = lax.broadcasted_iota(jnp.int32, (value, value), 1) // (value // POOL_HEADS)
    return (row == col).astype(F32)


def rows_forward_kernel(tensor, arrays, info_ref, *refs):
    mixed = refs[:tensor]
    tok_ref, vec_ref, bias_ref, proj_ref, cvec_ref = refs[tensor : tensor + 5]
    pieces = refs[tensor + 5 : tensor + 5 + arrays]
    (
        low_ref, xlow_ref, act_ref, slope_ref, xh1_ref, xh2_ref, rs_ref, stud_ref, e_ref,
        stats_ref, acc_s, w_s, wo_s, sems, o_sem,
    ) = refs[tensor + 5 + arrays :]
    j = pl.program_id(0)
    hidden = act_ref.shape[2]
    rows = tok_ref.shape[0]
    half = min(256, rows)

    @pl.when(j == 0)
    def _():
        start_weights(pieces, w_s, wo_s, sems, o_sem)
        pltpu.make_async_copy(wo_s, wo_s, o_sem).wait()

        def first_part(n, carry):
            here = pl.ds(n * half, half)
            total = tok_ref[here, :].astype(F32) + vec_ref[2:3, :]
            for s in range(tensor):
                total = total + dot_nt(mixed[s][here, :], wo_s[s])
            centered, rstd = center(total)
            xhat = centered * rstd
            xh1_ref[here, :] = xhat
            rs_ref[here, 0:1] = rstd
            x_one = xhat * vec_ref[3:4, :] + vec_ref[4:5, :]
            xlow_ref[here, :] = x_one.astype(BF16)
            acc_s[here, :] = x_one + vec_ref[5:6, :]
            return carry

        lax.fori_loop(0, rows // half, first_part, 0)

    pltpu.make_async_copy(w_s.at[j], w_s.at[j], sems.at[j]).wait()

    def rows_part(n, carry):
        here = pl.ds(n * half, half)
        upper = dot_nn(xlow_ref[here, :], w_s[j, :, 0:hidden]) + bias_ref[0]
        phi = 0.5 * (1.0 + lax.erf(upper * (0.5**0.5)))
        act = (upper * phi).astype(BF16)
        slope = phi + upper * (jnp.exp(-0.5 * upper * upper) * 0.3989422804014327)
        act_ref[0, here, :] = act
        slope_ref[0, here, :] = slope.astype(BF16)
        acc_s[here, :] = acc_s[here, :] + dot_nt(act, w_s[j, :, hidden:])
        return carry

    lax.fori_loop(0, rows // half, rows_part, 0)

    @pl.when(j == pl.num_programs(0) - 1)
    def _():
        def last_part(n, carry):
            here = pl.ds(n * half, half)
            centered, rstd = center(acc_s[here, :])
            xhat = centered * rstd
            xh2_ref[here, :] = xhat
            rs_ref[here, 1:2] = rstd
            low = (xhat * vec_ref[6:7, :] + vec_ref[7:8, :]).astype(BF16)
            low_ref[here, :] = low
            stud_ref[here, :] = dot_nn(low, proj_ref[...]) + cvec_ref[0:1, :]
            return carry

        lax.fori_loop(0, rows // half, last_part, 0)
        student = stud_ref[...]
        width = student.shape[1]
        scale = (width // POOL_HEADS) ** (-0.5)
        e = dot_nn(student * (cvec_ref[1:2, :] * scale), same_head(width), PRECISE)
        e_ref[...] = e
        top = jnp.max(e, axis=0, keepdims=True)
        w = jnp.exp(e - top)
        stats_ref[...] = jnp.concatenate(
            [
                top,
                jnp.sum(w, axis=0, keepdims=True),
                jnp.sum(w * student, axis=0, keepdims=True),
                jnp.zeros((5, width), F32),
            ],
            axis=0,
        )


def whole(*shape):
    return pl.BlockSpec(shape, lambda j, *_: (0,) * len(shape))


def block(*shape):
    return pl.BlockSpec((1,) + shape, lambda j, *_: (j,) + (0,) * len(shape))


def rows_forward(info, pieces, mixed, tokens, vec_table, ff_bias, cls_proj, cls_vec):
    tensor = len(mixed)
    rows, width = tokens.shape
    head_width = mixed[0].shape[1]
    hidden = ff_bias.shape[2]
    ch = cls_proj.shape[1]
    far = pl.BlockSpec(memory_space=pl.ANY)

    def of_block(j, info_ref):
        return (part_of(info_ref, j, tensor), 0, 0)

    return pl.pallas_call(
        functools.partial(rows_forward_kernel, tensor, len(pieces)),
        grid_spec=pltpu.PrefetchScalarGridSpec(
            num_scalar_prefetch=1,
            grid=(tensor,),
            in_specs=[whole(rows, head_width)] * tensor
            + [
                whole(rows, width),
                whole(8, width),
                pl.BlockSpec((1, 1, hidden), of_block),
                whole(width, ch),
                whole(3, ch),
            ]
            + [far] * len(pieces),
            out_specs=(
                whole(rows, width),
                whole(rows, width),
                block(rows, hidden),
                block(rows, hidden),
                whole(rows, width),
                whole(rows, width),
                whole(rows, 2),
                whole(rows, ch),
                whole(rows, ch),
                whole(8, ch),
            ),
            scratch_shapes=[
                pltpu.VMEM((rows, width), F32),
                pltpu.VMEM((tensor, width, 2 * hidden), BF16),
                pltpu.VMEM((tensor, width, head_width), BF16),
                pltpu.SemaphoreType.DMA((tensor,)),
                pltpu.SemaphoreType.DMA,
            ],
        ),
        out_shape=(
            pltpu.HBM((rows, width), BF16),
            pltpu.HBM((rows, width), BF16),
            pltpu.HBM((tensor, rows, hidden), BF16),
            pltpu.HBM((tensor, rows, hidden), BF16),
            pltpu.HBM((rows, width), F32),
            pltpu.HBM((rows, width), F32),
            pltpu.HBM((rows, 2), F32),
            pltpu.HBM((rows, ch), F32),
            pltpu.HBM((rows, ch), F32),
            jax.ShapeDtypeStruct((8, ch), F32),
        ),
        compiler_params=pltpu.CompilerParams(vmem_limit_bytes=34 * MIB),
        cost_estimate=LIGHT,
        name="rows_forward",
    )(info, *far_off(*mixed, tokens), vec_table, ff_bias, cls_proj, cls_vec,
      *far_off(*pieces))


def norm_back(grad, xhat, rstd, gain):
    g = grad * gain
    return (
        g - jnp.mean(g, axis=-1, keepdims=True) - xhat * jnp.mean(g * xhat, axis=-1, keepdims=True)
    ) * rstd


def rows_backward_kernel(tensor, arrays, info_ref, *refs):
    stats_refs = refs[:tensor]
    (
        stud_ref, e_ref, cot_ref, xh1_ref, xh2_ref, rs_ref, slope_ref, vec_ref, proj_ref,
        cvec_ref, chid_ref, cout_ref, cbias_ref, outlow_ref,
    ) = refs[tensor : tensor + 14]
    pieces = refs[tensor + 14 : tensor + 14 + arrays]
    (
        logit_ref, two_ref, gu_ref, one_ref, gh1_ref, gm_ref, small_ref, acc_s, pack_ref, gsl_s,
        w_s, wo_s, sems, o_sem,
    ) = refs[tensor + 14 + arrays :]
    j = pl.program_id(0)
    ch = stud_ref.shape[1]
    hidden = gu_ref.shape[2]
    scale = (ch // POOL_HEADS) ** (-0.5)
    rows, width = cot_ref.shape
    half = min(256, rows)
    sums_at = 8 + 2 * ch
    bias_at = sums_at + 6 * (width // ch)

    def pack_row(row, value):
        at = sums_at + (row - 2) * (width // ch)
        for n in range(width // ch):
            pack_ref[at + n : at + n + 1, :] = value[:, n * ch : (n + 1) * ch]

    @pl.when(j == 0)
    def _():
        start_weights(pieces, w_s, wo_s, sems, o_sem)
        head_of = same_head(ch)
        first = (info_ref[INFO_Z] == 0).astype(F32)
        stats = [r[...] for r in stats_refs]
        top = functools.reduce(jnp.maximum, [v[0:1, :] for v in stats])
        weights = [jnp.exp(v[0:1, :] - top) for v in stats]
        total = sum(v[1:2, :] * w for v, w in zip(stats, weights))
        pooled = sum(v[2:3, :] * w for v, w in zip(stats, weights)) / total

        first_row = lax.broadcasted_iota(jnp.int32, (8, ch), 0) == 0
        lane = lax.broadcasted_iota(jnp.int32, (8, ch), 1)
        pooled8 = jnp.broadcast_to(pooled, (8, ch))
        chid = chid_ref[...].astype(F32)
        cout = cout_ref[...].astype(F32)
        hid = jnp.tanh(dot_nn(pooled8, chid, PRECISE) + cvec_ref[2:3, :])
        logits = dot_nn(hid, cout, PRECISE) + cbias_ref[...]
        logit_ref[...] = logits
        real = lane < CLASSES
        masked = jnp.where(real, logits, MASK_FILL)
        powers = jnp.where(real, jnp.exp(masked - jnp.max(masked, axis=1, keepdims=True)), 0.0)
        probs = powers / jnp.sum(powers, axis=1, keepdims=True)
        grad_logits = probs - (lane == info_ref[INFO_LABEL]).astype(F32)
        grad_pre = (1.0 - hid * hid) * dot_nt(grad_logits, cout, PRECISE)
        grad_pooled = dot_nt(grad_pre, chid, PRECISE)
        gl_row = jnp.where(first_row, grad_logits, 0.0) * first
        gp_row = jnp.where(first_row, grad_pre, 0.0) * first
        pack_ref[8 : 8 + ch, :] = dot_tn(pooled8, gp_row, PRECISE)
        pack_ref[8 + ch : 8 + 2 * ch, :] = dot_tn(hid, gl_row, PRECISE)
        base = dot_nn(grad_pooled * pooled8, head_of, PRECISE)[0:1, :]
        gp = grad_pooled[0:1, :]
        query = cvec_ref[1:2, :] * scale
        student = stud_ref[...]
        w = jnp.exp(e_ref[...] - top) / total
        grad_w = dot_nn(student * gp, head_of, PRECISE)
        grad_e = w * (grad_w - base)
        grad_student = w * gp + grad_e * query
        gsl = grad_student.astype(BF16)
        small_ref[0:width, :] = dot_tn(outlow_ref[...], gsl).astype(BF16)
        pack_ref[0:8, :] = jnp.concatenate(
            [
                jnp.sum(grad_student, axis=0, keepdims=True),
                jnp.sum(grad_e * student, axis=0, keepdims=True) * scale,
                gp_row[0:1, :],
                gl_row[0:1, :],
                jnp.zeros((4, ch), F32),
            ],
            axis=0,
        )
        gsl_s[...] = gsl

        def first_part(n, sums):
            here = pl.ds(n * half, half)
            grad = cot_ref[here, :].astype(F32) + dot_nt(gsl_s[here, :], proj_ref[...])
            xhat = xh2_ref[here, :]
            two = norm_back(grad, xhat, rs_ref[here, 1:2], vec_ref[6:7, :])
            acc_s[here, :] = two
            two_ref[here, :] = two.astype(BF16)
            parts = (two, grad * xhat, grad)
            return tuple(s + jnp.sum(v, axis=0, keepdims=True) for s, v in zip(sums, parts))

        sums = lax.fori_loop(0, rows // half, first_part, (jnp.zeros((1, width), F32),) * 3)
        for n in range(3):
            pack_row(5 + n, sums[n])

    pltpu.make_async_copy(w_s.at[j], w_s.at[j], sems.at[j]).wait()
    heads_row = part_of(info_ref, j, tensor)

    def rows_part(n, bias_row):
        here = pl.ds(n * half, half)
        upper = dot_nn(two_ref[here, :], w_s[j, :, hidden:]) * slope_ref[0, here, :].astype(F32)
        low = upper.astype(BF16)
        gu_ref[0, here, :] = low
        acc_s[here, :] = acc_s[here, :] + dot_nt(low, w_s[j, :, 0:hidden])
        return bias_row + jnp.sum(upper, axis=0, keepdims=True)

    bias_row = lax.fori_loop(
        0, rows // half, rows_part, jnp.zeros((1, hidden), F32)
    )
    for n in range(hidden // ch):
        pack_ref[pl.ds(bias_at + heads_row * (hidden // ch) + n, 1), :] = bias_row[
            :, n * ch : (n + 1) * ch
        ]

    @pl.when(j == pl.num_programs(0) - 1)
    def _():
        pltpu.make_async_copy(wo_s, wo_s, o_sem).wait()

        def last_part(n, sums):
            here = pl.ds(n * half, half)
            grad = acc_s[here, :]
            xhat = xh1_ref[here, :]
            one = norm_back(grad, xhat, rs_ref[here, 0:1], vec_ref[3:4, :])
            gh1_ref[here, :] = one
            low = one.astype(BF16)
            one_ref[here, :] = low
            for s in range(tensor):
                gm_ref[s, here, :] = dot_nn(low, wo_s[s]).astype(BF16)
            parts = (one, grad * xhat, grad)
            return tuple(s + jnp.sum(v, axis=0, keepdims=True) for s, v in zip(sums, parts))

        sums = lax.fori_loop(0, rows // half, last_part, (jnp.zeros((1, width), F32),) * 3)
        for n in range(3):
            pack_row(2 + n, sums[n])
        small_ref[width:, :] = pack_ref[...].astype(BF16)


def rows_backward(
    info, pieces, stats, kept, cotangent, vec_table, cls_proj, cls_vec, cls_hidden,
    cls_out, cls_bias,
):
    out_low, _, _, slope, xh1, xh2, rs, student, pool_logit, _ = kept
    tensor, rows, hidden = slope.shape
    width = xh1.shape[1]
    head_width = pieces[0].shape[3] - 2 * hidden
    ch = student.shape[1]
    far = pl.BlockSpec(memory_space=pl.ANY)
    pack_rows = 8 + 2 * ch + (6 * width + tensor * hidden) // ch

    return pl.pallas_call(
        functools.partial(rows_backward_kernel, tensor, len(pieces)),
        grid_spec=pltpu.PrefetchScalarGridSpec(
            num_scalar_prefetch=1,
            grid=(tensor,),
            in_specs=[whole(8, ch)] * tensor
            + [
                whole(rows, ch),
                whole(rows, ch),
                whole(rows, width),
                whole(rows, width),
                whole(rows, width),
                whole(rows, 2),
                block(rows, hidden),
                whole(8, width),
                whole(width, ch),
                whole(3, ch),
                whole(ch, ch),
                whole(ch, ch),
                whole(1, ch),
                whole(rows, width),
            ]
            + [far] * len(pieces),
            out_specs=(
                whole(8, ch),
                whole(rows, width),
                block(rows, hidden),
                whole(rows, width),
                whole(rows, width),
                whole(tensor, rows, head_width),
                whole(width + pack_rows, ch),
            ),
            scratch_shapes=[
                pltpu.VMEM((rows, width), F32),
                pltpu.VMEM((pack_rows, ch), F32),
                pltpu.VMEM((rows, ch), BF16),
                pltpu.VMEM((tensor, width, 2 * hidden), BF16),
                pltpu.VMEM((tensor, width, head_width), BF16),
                pltpu.SemaphoreType.DMA((tensor,)),
                pltpu.SemaphoreType.DMA,
            ],
        ),
        out_shape=(
            jax.ShapeDtypeStruct((8, ch), F32),
            jax.ShapeDtypeStruct((rows, width), BF16),
            jax.ShapeDtypeStruct((tensor, rows, hidden), BF16),
            jax.ShapeDtypeStruct((rows, width), BF16),
            jax.ShapeDtypeStruct((rows, width), F32),
            jax.ShapeDtypeStruct((tensor, rows, head_width), BF16),
            jax.ShapeDtypeStruct((width + pack_rows, ch), BF16),
        ),
        compiler_params=pltpu.CompilerParams(vmem_limit_bytes=34 * MIB),
        cost_estimate=LIGHT,
        name="rows_backward",
    )(
        info, *stats, *far_off(student, pool_logit, cotangent, xh1, xh2, rs, slope), vec_table,
        cls_proj, cls_vec, cls_hidden, cls_out, cls_bias, *far_off(out_low, *pieces),
    )


def weight_grads_kernel(dp, shard, tensor, info_ref, x_ref, two_ref, one_ref, gu_ref, act_ref, *refs):
    mixed, outs, lefts, mixed_s = refs[:tensor], refs[tensor:-4], refs[-4:-1], refs[-1]
    j = pl.program_id(0)
    hidden = gu_ref.shape[2]
    width = x_ref.shape[1]
    halves = 2 if len(outs) == 4 else 1

    @pl.when(j == 0)
    def _():
        for t in range(tensor):
            mixed_s[t] = mixed[t][...]
        for source, left in zip((x_ref, two_ref, one_ref), lefts):
            turned = source[...].T
            if halves == 1:
                left[...] = turned
                continue
            for b in range(dp):
                offset = jnp.bitwise_xor(info_ref[INFO_D], b)
                at = lax.rem(offset, 2) * (dp // 2) + offset // 2
                left[pl.ds(at * shard, shard), :] = turned[b * shard : (b + 1) * shard, :]

    count = width // halves
    rights = (gu_ref[0], act_ref[0], mixed_s[j])
    ends = (0, hidden, 2 * hidden, 2 * hidden + mixed_s.shape[2])

    def write(out, n):
        here = slice(n * count, (n + 1) * count)
        for m in range(3):
            part = dot_nn(lefts[m][here, :], rights[m]).astype(BF16)
            out[0, :, :, ends[m] : ends[m + 1]] = part.reshape(
                out.shape[1], out.shape[2], ends[m + 1] - ends[m]
            )

    if halves == 1:
        write(outs[0], 0)
    for side in range(halves if halves > 1 else 0):

        @pl.when((j < tensor // 2) if side == 0 else (j >= tensor // 2))
        def _():
            write(outs[side], 0)
            write(outs[2 + side], 1)


def weight_grads(info, dp, shard, x_low, two_low, one_low, upper_low, act, mixed):
    tensor, rows, hidden = upper_low.shape
    width = x_low.shape[1]
    head_width = mixed[0].shape[1]
    total = 2 * hidden + head_width
    half = tensor // 2
    if shard % 16:
        out_specs = (block(1, width, total),)
        shapes = (jax.ShapeDtypeStruct((tensor, 1, width, total), BF16),)
    else:
        shape = (dp // 2, shard, total)
        near = pl.BlockSpec((1,) + shape, lambda j, *_: (jnp.minimum(j, half - 1), 0, 0, 0))
        far = pl.BlockSpec((1,) + shape, lambda j, *_: (jnp.maximum(j - half, 0), 0, 0, 0))
        out_specs = (near, far) * 2
        shapes = (jax.ShapeDtypeStruct((half,) + shape, BF16),) * 4
    return pl.pallas_call(
        functools.partial(weight_grads_kernel, dp, shard, tensor),
        grid_spec=pltpu.PrefetchScalarGridSpec(
            num_scalar_prefetch=1,
            grid=(tensor,),
            in_specs=[
                whole(rows, width),
                whole(rows, width),
                whole(rows, width),
                block(rows, hidden),
                block(rows, hidden),
            ]
            + [whole(rows, head_width)] * tensor,
            out_specs=out_specs,
            scratch_shapes=[pltpu.VMEM((width, rows), BF16)] * 3
            + [pltpu.VMEM((tensor, rows, head_width), BF16)],
        ),
        out_shape=shapes,
        compiler_params=pltpu.CompilerParams(vmem_limit_bytes=26 * MIB),
        cost_estimate=LIGHT,
        name="weight_grads",
    )(info, *far_off(x_low), two_low, one_low, upper_low, *far_off(act, *mixed))


def weights_to_owner(parts, dp, tensor, z):
    if len(parts) == 1:
        order = (z - jnp.arange(tensor)) % tensor
        whole_parts = jnp.take(parts[0], order, axis=0)
        owned = lax.psum_scatter(
            whole_parts.reshape(-1, whole_parts.shape[-1]), ("tensor", "dp"),
            scatter_dimension=0, tiled=True,
        ).astype(F32)

        def done(came, late):
            yield (), owned
            return owned

        return (), (), lambda sent: (), done
    keep, give = parts[:2], parts[2:]
    bits = bits_of(dp)
    got = [swapped(v, "dp", dp, bits[0]) for v in give]
    half = tensor // 2
    orders = (bits[1:], bits[1:][::-1])
    sent = []
    for side, order in enumerate(orders):
        value = split_by(keep[side], bits[1:], order[0], 1).astype(F32)
        value = value + split_by(got[side], bits[1:], order[0], 1).astype(F32)
        sent.append(value.astype(BF16))

    def first(sent):
        return [swapped(sent[k], "dp", dp, orders[k][0]) for k in range(2)]

    def finish(came, late):
        sent = None
        values, lefts = [], [list(bits[1:]), list(bits[1:])]
        for side, order in enumerate(orders):
            value = split_by(keep[side], bits[1:], order[0], 0).astype(F32)
            values.append(value + split_by(late[side], bits[1:], order[0], 0).astype(F32))
        for n in range(len(bits) - 1):
            if n:
                came = [swapped(sent[k], "dp", dp, orders[k][n]) for k in range(2)]
                came = yield sent, came
            sent = []
            for k in range(2):
                value = values[k] + came[k].astype(F32)
                lefts[k].remove(orders[k][n])
                if n + 2 < len(bits):
                    bit = orders[k][n + 1]
                    sent.append(split_by(value, lefts[k], bit, 1).astype(BF16))
                    value = split_by(value, lefts[k], bit, 0)
                values[k] = value
        own = [value[t, 0] for value in values for t in range(half)]
        total = own[1]
        for t in list(range(2, tensor)) + [0]:
            total = total.astype(BF16)
            came = yield total, shifted(total, "tensor", tensor, 1)
            total = own[t] + came.astype(F32)
        return total

    return sent, got, first, finish


def split_by(value, left, bit, side):
    shape = value.shape
    place = left.index(bit)
    low, high = 1 << place, 1 << (len(left) - 1 - place)
    pairs = value.reshape(shape[0], high, 2, low, *shape[2:])
    return pairs[:, :, side].reshape(shape[0], high * low, *shape[2:])


def first_rows_kernel(d_ref, w_ref, out_ref):
    out_ref[...] = dot_nt(d_ref[0], w_ref[...]).astype(BF16)


def first_rows(d_chunks, w_in):
    _, rows, width = d_chunks.shape
    return pl.pallas_call(
        first_rows_kernel,
        grid=(1,),
        out_shape=jax.ShapeDtypeStruct((rows, w_in.shape[0]), BF16),
        in_specs=[
            pl.BlockSpec((1, rows, width), lambda n: (1, 0, 0)),
            whole(*w_in.shape),
        ],
        out_specs=whole(rows, w_in.shape[0]),
        compiler_params=pltpu.CompilerParams(vmem_limit_bytes=12 * MIB),
        cost_estimate=LIGHT,
        name="first_rows",
    )(d_chunks, w_in)


def rest_rows_kernel(d_ref, w_ref, out_ref):
    out_ref[0] = dot_nt(d_ref[0], w_ref[...]).astype(BF16)


def rest_rows(d_chunks, w_in):
    tensor, rows, width = d_chunks.shape
    model = w_in.shape[0]
    return pl.pallas_call(
        rest_rows_kernel,
        grid=(tensor - 1,),
        out_shape=jax.ShapeDtypeStruct((tensor - 1, rows, model), BF16),
        in_specs=[
            pl.BlockSpec((1, rows, width), lambda n: (lax.rem(n + 2, tensor), 0, 0)),
            whole(*w_in.shape),
        ],
        out_specs=block(rows, model),
        compiler_params=pltpu.CompilerParams(vmem_limit_bytes=12 * MIB),
        cost_estimate=LIGHT,
        name="rest_rows",
    )(d_chunks, w_in)


def in_grad_kernel(tensor, d_ref, *refs):
    seq_refs, grad_ref = refs[:tensor], refs[tensor]
    n = pl.program_id(0)
    for t in range(tensor):

        @pl.when(n == t)
        def _():
            part = dot_tn(seq_refs[t][...], d_ref[0])
            if t == 0:
                grad_ref[...] = part
            else:
                grad_ref[...] += part


def in_grad(d_chunks, seq_rows):
    tensor, rows, width = d_chunks.shape
    model = seq_rows[0].shape[1]
    return pl.pallas_call(
        functools.partial(in_grad_kernel, tensor),
        grid=(tensor,),
        out_shape=jax.ShapeDtypeStruct((model, width), F32),
        in_specs=[block(rows, width)] + [whole(rows, model)] * tensor,
        out_specs=whole(model, width),
        compiler_params=pltpu.CompilerParams(vmem_limit_bytes=16 * MIB),
        cost_estimate=HEAVY,
        name="in_grad",
    )(d_chunks, *seq_rows)


def per_device(
    dp, tensor, tokens, cotangent, labels, piece_start, piece_len, w_qkv, w_out, w_up, w_down,
    vec_table, ff_bias, cls_proj, cls_vec, cls_hidden, cls_out, cls_bias,
):
    rows, width = tokens.shape
    local = w_qkv.shape[2]
    heads = local // HEAD_DIM
    padded = -(-local // LANES) * LANES
    shard = w_qkv.shape[0]
    hidden = w_up.shape[1]
    ch = cls_proj.shape[1]
    z = lax.axis_index("tensor")
    info = jnp.concatenate(
        [z.reshape(1), lax.axis_index("dp").reshape(1), labels, piece_start[0], piece_len[0]]
    ).astype(jnp.int32)

    extra = padded - local
    qkv_shard = jnp.pad(w_qkv, ((0, 0), (0, 0), (0, extra))).reshape(shard, 3 * padded)
    ff_ring, seq_rows = [], []
    ff_shard = jnp.concatenate([w_up, w_down.T, w_out.T], axis=1)
    _, _, w_in = in_turn(
        vec_table[0, 0],
        {
            "rows": ring_chain(tokens, tensor, seq_rows),
            "ff": ring_chain(ff_shard, tensor, ff_ring),
            "in": gather_chain(qkv_shard, "dp", dp),
        },
        [("in",), ("in", "ff"), ("in",), ("ff",), ("rows",), ("ff",), ("rows",), ("rows",)],
    )
    half = tensor // 2
    pieces = [
        lax.all_gather(jnp.stack(ff_ring[n : n + half]), "dp") for n in (0, half)
    ]
    if shard % 16:
        pieces = [
            p.transpose(1, 0, 2, 3).reshape(1, half, dp * shard, p.shape[-1]) for p in pieces
        ]

    q_bias = lax.dynamic_slice_in_dim(vec_table[0], z * local, local, 0)
    v_bias = lax.dynamic_slice_in_dim(vec_table[1], z * local, local, 0)
    in_bias = jnp.pad(
        jnp.stack([q_bias, jnp.zeros_like(q_bias), v_bias]), ((0, 0), (0, extra))
    ).reshape(1, 3 * padded)

    def exchanged(parts):
        return [parts[0]] + [
            shifted(parts[tensor - s], "tensor", tensor, s) for s in range(1, tensor)
        ]

    chunks = [
        (jnp.dot(part, w_in, preferred_element_type=F32) + in_bias).astype(BF16)
        for part in seq_rows
    ]
    mixed, lse = attend_forward(info, chunks, heads)
    mixed_parts = exchanged(mixed)
    kept = rows_forward(
        info, pieces, mixed_parts, tokens, vec_table,
        ff_bias.reshape(tensor, 1, hidden), cls_proj, cls_vec,
    )
    out_low, x_low, act, _, _, _, _, _, _, stats = kept
    all_stats = exchanged([stats] * tensor)
    (
        logits, two_low, upper_low, one_low, grad_h_one, grad_mixed, small,
    ) = rows_backward(
        info, pieces, all_stats, kept, cotangent, vec_table, cls_proj, cls_vec,
        cls_hidden, jnp.pad(cls_out, ((0, 0), (0, ch - CLASSES))),
        jnp.pad(cls_bias, (0, ch - CLASSES)).reshape(1, ch),
    )
    grad_rows = exchanged(grad_mixed)
    bits = bits_of(tensor)
    small_came = swapped(small, "tensor", tensor, bits[0])
    ff_parts = weight_grads(
        info, dp, shard, x_low, two_low, one_low, upper_low, act, mixed_parts
    )
    ff_parts, grad_rows[1], small_came = lax.optimization_barrier(
        (ff_parts, grad_rows[1], small_came)
    )
    sent, got, first, finish = weights_to_owner(ff_parts, dp, tensor, z)
    small = small + small_came
    sent, small, grad_rows = lax.optimization_barrier((sent, small, grad_rows))
    small_came = swapped(small, "tensor", tensor, bits[1])

    d_chunks, bias_sums = attend_backward(info, chunks, grad_rows, mixed, lse, heads)
    d_chunks, bias_sums, came, late, small_came = lax.optimization_barrier(
        (d_chunks, bias_sums, first(sent), got, small_came)
    )
    first_part = first_rows(d_chunks, w_in)
    came, late = after((came, late), first_part)

    def small_chain():
        total = small + small_came
        for bit in bits[2:]:
            got = yield total, swapped(total, "tensor", tensor, bit)
            total = total + got
        for bit in bits_of(dp):
            got = yield total, swapped(total, "dp", dp, bit)
            total = total + got
        return total.astype(F32)

    def rows_chain():
        came = shifted(first_part, "tensor", tensor, 1)
        later = yield first_part, d_chunks
        rest = rest_rows(later, w_in)
        total = first_part
        for t in range(2, tensor):
            came = yield (total, rest), came
            total = (rest[t - 2].astype(F32) + came.astype(F32)).astype(BF16)
            came = shifted(total, "tensor", tensor, 1)
        came = yield total, came
        return grad_h_one + rest[tensor - 2].astype(F32) + came.astype(F32)

    def in_chain():
        later = yield (), d_chunks
        grad = in_grad(later, seq_rows)
        grad = yield (), grad
        rider = jnp.pad(bias_sums, ((0, 8), (0, 2 * padded)))
        return (
            yield from owner_chain(
                grad.reshape(dp, shard, 3 * padded), rider, "dp", dp, "tensor", tensor
            )
        )

    grad_tokens, ff_own, (grad_in, riders), sums = in_turn(
        bias_sums[0, 0],
        {
            "rows": rows_chain(),
            "ff": finish(came, late),
            "in": in_chain(),
            "small": small_chain(),
        },
        [
            ("rows",), ("rows",), ("ff",), ("in",), ("in",), ("small",), ("rows",), ("in",),
            ("small",), ("ff",), ("in",), ("small",), ("in",), ("ff",), ("in",), ("rows",),
            ("ff",),
        ],
    )
    grad_w_qkv = grad_in.reshape(shard, 3, padded)[:, :, :local]
    bias_sum = riders[:, :2, :local].transpose(1, 0, 2).reshape(2, width)

    proj_sum, pack_sum = sums[:width], sums[width:]
    hid_sum = pack_sum[8 : 8 + ch]
    out_w_sum = pack_sum[8 + ch : 8 + 2 * ch, :CLASSES]
    at = 8 + 2 * ch
    vec_sum = pack_sum[at : at + 6 * width // ch].reshape(6, width)
    ff_bias_sum = pack_sum[at + 6 * width // ch :].reshape(-1)
    return (
        out_low,
        logits[0:1, :CLASSES],
        grad_tokens,
        grad_w_qkv,
        ff_own[:, 2 * hidden :].T,
        ff_own[:, :hidden],
        ff_own[:, hidden : 2 * hidden].T,
        jnp.concatenate([bias_sum, vec_sum], axis=0),
        ff_bias_sum,
        proj_sum,
        pack_sum[:3],
        hid_sum,
        out_w_sum,
        pack_sum[3, :CLASSES],
    )


def solution(mesh):
    dp, tensor = mesh.shape["dp"], mesh.shape["tensor"]
    rows = P(("dp", "tensor"), None)
    cut = P("dp", "tensor")
    turned_cut = P("tensor", "dp")
    return jax.shard_map(
        functools.partial(per_device, dp, tensor),
        mesh=mesh,
        in_specs=(
            rows, rows, P("dp"), P("dp", None), P("dp", None), P("dp", None, "tensor"),
            turned_cut, cut, turned_cut, P(), P(), P(), P(), P(), P(), P(),
        ),
        out_specs=(
            rows, P("dp", None), rows, P("dp", None, "tensor"), turned_cut, cut, turned_cut,
            P(), P(), P(), P(), P(), P(), P(),
        ),
        check_vma=False,
    )
```

```python
import functools

import jax
import jax.numpy as jnp
from jax import lax
from jax.experimental import pallas as pl
from jax.experimental.pallas import tpu as pltpu
from jax.sharding import PartitionSpec as P

HEAD_DIM = 64
CLASSES = 14
PIECE_BLOCK = 256
POOL_HEADS = 2
LANES = 128
NORM_EPS = 1e-05
MASK_FILL = -1e30
PRECISE = lax.Precision.HIGHEST
F32 = jnp.float32
BF16 = jnp.bfloat16
MIB = 1024 * 1024
LIGHT = pl.CostEstimate(flops=1024, bytes_accessed=1024, transcendentals=0)
HEAVY = pl.CostEstimate(flops=4 * 10**10, bytes_accessed=1024, transcendentals=0)


def dot_nn(a, b, precision=None):
    return lax.dot_general(
        a, b, (((1,), (0,)), ((), ())), preferred_element_type=F32, precision=precision
    )


def dot_nt(a, b, precision=None):
    return lax.dot_general(
        a, b, (((1,), (1,)), ((), ())), preferred_element_type=F32, precision=precision
    )


def dot_tn(a, b, precision=None):
    return lax.dot_general(
        a, b, (((0,), (0,)), ((), ())), preferred_element_type=F32, precision=precision
    )


def bits_of(size):
    return [1 << n for n in range(size.bit_length() - 1)]


def swapped(value, axis, size, bit):
    return lax.ppermute(value, axis, [(i, i ^ bit) for i in range(size)])


def shifted(value, axis, size, by):
    return lax.ppermute(value, axis, [(i, (i + by) % size) for i in range(size)])


def after(value, *others):
    return lax.optimization_barrier((value, others))[0]


def in_turn(mark, chains, turns):
    under_way, results = {}, {}

    def advance(name, value):
        try:
            under_way[name] = chains[name].send(value)
        except StopIteration as end:
            under_way.pop(name, None)
            results[name] = end.value

    for name in chains:
        advance(name, None)
    turns = list(turns)
    while under_way:
        turn = turns.pop(0) if turns else tuple(under_way)
        names = [name for name in turn if name in under_way]
        if not names:
            continue
        sent = [value for value, _ in under_way.values()]
        there, mark, _ = lax.optimization_barrier(
            ([under_way[name][1] for name in names], mark, sent)
        )
        for name, value in zip(names, there):
            advance(name, value)
    return [results[name] for name in chains]


def ring_chain(value, size, kept):
    kept.append(value)
    for _ in range(size - 1):
        value = yield value, shifted(value, "tensor", size, 1)
        kept.append(value)
    return kept


def gather_chain(value, axis, size):
    index = lax.axis_index(axis)
    for bit in bits_of(size):
        other = yield value, swapped(value, axis, size, bit)
        low = (index // bit) % 2 == 0
        value = jnp.where(
            low, jnp.concatenate([value, other], 0), jnp.concatenate([other, value], 0)
        )
    return value


def owner_chain(parts, rider, axis, size, other, other_size):
    index = lax.axis_index(axis)
    riding = rider.shape[0]
    for bit in bits_of(size):
        mine = (index // bit) % 2
        count, rows, columns = parts.shape
        pairs = parts.reshape(count // 2, 2, rows, columns)
        keep = lax.dynamic_index_in_dim(pairs, mine, 1, keepdims=False)
        give = lax.dynamic_index_in_dim(pairs, 1 - mine, 1, keepdims=False)
        give = give.reshape(count // 2 * rows, columns)
        give = jnp.concatenate([give, rider]).astype(BF16)
        got = yield give, swapped(give, axis, size, bit)
        parts = keep + got[:-riding].reshape(keep.shape).astype(F32)
        rider = rider.astype(BF16).astype(F32) + got[-riding:].astype(F32)
    rider = rider[:2]
    got = yield rider, [shifted(rider, other, other_size, by) for by in range(1, other_size)]
    index = lax.axis_index(other)
    places = jnp.arange(other_size)[:, None, None]
    riders = 0.0
    for by, value in enumerate([rider] + list(got)):
        mine = places == (index - by) % other_size
        riders = riders + jnp.where(mine, value[None], 0.0)
    return parts[0], riders


def far_off(*values):
    return [pltpu.with_memory_space_constraint(v, pltpu.HBM) for v in values]


INFO_Z, INFO_D, INFO_LABEL, INFO_PIECES = 0, 1, 2, 3


def part_of(info_ref, place, tensor):
    return lax.rem(info_ref[INFO_Z] - place + tensor, tensor)


def block_range(info_ref, block):
    first, stop, inside_any = block, block + 1, jnp.int32(0)
    pieces = (info_ref.shape[0] - INFO_PIECES) // 2
    for piece in range(pieces):
        begin, count = info_ref[INFO_PIECES + piece], info_ref[INFO_PIECES + pieces + piece]
        inside = jnp.logical_and(block >= begin, block < begin + count)
        first = jnp.where(inside, begin, first)
        stop = jnp.where(inside, begin + count, stop)
        inside_any = jnp.where(inside, jnp.int32(1), inside_any)
    return first, stop, inside_any


def head_lanes(shape, head):
    lane = lax.broadcasted_iota(jnp.int32, shape, len(shape) - 1)
    return (lane >= head * HEAD_DIM) & (lane < (head + 1) * HEAD_DIM)


def attend_forward_kernel(heads, info_ref, *refs):
    tensor = len(refs) - 2 - 3
    chunks = refs[:tensor]
    o_ref, lse_ref = refs[tensor : tensor + 2]
    q_s, k_s, vt_s = refs[tensor + 2 :]
    rows, padded = chunks[0].shape[0], chunks[0].shape[1] // 3
    blk = PIECE_BLOCK
    blocks = tensor * rows // blk
    per_chunk = rows // blk
    scale = HEAD_DIM ** (-0.5)
    for t in range(tensor):
        quarter = part_of(info_ref, t, tensor)

        def one_block(part, carry):
            b = quarter * per_chunk + part
            here = pl.ds(part * blk, blk)
            q = chunks[t][here, 0:padded]
            for h in range(heads):
                q_s[h, b] = jnp.where(head_lanes(q.shape, h), q * scale, 0.0).astype(BF16)
            pair, at = b // 2, pl.multiple_of(lax.rem(b, 2) * blk, blk)
            k_s[pair, pl.ds(at, blk), :] = chunks[t][here, padded : 2 * padded]
            vt_s[pair, :, pl.ds(at, blk)] = chunks[t][here, 2 * padded : 3 * padded].T
            return carry

        lax.fori_loop(0, per_chunk, one_block, 0)


    def one_query(i, carry):
        _, stop, inside = block_range(info_ref, i)
        q_h = [q_s[h, i] for h in range(heads)]
        query = i * blk + lax.broadcasted_iota(jnp.int32, (1, blk), 1)
        limit = jnp.maximum(query, jnp.where(inside > 0, stop * blk - 1, 0))

        def step(j, state, masked):
            tops, totals, mixed = state
            keys = 2 * blk
            if masked:
                key = j * keys + lax.broadcasted_iota(jnp.int32, (keys, blk), 0)
                seen = key <= limit
            k_j = k_s[j]
            scores = [dot_nt(k_j, q_h[h]) for h in range(heads)]
            if masked:
                scores = [jnp.where(seen, s, MASK_FILL) for s in scores]
            new_tops = [
                jnp.maximum(tops[h], jnp.max(scores[h], axis=0, keepdims=True))
                for h in range(heads)
            ]
            ps = [jnp.exp(scores[h] - new_tops[h]) for h in range(heads)]
            fades = [jnp.exp(tops[h] - new_tops[h]) for h in range(heads)]
            new_totals = [
                totals[h] * fades[h] + jnp.sum(ps[h], axis=0, keepdims=True) for h in range(heads)
            ]
            new_mixed = [
                mixed[h] * fades[h]
                + dot_nn(vt_s[j, h * HEAD_DIM : (h + 1) * HEAD_DIM, :], ps[h].astype(BF16))
                for h in range(heads)
            ]
            return tuple(new_tops), tuple(new_totals), tuple(new_mixed)

        state = (
            tuple(jnp.full((1, blk), MASK_FILL, F32) for _ in range(heads)),
            tuple(jnp.zeros((1, blk), F32) for _ in range(heads)),
            tuple(jnp.zeros((HEAD_DIM, blk), F32) for _ in range(heads)),
        )
        last = i // 2
        state = lax.fori_loop(0, last, lambda j, c: step(j, c, False), state)
        tops, totals, mixed = lax.fori_loop(
            last, (stop + 1) // 2, lambda j, c: step(j, c, True), state
        )
        outs = [mixed[h] * (1.0 / totals[h]) for h in range(heads)]
        lses = [tops[h] + jnp.log(totals[h]) for h in range(heads)]
        t = part_of(info_ref, i // per_chunk, tensor)
        here = pl.ds(lax.rem(i, per_chunk) * blk, blk)
        o_ref[t, here, :] = jnp.concatenate(outs, axis=0).T.astype(BF16)
        lse_ref[i] = jnp.concatenate(lses + [jnp.zeros((8 - heads, blk), F32)], axis=0)
        return carry

    lax.fori_loop(0, blocks, one_query, 0)


def attend_forward(info, chunks, heads):
    tensor = len(chunks)
    rows, width = chunks[0].shape
    padded = width // 3
    seq, blk = tensor * rows, PIECE_BLOCK
    blocks = seq // blk
    smem = pl.BlockSpec(memory_space=pltpu.SMEM)
    vmem = pl.BlockSpec(memory_space=pltpu.VMEM)
    return pl.pallas_call(
        functools.partial(attend_forward_kernel, heads),
        out_shape=(
            jax.ShapeDtypeStruct((tensor, rows, heads * HEAD_DIM), BF16),
            jax.ShapeDtypeStruct((blocks, 8, blk), F32),
        ),
        in_specs=[smem] + [vmem] * tensor,
        out_specs=(vmem, vmem),
        scratch_shapes=[
            pltpu.VMEM((heads, blocks, blk, padded), BF16),
            pltpu.VMEM((blocks // 2, 2 * blk, padded), BF16),
            pltpu.VMEM((blocks // 2, padded, 2 * blk), BF16),
        ],
        compiler_params=pltpu.CompilerParams(vmem_limit_bytes=24 * MIB),
        cost_estimate=LIGHT,
        name="attend_forward",
    )(info, *chunks)


def attend_backward_kernel(heads, info_ref, *refs):
    tensor = (len(refs) - 2 - 2 - 9) // 2
    chunks, grads = refs[:tensor], refs[tensor : 2 * tensor]
    o_ref, lse_ref, dqkv_ref, bias_ref = refs[2 * tensor : 2 * tensor + 4]
    q_s, k_s, kt_s, v_s, g_s, delta_s, dqt_s, dk_s, dv_s = refs[2 * tensor + 4 :]
    rows, padded = chunks[0].shape[0], chunks[0].shape[1] // 3
    width = heads * HEAD_DIM
    blk = PIECE_BLOCK
    blocks = tensor * rows // blk
    per_chunk = rows // blk
    scale = HEAD_DIM ** (-0.5)
    for t in range(tensor):
        quarter = part_of(info_ref, t, tensor)

        def one_block(part, carry):
            b = quarter * per_chunk + part
            here = pl.ds(part * blk, blk)
            q = chunks[t][here, 0:padded]
            g = grads[t][here, :]
            for h in range(heads):
                q_s[h, b] = jnp.where(head_lanes(q.shape, h), q * scale, 0.0).astype(BF16)
                g_s[h, b, :, 0:width] = jnp.where(head_lanes(g.shape, h), g, 0.0).astype(BF16)
                if padded > width:
                    g_s[h, b, :, width:padded] = jnp.zeros((blk, padded - width), BF16)
            k = chunks[t][here, padded : 2 * padded]
            pair, at = b // 2, pl.multiple_of(lax.rem(b, 2) * blk, blk)
            k_s[pair, pl.ds(at, blk), :] = k
            v_s[pair, pl.ds(at, blk), :] = chunks[t][here, 2 * padded : 3 * padded]
            kt_s[pair, :, pl.ds(at, blk)] = k.T
            prod = (g.astype(F32) * o_ref[t, here, :].astype(F32)).T
            sums = [
                jnp.sum(prod[h * HEAD_DIM : (h + 1) * HEAD_DIM, :], axis=0, keepdims=True)
                for h in range(heads)
            ]
            delta_s[b] = jnp.concatenate(sums + [jnp.zeros((8 - heads, blk), F32)], axis=0)
            dqt_s[b] = jnp.zeros((padded, blk), F32)
            return carry

        lax.fori_loop(0, per_chunk, one_block, 0)
    bias_ref[...] = jnp.zeros_like(bias_ref)

    keys = 2 * blk

    def one_pair(j, carry):
        first, _, _ = block_range(info_ref, 2 * j)
        also, _, _ = block_range(info_ref, 2 * j + 1)
        dk_s[...] = jnp.zeros_like(dk_s)
        dv_s[...] = jnp.zeros_like(dv_s)

        def step(i, masked):
            lse, delta = lse_ref[i], delta_s[i]
            if masked:
                _, stop, inside = block_range(info_ref, i)
                query = i * blk + lax.broadcasted_iota(jnp.int32, (1, blk), 1)
                limit = jnp.maximum(query, jnp.where(inside > 0, stop * blk - 1, 0))
                key = j * keys + lax.broadcasted_iota(jnp.int32, (keys, blk), 0)
                seen = key <= limit
            k_j, v_j = k_s[j], v_s[j]
            q_h = [q_s[h, i] for h in range(heads)]
            g_h = [g_s[h, i] for h in range(heads)]
            lows, ds = [], []
            for h in range(heads):
                p = jnp.exp(dot_nt(k_j, q_h[h]) - lse[h : h + 1, :])
                dp = dot_nt(v_j, g_h[h])
                if masked:
                    p = jnp.where(seen, p, 0.0)
                lows.append(p.astype(BF16))
                ds.append((p * (dp - delta[h : h + 1, :])).astype(BF16))
            dv_s[...] += dot_nn(jnp.concatenate(lows, axis=1), jnp.concatenate(g_h, axis=0))
            dk_s[...] += dot_nn(jnp.concatenate(ds, axis=1), jnp.concatenate(q_h, axis=0))
            for h in range(heads):
                lo, hi = h * HEAD_DIM, (h + 1) * HEAD_DIM
                dqt_s[i, lo:hi, :] += dot_nn(kt_s[j, lo:hi, :], ds[h])

        def masked_step(i, c):
            step(i, True)
            return c

        def open_step(i, c):
            step(i, False)
            return c

        lax.fori_loop(jnp.minimum(first, also), 2 * j + 2, masked_step, 0)
        lax.fori_loop(2 * j + 2, blocks, open_step, 0)
        for part in range(2):
            b = 2 * j + part
            t = part_of(info_ref, b // per_chunk, tensor)
            here = pl.ds(lax.rem(b, per_chunk) * blk, blk)
            side = slice(part * blk, (part + 1) * blk)
            dqkv_ref[t, here, padded : 2 * padded] = dk_s[side, :].astype(BF16)
            dqkv_ref[t, here, 2 * padded : 3 * padded] = dv_s[side, :].astype(BF16)
        bias_ref[1:2, :] = bias_ref[1:2, :] + jnp.sum(dv_s[...], axis=0, keepdims=True)
        return carry

    lax.fori_loop(0, blocks // 2, one_pair, 0)

    def one_query(i, carry):
        dq = dqt_s[i].T * scale
        t = part_of(info_ref, i // per_chunk, tensor)
        here = pl.ds(lax.rem(i, per_chunk) * blk, blk)
        dqkv_ref[t, here, 0:padded] = dq.astype(BF16)
        bias_ref[0:1, :] = bias_ref[0:1, :] + jnp.sum(dq, axis=0, keepdims=True)
        return carry

    lax.fori_loop(0, blocks, one_query, 0)


def attend_backward(info, chunks, grads, mixed, lse, heads):
    tensor = len(chunks)
    rows, width = chunks[0].shape
    padded = width // 3
    seq, blk = tensor * rows, PIECE_BLOCK
    blocks = seq // blk
    smem = pl.BlockSpec(memory_space=pltpu.SMEM)
    vmem = pl.BlockSpec(memory_space=pltpu.VMEM)
    return pl.pallas_call(
        functools.partial(attend_backward_kernel, heads),
        out_shape=(
            jax.ShapeDtypeStruct((tensor, rows, width), BF16),
            jax.ShapeDtypeStruct((8, padded), F32),
        ),
        in_specs=[smem] + [vmem] * (2 * tensor + 2),
        out_specs=(vmem, vmem),
        scratch_shapes=[
            pltpu.VMEM((heads, blocks, blk, padded), BF16),
            pltpu.VMEM((blocks // 2, 2 * blk, padded), BF16),
            pltpu.VMEM((blocks // 2, padded, 2 * blk), BF16),
            pltpu.VMEM((blocks // 2, 2 * blk, padded), BF16),
            pltpu.VMEM((heads, blocks, blk, padded), BF16),
            pltpu.VMEM((blocks, 8, blk), F32),
            pltpu.VMEM((blocks, padded, blk), F32),
            pltpu.VMEM((2 * blk, padded), F32),
            pltpu.VMEM((2 * blk, padded), F32),
        ],
        compiler_params=pltpu.CompilerParams(vmem_limit_bytes=34 * MIB),
        cost_estimate=LIGHT,
        name="attend_backward",
    )(info, *far_off(*chunks, *grads, mixed, lse))


def start_weights(pieces, w_s, wo_s, sems, o_sem):
    wide = w_s.shape[2]
    copies = []
    t = 0
    for piece in pieces:
        blocks, parts, rows, _ = piece.shape
        for part in range(parts):
            for n in range(blocks):
                copies.append((piece.at[n, part], t, pl.ds(n * rows, rows)))
            t += 1
    for source, t, here in copies:
        pltpu.make_async_copy(source.at[:, wide:], wo_s.at[t, here, :], o_sem).start()
    for source, t, here in copies:
        pltpu.make_async_copy(source.at[:, :wide], w_s.at[t, here, :], sems.at[t]).start()


def center(values):
    mean = jnp.mean(values, axis=-1, keepdims=True)
    centered = values - mean
    spread = jnp.mean(centered * centered, axis=-1, keepdims=True)
    return centered, lax.rsqrt(spread + NORM_EPS)


def same_head(value):
    row = lax.broadcasted_iota(jnp.int32, (value, value), 0) // (value // POOL_HEADS)
    col = lax.broadcasted_iota(jnp.int32, (value, value), 1) // (value // POOL_HEADS)
    return (row == col).astype(F32)


def rows_forward_kernel(tensor, arrays, info_ref, *refs):
    mixed = refs[:tensor]
    tok_ref, vec_ref, bias_ref, proj_ref, cvec_ref = refs[tensor : tensor + 5]
    pieces = refs[tensor + 5 : tensor + 5 + arrays]
    (
        low_ref, xlow_ref, act_ref, slope_ref, xh1_ref, xh2_ref, rs_ref, stud_ref, e_ref,
        stats_ref, acc_s, w_s, wo_s, sems, o_sem,
    ) = refs[tensor + 5 + arrays :]
    j = pl.program_id(0)
    hidden = act_ref.shape[2]
    rows = tok_ref.shape[0]
    half = min(256, rows)

    @pl.when(j == 0)
    def _():
        start_weights(pieces, w_s, wo_s, sems, o_sem)
        pltpu.make_async_copy(wo_s, wo_s, o_sem).wait()

        def first_part(n, carry):
            here = pl.ds(n * half, half)
            total = tok_ref[here, :].astype(F32) + vec_ref[2:3, :]
            for s in range(tensor):
                total = total + dot_nt(mixed[s][here, :], wo_s[s])
            centered, rstd = center(total)
            xhat = centered * rstd
            xh1_ref[here, :] = xhat
            rs_ref[here, 0:1] = rstd
            x_one = xhat * vec_ref[3:4, :] + vec_ref[4:5, :]
            xlow_ref[here, :] = x_one.astype(BF16)
            acc_s[here, :] = x_one + vec_ref[5:6, :]
            return carry

        lax.fori_loop(0, rows // half, first_part, 0)

    pltpu.make_async_copy(w_s.at[j], w_s.at[j], sems.at[j]).wait()

    def rows_part(n, carry):
        here = pl.ds(n * half, half)
        upper = dot_nn(xlow_ref[here, :], w_s[j, :, 0:hidden]) + bias_ref[0]
        phi = 0.5 * (1.0 + lax.erf(upper * (0.5**0.5)))
        act = (upper * phi).astype(BF16)
        slope = phi + upper * (jnp.exp(-0.5 * upper * upper) * 0.3989422804014327)
        act_ref[0, here, :] = act
        slope_ref[0, here, :] = slope.astype(BF16)
        acc_s[here, :] = acc_s[here, :] + dot_nt(act, w_s[j, :, hidden:])
        return carry

    lax.fori_loop(0, rows // half, rows_part, 0)

    @pl.when(j == pl.num_programs(0) - 1)
    def _():
        def last_part(n, carry):
            here = pl.ds(n * half, half)
            centered, rstd = center(acc_s[here, :])
            xhat = centered * rstd
            xh2_ref[here, :] = xhat
            rs_ref[here, 1:2] = rstd
            low = (xhat * vec_ref[6:7, :] + vec_ref[7:8, :]).astype(BF16)
            low_ref[here, :] = low
            stud_ref[here, :] = dot_nn(low, proj_ref[...]) + cvec_ref[0:1, :]
            return carry

        lax.fori_loop(0, rows // half, last_part, 0)
        student = stud_ref[...]
        width = student.shape[1]
        scale = (width // POOL_HEADS) ** (-0.5)
        e = dot_nn(student * (cvec_ref[1:2, :] * scale), same_head(width), PRECISE)
        e_ref[...] = e
        top = jnp.max(e, axis=0, keepdims=True)
        w = jnp.exp(e - top)
        stats_ref[...] = jnp.concatenate(
            [
                top,
                jnp.sum(w, axis=0, keepdims=True),
                jnp.sum(w * student, axis=0, keepdims=True),
                jnp.zeros((5, width), F32),
            ],
            axis=0,
        )


def whole(*shape):
    return pl.BlockSpec(shape, lambda j, *_: (0,) * len(shape))


def block(*shape):
    return pl.BlockSpec((1,) + shape, lambda j, *_: (j,) + (0,) * len(shape))


def rows_forward(info, pieces, mixed, tokens, vec_table, ff_bias, cls_proj, cls_vec):
    tensor = len(mixed)
    rows, width = tokens.shape
    head_width = mixed[0].shape[1]
    hidden = ff_bias.shape[2]
    ch = cls_proj.shape[1]
    far = pl.BlockSpec(memory_space=pl.ANY)

    def of_block(j, info_ref):
        return (part_of(info_ref, j, tensor), 0, 0)

    return pl.pallas_call(
        functools.partial(rows_forward_kernel, tensor, len(pieces)),
        grid_spec=pltpu.PrefetchScalarGridSpec(
            num_scalar_prefetch=1,
            grid=(tensor,),
            in_specs=[whole(rows, head_width)] * tensor
            + [
                whole(rows, width),
                whole(8, width),
                pl.BlockSpec((1, 1, hidden), of_block),
                whole(width, ch),
                whole(3, ch),
            ]
            + [far] * len(pieces),
            out_specs=(
                whole(rows, width),
                whole(rows, width),
                block(rows, hidden),
                block(rows, hidden),
                whole(rows, width),
                whole(rows, width),
                whole(rows, 2),
                whole(rows, ch),
                whole(rows, ch),
                whole(8, ch),
            ),
            scratch_shapes=[
                pltpu.VMEM((rows, width), F32),
                pltpu.VMEM((tensor, width, 2 * hidden), BF16),
                pltpu.VMEM((tensor, width, head_width), BF16),
                pltpu.SemaphoreType.DMA((tensor,)),
                pltpu.SemaphoreType.DMA,
            ],
        ),
        out_shape=(
            pltpu.HBM((rows, width), BF16),
            pltpu.HBM((rows, width), BF16),
            pltpu.HBM((tensor, rows, hidden), BF16),
            pltpu.HBM((tensor, rows, hidden), BF16),
            pltpu.HBM((rows, width), F32),
            pltpu.HBM((rows, width), F32),
            pltpu.HBM((rows, 2), F32),
            pltpu.HBM((rows, ch), F32),
            pltpu.HBM((rows, ch), F32),
            jax.ShapeDtypeStruct((8, ch), F32),
        ),
        compiler_params=pltpu.CompilerParams(vmem_limit_bytes=34 * MIB),
        cost_estimate=LIGHT,
        name="rows_forward",
    )(info, *far_off(*mixed, tokens), vec_table, ff_bias, cls_proj, cls_vec,
      *far_off(*pieces))


def norm_back(grad, xhat, rstd, gain):
    g = grad * gain
    return (
        g - jnp.mean(g, axis=-1, keepdims=True) - xhat * jnp.mean(g * xhat, axis=-1, keepdims=True)
    ) * rstd


def rows_backward_kernel(tensor, arrays, info_ref, *refs):
    stats_refs = refs[:tensor]
    (
        stud_ref, e_ref, cot_ref, xh1_ref, xh2_ref, rs_ref, slope_ref, vec_ref, proj_ref,
        cvec_ref, chid_ref, cout_ref, cbias_ref, outlow_ref,
    ) = refs[tensor : tensor + 14]
    pieces = refs[tensor + 14 : tensor + 14 + arrays]
    (
        logit_ref, two_ref, gu_ref, one_ref, gh1_ref, gm_ref, small_ref, acc_s, pack_ref, gsl_s,
        w_s, wo_s, sems, o_sem,
    ) = refs[tensor + 14 + arrays :]
    j = pl.program_id(0)
    ch = stud_ref.shape[1]
    hidden = gu_ref.shape[2]
    scale = (ch // POOL_HEADS) ** (-0.5)
    rows, width = cot_ref.shape
    half = min(256, rows)
    sums_at = 8 + 2 * ch
    bias_at = sums_at + 6 * (width // ch)

    def pack_row(row, value):
        at = sums_at + (row - 2) * (width // ch)
        for n in range(width // ch):
            pack_ref[at + n : at + n + 1, :] = value[:, n * ch : (n + 1) * ch]

    @pl.when(j == 0)
    def _():
        start_weights(pieces, w_s, wo_s, sems, o_sem)
        head_of = same_head(ch)
        first = (info_ref[INFO_Z] == 0).astype(F32)
        stats = [r[...] for r in stats_refs]
        top = functools.reduce(jnp.maximum, [v[0:1, :] for v in stats])
        weights = [jnp.exp(v[0:1, :] - top) for v in stats]
        total = sum(v[1:2, :] * w for v, w in zip(stats, weights))
        pooled = sum(v[2:3, :] * w for v, w in zip(stats, weights)) / total

        first_row = lax.broadcasted_iota(jnp.int32, (8, ch), 0) == 0
        lane = lax.broadcasted_iota(jnp.int32, (8, ch), 1)
        pooled8 = jnp.broadcast_to(pooled, (8, ch))
        chid = chid_ref[...].astype(F32)
        cout = cout_ref[...].astype(F32)
        hid = jnp.tanh(dot_nn(pooled8, chid, PRECISE) + cvec_ref[2:3, :])
        logits = dot_nn(hid, cout, PRECISE) + cbias_ref[...]
        logit_ref[...] = logits
        real = lane < CLASSES
        masked = jnp.where(real, logits, MASK_FILL)
        powers = jnp.where(real, jnp.exp(masked - jnp.max(masked, axis=1, keepdims=True)), 0.0)
        probs = powers / jnp.sum(powers, axis=1, keepdims=True)
        grad_logits = probs - (lane == info_ref[INFO_LABEL]).astype(F32)
        grad_pre = (1.0 - hid * hid) * dot_nt(grad_logits, cout, PRECISE)
        grad_pooled = dot_nt(grad_pre, chid, PRECISE)
        gl_row = jnp.where(first_row, grad_logits, 0.0) * first
        gp_row = jnp.where(first_row, grad_pre, 0.0) * first
        pack_ref[8 : 8 + ch, :] = dot_tn(pooled8, gp_row, PRECISE)
        pack_ref[8 + ch : 8 + 2 * ch, :] = dot_tn(hid, gl_row, PRECISE)
        base = dot_nn(grad_pooled * pooled8, head_of, PRECISE)[0:1, :]
        gp = grad_pooled[0:1, :]
        query = cvec_ref[1:2, :] * scale
        student = stud_ref[...]
        w = jnp.exp(e_ref[...] - top) / total
        grad_w = dot_nn(student * gp, head_of, PRECISE)
        grad_e = w * (grad_w - base)
        grad_student = w * gp + grad_e * query
        gsl = grad_student.astype(BF16)
        small_ref[0:width, :] = dot_tn(outlow_ref[...], gsl).astype(BF16)
        pack_ref[0:8, :] = jnp.concatenate(
            [
                jnp.sum(grad_student, axis=0, keepdims=True),
                jnp.sum(grad_e * student, axis=0, keepdims=True) * scale,
                gp_row[0:1, :],
                gl_row[0:1, :],
                jnp.zeros((4, ch), F32),
            ],
            axis=0,
        )
        gsl_s[...] = gsl

        def first_part(n, sums):
            here = pl.ds(n * half, half)
            grad = cot_ref[here, :].astype(F32) + dot_nt(gsl_s[here, :], proj_ref[...])
            xhat = xh2_ref[here, :]
            two = norm_back(grad, xhat, rs_ref[here, 1:2], vec_ref[6:7, :])
            acc_s[here, :] = two
            two_ref[here, :] = two.astype(BF16)
            parts = (two, grad * xhat, grad)
            return tuple(s + jnp.sum(v, axis=0, keepdims=True) for s, v in zip(sums, parts))

        sums = lax.fori_loop(0, rows // half, first_part, (jnp.zeros((1, width), F32),) * 3)
        for n in range(3):
            pack_row(5 + n, sums[n])

    pltpu.make_async_copy(w_s.at[j], w_s.at[j], sems.at[j]).wait()
    heads_row = part_of(info_ref, j, tensor)

    def rows_part(n, bias_row):
        here = pl.ds(n * half, half)
        upper = dot_nn(two_ref[here, :], w_s[j, :, hidden:]) * slope_ref[0, here, :].astype(F32)
        low = upper.astype(BF16)
        gu_ref[0, here, :] = low
        acc_s[here, :] = acc_s[here, :] + dot_nt(low, w_s[j, :, 0:hidden])
        return bias_row + jnp.sum(upper, axis=0, keepdims=True)

    bias_row = lax.fori_loop(
        0, rows // half, rows_part, jnp.zeros((1, hidden), F32)
    )
    for n in range(hidden // ch):
        pack_ref[pl.ds(bias_at + heads_row * (hidden // ch) + n, 1), :] = bias_row[
            :, n * ch : (n + 1) * ch
        ]

    @pl.when(j == pl.num_programs(0) - 1)
    def _():
        pltpu.make_async_copy(wo_s, wo_s, o_sem).wait()

        def last_part(n, sums):
            here = pl.ds(n * half, half)
            grad = acc_s[here, :]
            xhat = xh1_ref[here, :]
            one = norm_back(grad, xhat, rs_ref[here, 0:1], vec_ref[3:4, :])
            gh1_ref[here, :] = one
            low = one.astype(BF16)
            one_ref[here, :] = low
            for s in range(tensor):
                gm_ref[s, here, :] = dot_nn(low, wo_s[s]).astype(BF16)
            parts = (one, grad * xhat, grad)
            return tuple(s + jnp.sum(v, axis=0, keepdims=True) for s, v in zip(sums, parts))

        sums = lax.fori_loop(0, rows // half, last_part, (jnp.zeros((1, width), F32),) * 3)
        for n in range(3):
            pack_row(2 + n, sums[n])
        small_ref[width:, :] = pack_ref[...].astype(BF16)


def rows_backward(
    info, pieces, stats, kept, cotangent, vec_table, cls_proj, cls_vec, cls_hidden,
    cls_out, cls_bias,
):
    out_low, _, _, slope, xh1, xh2, rs, student, pool_logit, _ = kept
    tensor, rows, hidden = slope.shape
    width = xh1.shape[1]
    head_width = pieces[0].shape[3] - 2 * hidden
    ch = student.shape[1]
    far = pl.BlockSpec(memory_space=pl.ANY)
    pack_rows = 8 + 2 * ch + (6 * width + tensor * hidden) // ch

    return pl.pallas_call(
        functools.partial(rows_backward_kernel, tensor, len(pieces)),
        grid_spec=pltpu.PrefetchScalarGridSpec(
            num_scalar_prefetch=1,
            grid=(tensor,),
            in_specs=[whole(8, ch)] * tensor
            + [
                whole(rows, ch),
                whole(rows, ch),
                whole(rows, width),
                whole(rows, width),
                whole(rows, width),
                whole(rows, 2),
                block(rows, hidden),
                whole(8, width),
                whole(width, ch),
                whole(3, ch),
                whole(ch, ch),
                whole(ch, ch),
                whole(1, ch),
                whole(rows, width),
            ]
            + [far] * len(pieces),
            out_specs=(
                whole(8, ch),
                whole(rows, width),
                block(rows, hidden),
                whole(rows, width),
                whole(rows, width),
                whole(tensor, rows, head_width),
                whole(width + pack_rows, ch),
            ),
            scratch_shapes=[
                pltpu.VMEM((rows, width), F32),
                pltpu.VMEM((pack_rows, ch), F32),
                pltpu.VMEM((rows, ch), BF16),
                pltpu.VMEM((tensor, width, 2 * hidden), BF16),
                pltpu.VMEM((tensor, width, head_width), BF16),
                pltpu.SemaphoreType.DMA((tensor,)),
                pltpu.SemaphoreType.DMA,
            ],
        ),
        out_shape=(
            jax.ShapeDtypeStruct((8, ch), F32),
            jax.ShapeDtypeStruct((rows, width), BF16),
            jax.ShapeDtypeStruct((tensor, rows, hidden), BF16),
            jax.ShapeDtypeStruct((rows, width), BF16),
            jax.ShapeDtypeStruct((rows, width), F32),
            jax.ShapeDtypeStruct((tensor, rows, head_width), BF16),
            jax.ShapeDtypeStruct((width + pack_rows, ch), BF16),
        ),
        compiler_params=pltpu.CompilerParams(vmem_limit_bytes=34 * MIB),
        cost_estimate=LIGHT,
        name="rows_backward",
    )(
        info, *stats, *far_off(student, pool_logit, cotangent, xh1, xh2, rs, slope), vec_table,
        cls_proj, cls_vec, cls_hidden, cls_out, cls_bias, *far_off(out_low, *pieces),
    )


def weight_grads_kernel(dp, shard, tensor, info_ref, x_ref, two_ref, one_ref, gu_ref, act_ref, *refs):
    mixed, outs, lefts, mixed_s = refs[:tensor], refs[tensor:-4], refs[-4:-1], refs[-1]
    j = pl.program_id(0)
    hidden = gu_ref.shape[2]
    width = x_ref.shape[1]
    halves = 2 if len(outs) == 4 else 1

    @pl.when(j == 0)
    def _():
        for t in range(tensor):
            mixed_s[t] = mixed[t][...]
        for source, left in zip((x_ref, two_ref, one_ref), lefts):
            turned = source[...].T
            if halves == 1:
                left[...] = turned
                continue
            for b in range(dp):
                offset = jnp.bitwise_xor(info_ref[INFO_D], b)
                at = lax.rem(offset, 2) * (dp // 2) + offset // 2
                left[pl.ds(at * shard, shard), :] = turned[b * shard : (b + 1) * shard, :]

    count = width // halves
    rights = (gu_ref[0], act_ref[0], mixed_s[j])
    ends = (0, hidden, 2 * hidden, 2 * hidden + mixed_s.shape[2])

    def write(out, n):
        here = slice(n * count, (n + 1) * count)
        for m in range(3):
            part = dot_nn(lefts[m][here, :], rights[m]).astype(BF16)
            out[0, :, :, ends[m] : ends[m + 1]] = part.reshape(
                out.shape[1], out.shape[2], ends[m + 1] - ends[m]
            )

    if halves == 1:
        write(outs[0], 0)
    for side in range(halves if halves > 1 else 0):

        @pl.when((j < tensor // 2) if side == 0 else (j >= tensor // 2))
        def _():
            write(outs[side], 0)
            write(outs[2 + side], 1)


def weight_grads(info, dp, shard, x_low, two_low, one_low, upper_low, act, mixed):
    tensor, rows, hidden = upper_low.shape
    width = x_low.shape[1]
    head_width = mixed[0].shape[1]
    total = 2 * hidden + head_width
    half = tensor // 2
    if shard % 16:
        out_specs = (block(1, width, total),)
        shapes = (jax.ShapeDtypeStruct((tensor, 1, width, total), BF16),)
    else:
        shape = (dp // 2, shard, total)
        near = pl.BlockSpec((1,) + shape, lambda j, *_: (jnp.minimum(j, half - 1), 0, 0, 0))
        far = pl.BlockSpec((1,) + shape, lambda j, *_: (jnp.maximum(j - half, 0), 0, 0, 0))
        out_specs = (near, far) * 2
        shapes = (jax.ShapeDtypeStruct((half,) + shape, BF16),) * 4
    return pl.pallas_call(
        functools.partial(weight_grads_kernel, dp, shard, tensor),
        grid_spec=pltpu.PrefetchScalarGridSpec(
            num_scalar_prefetch=1,
            grid=(tensor,),
            in_specs=[
                whole(rows, width),
                whole(rows, width),
                whole(rows, width),
                block(rows, hidden),
                block(rows, hidden),
            ]
            + [whole(rows, head_width)] * tensor,
            out_specs=out_specs,
            scratch_shapes=[pltpu.VMEM((width, rows), BF16)] * 3
            + [pltpu.VMEM((tensor, rows, head_width), BF16)],
        ),
        out_shape=shapes,
        compiler_params=pltpu.CompilerParams(vmem_limit_bytes=26 * MIB),
        cost_estimate=LIGHT,
        name="weight_grads",
    )(info, *far_off(x_low), two_low, one_low, upper_low, *far_off(act, *mixed))


def weights_to_owner(parts, dp, tensor, z):
    if len(parts) == 1:
        order = (z - jnp.arange(tensor)) % tensor
        whole_parts = jnp.take(parts[0], order, axis=0)
        owned = lax.psum_scatter(
            whole_parts.reshape(-1, whole_parts.shape[-1]), ("tensor", "dp"),
            scatter_dimension=0, tiled=True,
        ).astype(F32)

        def done(came, late):
            yield (), owned
            return owned

        return (), (), lambda sent: (), done
    keep, give = parts[:2], parts[2:]
    bits = bits_of(dp)
    got = [swapped(v, "dp", dp, bits[0]) for v in give]
    half = tensor // 2
    orders = (bits[1:], bits[1:][::-1])
    sent = []
    for side, order in enumerate(orders):
        value = split_by(keep[side], bits[1:], order[0], 1).astype(F32)
        value = value + split_by(got[side], bits[1:], order[0], 1).astype(F32)
        sent.append(value.astype(BF16))

    def first(sent):
        return [swapped(sent[k], "dp", dp, orders[k][0]) for k in range(2)]

    def finish(came, late):
        sent = None
        values, lefts = [], [list(bits[1:]), list(bits[1:])]
        for side, order in enumerate(orders):
            value = split_by(keep[side], bits[1:], order[0], 0).astype(F32)
            values.append(value + split_by(late[side], bits[1:], order[0], 0).astype(F32))
        for n in range(len(bits) - 1):
            if n:
                came = [swapped(sent[k], "dp", dp, orders[k][n]) for k in range(2)]
                came = yield sent, came
            sent = []
            for k in range(2):
                value = values[k] + came[k].astype(F32)
                lefts[k].remove(orders[k][n])
                if n + 2 < len(bits):
                    bit = orders[k][n + 1]
                    sent.append(split_by(value, lefts[k], bit, 1).astype(BF16))
                    value = split_by(value, lefts[k], bit, 0)
                values[k] = value
        own = [value[t, 0] for value in values for t in range(half)]
        total = own[1]
        for t in list(range(2, tensor)) + [0]:
            total = total.astype(BF16)
            came = yield total, shifted(total, "tensor", tensor, 1)
            total = own[t] + came.astype(F32)
        return total

    return sent, got, first, finish


def split_by(value, left, bit, side):
    shape = value.shape
    place = left.index(bit)
    low, high = 1 << place, 1 << (len(left) - 1 - place)
    pairs = value.reshape(shape[0], high, 2, low, *shape[2:])
    return pairs[:, :, side].reshape(shape[0], high * low, *shape[2:])


def first_rows_kernel(d_ref, w_ref, out_ref):
    out_ref[...] = dot_nt(d_ref[0], w_ref[...]).astype(BF16)


def first_rows(d_chunks, w_in):
    _, rows, width = d_chunks.shape
    return pl.pallas_call(
        first_rows_kernel,
        grid=(1,),
        out_shape=jax.ShapeDtypeStruct((rows, w_in.shape[0]), BF16),
        in_specs=[
            pl.BlockSpec((1, rows, width), lambda n: (1, 0, 0)),
            whole(*w_in.shape),
        ],
        out_specs=whole(rows, w_in.shape[0]),
        compiler_params=pltpu.CompilerParams(vmem_limit_bytes=12 * MIB),
        cost_estimate=LIGHT,
        name="first_rows",
    )(d_chunks, w_in)


def rest_rows_kernel(d_ref, w_ref, out_ref):
    out_ref[0] = dot_nt(d_ref[0], w_ref[...]).astype(BF16)


def rest_rows(d_chunks, w_in):
    tensor, rows, width = d_chunks.shape
    model = w_in.shape[0]
    return pl.pallas_call(
        rest_rows_kernel,
        grid=(tensor - 1,),
        out_shape=jax.ShapeDtypeStruct((tensor - 1, rows, model), BF16),
        in_specs=[
            pl.BlockSpec((1, rows, width), lambda n: (lax.rem(n + 2, tensor), 0, 0)),
            whole(*w_in.shape),
        ],
        out_specs=block(rows, model),
        compiler_params=pltpu.CompilerParams(vmem_limit_bytes=12 * MIB),
        cost_estimate=LIGHT,
        name="rest_rows",
    )(d_chunks, w_in)


def in_grad_kernel(tensor, d_ref, *refs):
    seq_refs, grad_ref = refs[:tensor], refs[tensor]
    n = pl.program_id(0)
    for t in range(tensor):

        @pl.when(n == t)
        def _():
            part = dot_tn(seq_refs[t][...], d_ref[0])
            if t == 0:
                grad_ref[...] = part
            else:
                grad_ref[...] += part


def in_grad(d_chunks, seq_rows):
    tensor, rows, width = d_chunks.shape
    model = seq_rows[0].shape[1]
    return pl.pallas_call(
        functools.partial(in_grad_kernel, tensor),
        grid=(tensor,),
        out_shape=jax.ShapeDtypeStruct((model, width), F32),
        in_specs=[block(rows, width)] + [whole(rows, model)] * tensor,
        out_specs=whole(model, width),
        compiler_params=pltpu.CompilerParams(vmem_limit_bytes=16 * MIB),
        cost_estimate=HEAVY,
        name="in_grad",
    )(d_chunks, *seq_rows)


def per_device(
    dp, tensor, tokens, cotangent, labels, piece_start, piece_len, w_qkv, w_out, w_up, w_down,
    vec_table, ff_bias, cls_proj, cls_vec, cls_hidden, cls_out, cls_bias,
):
    rows, width = tokens.shape
    local = w_qkv.shape[2]
    heads = local // HEAD_DIM
    padded = -(-local // LANES) * LANES
    shard = w_qkv.shape[0]
    hidden = w_up.shape[1]
    ch = cls_proj.shape[1]
    z = lax.axis_index("tensor")
    info = jnp.concatenate(
        [z.reshape(1), lax.axis_index("dp").reshape(1), labels, piece_start[0], piece_len[0]]
    ).astype(jnp.int32)

    extra = padded - local
    qkv_shard = jnp.pad(w_qkv, ((0, 0), (0, 0), (0, extra))).reshape(shard, 3 * padded)
    ff_ring, seq_rows, shared = [], [], {}
    q_bias = lax.dynamic_slice_in_dim(vec_table[0], z * local, local, 0)
    v_bias = lax.dynamic_slice_in_dim(vec_table[1], z * local, local, 0)
    in_bias = jnp.pad(
        jnp.stack([q_bias, jnp.zeros_like(q_bias), v_bias]), ((0, 0), (0, extra))
    ).reshape(1, 3 * padded)


    def in_weights_chain():
        shared["in"] = yield from gather_chain(qkv_shard, "dp", dp)
        return shared["in"]

    def project_chain():
        done = []
        while len(done) < tensor:
            if "in" in shared:
                for part in seq_rows[len(done) :]:
                    value = jnp.dot(part, shared["in"], preferred_element_type=F32) + in_bias
                    done.append(value.astype(BF16))
            if len(done) < tensor:
                yield done, ()
        return done

    ff_shard = jnp.concatenate([w_up, w_down.T, w_out.T], axis=1)
    _, _, w_in, chunks = in_turn(
        vec_table[0, 0],
        {
            "rows": ring_chain(tokens, tensor, seq_rows),
            "ff": ring_chain(ff_shard, tensor, ff_ring),
            "in": in_weights_chain(),
            "project": project_chain(),
        },
        [("in",)] + [("rows", "ff", "in", "project")] * 3,
    )
    half = tensor // 2
    pieces = [
        lax.all_gather(jnp.stack(ff_ring[n : n + half]), "dp") for n in (0, half)
    ]
    if shard % 16:
        pieces = [
            p.transpose(1, 0, 2, 3).reshape(1, half, dp * shard, p.shape[-1]) for p in pieces
        ]

    def exchanged(parts):
        return [parts[0]] + [
            shifted(parts[tensor - s], "tensor", tensor, s) for s in range(1, tensor)
        ]

    mixed, lse = attend_forward(info, chunks, heads)
    mixed_parts = exchanged(mixed)
    kept = rows_forward(
        info, pieces, mixed_parts, tokens, vec_table,
        ff_bias.reshape(tensor, 1, hidden), cls_proj, cls_vec,
    )
    out_low, x_low, act, _, _, _, _, _, _, stats = kept
    all_stats = exchanged([stats] * tensor)
    (
        logits, two_low, upper_low, one_low, grad_h_one, grad_mixed, small,
    ) = rows_backward(
        info, pieces, all_stats, kept, cotangent, vec_table, cls_proj, cls_vec,
        cls_hidden, jnp.pad(cls_out, ((0, 0), (0, ch - CLASSES))),
        jnp.pad(cls_bias, (0, ch - CLASSES)).reshape(1, ch),
    )
    grad_rows = exchanged(grad_mixed)
    bits = bits_of(tensor)
    small_came = swapped(small, "tensor", tensor, bits[0])
    ff_parts = weight_grads(
        info, dp, shard, x_low, two_low, one_low, upper_low, act, mixed_parts
    )
    ff_parts, grad_rows[1], small_came = lax.optimization_barrier(
        (ff_parts, grad_rows[1], small_came)
    )
    sent, got, first, finish = weights_to_owner(ff_parts, dp, tensor, z)
    small = small + small_came
    sent, small, grad_rows = lax.optimization_barrier((sent, small, grad_rows))
    small_came = swapped(small, "tensor", tensor, bits[1])

    d_chunks, bias_sums = attend_backward(info, chunks, grad_rows, mixed, lse, heads)
    d_chunks, bias_sums, came, late, small_came = lax.optimization_barrier(
        (d_chunks, bias_sums, first(sent), got, small_came)
    )
    first_part = first_rows(d_chunks, w_in)
    came, late = after((came, late), first_part)

    def small_chain():
        total = small + small_came
        for bit in bits[2:]:
            got = yield total, swapped(total, "tensor", tensor, bit)
            total = total + got
        for bit in bits_of(dp):
            got = yield total, swapped(total, "dp", dp, bit)
            total = total + got
        return total.astype(F32)

    def rows_chain():
        came = shifted(first_part, "tensor", tensor, 1)
        later = yield first_part, d_chunks
        rest = rest_rows(later, w_in)
        total = first_part
        for t in range(2, tensor):
            came = yield (total, rest), came
            total = (rest[t - 2].astype(F32) + came.astype(F32)).astype(BF16)
            came = shifted(total, "tensor", tensor, 1)
        came = yield total, came
        return grad_h_one + rest[tensor - 2].astype(F32) + came.astype(F32)

    def in_chain():
        later = yield (), d_chunks
        grad = in_grad(later, seq_rows)
        grad = yield (), grad
        rider = jnp.pad(bias_sums, ((0, 8), (0, 2 * padded)))
        return (
            yield from owner_chain(
                grad.reshape(dp, shard, 3 * padded), rider, "dp", dp, "tensor", tensor
            )
        )

    grad_tokens, ff_own, (grad_in, riders), sums = in_turn(
        bias_sums[0, 0],
        {
            "rows": rows_chain(),
            "ff": finish(came, late),
            "in": in_chain(),
            "small": small_chain(),
        },
        [
            ("rows",), ("rows",), ("ff",), ("in",), ("in",), ("small",), ("rows",), ("in",),
            ("small",), ("ff",), ("in",), ("small",), ("in",), ("ff",), ("in",), ("rows",),
            ("ff",),
        ],
    )
    grad_w_qkv = grad_in.reshape(shard, 3, padded)[:, :, :local]
    bias_sum = riders[:, :2, :local].transpose(1, 0, 2).reshape(2, width)

    proj_sum, pack_sum = sums[:width], sums[width:]
    hid_sum = pack_sum[8 : 8 + ch]
    out_w_sum = pack_sum[8 + ch : 8 + 2 * ch, :CLASSES]
    at = 8 + 2 * ch
    vec_sum = pack_sum[at : at + 6 * width // ch].reshape(6, width)
    ff_bias_sum = pack_sum[at + 6 * width // ch :].reshape(-1)
    return (
        out_low,
        logits[0:1, :CLASSES],
        grad_tokens,
        grad_w_qkv,
        ff_own[:, 2 * hidden :].T,
        ff_own[:, :hidden],
        ff_own[:, hidden : 2 * hidden].T,
        jnp.concatenate([bias_sum, vec_sum], axis=0),
        ff_bias_sum,
        proj_sum,
        pack_sum[:3],
        hid_sum,
        out_w_sum,
        pack_sum[3, :CLASSES],
    )


def solution(mesh):
    dp, tensor = mesh.shape["dp"], mesh.shape["tensor"]
    rows = P(("dp", "tensor"), None)
    cut = P("dp", "tensor")
    turned_cut = P("tensor", "dp")
    return jax.shard_map(
        functools.partial(per_device, dp, tensor),
        mesh=mesh,
        in_specs=(
            rows, rows, P("dp"), P("dp", None), P("dp", None), P("dp", None, "tensor"),
            turned_cut, cut, turned_cut, P(), P(), P(), P(), P(), P(), P(),
        ),
        out_specs=(
            rows, P("dp", None), rows, P("dp", None, "tensor"), turned_cut, cut, turned_cut,
            P(), P(), P(), P(), P(), P(), P(),
        ),
        check_vma=False,
    )
```
